32 devices in a mesh: dp: 16 (over z, y, x), stream: 2 (over core).
Axes of the slice: x: 2, y: 2, z: 4, core: 2. Of those that a mesh axis runs over, the one named last changes fastest.
Arguments:
- feats: float32 [256, 180, 128], P('dp', 'stream'), may hold values from -6 to 6
- occupied: int32 [256, 180], P('dp', 'stream'), may hold values from 0 to 1, as said below
- cotangent: float32 [256, 180, 70], P('dp', 'stream'), may hold values from -6 to 6
- vector_params: float32 [1734], replicated, may hold values from 0.5 to 1.5
- vector_moment: float32 [1734], replicated, may hold values from -40 to 40
- vector_square: float32 [1734], replicated, may hold values from 216.576 to 875.52
- down_weight: float32 [1152, 256], P('dp'), may hold values from -0.1875 to 0.1875
- down_moment: float32 [1152, 256], P('dp'), may hold values from -16 to 16
- down_square: float32 [1152, 256], P('dp'), may hold values from 35.0208 to 138.24
- down_gram: float32 [256, 256], replicated, as said below
- down_basis: float32 [256, 256], replicated, as said below
- upward_weight: float32 [1024, 256], P('dp'), may hold values from -0.375 to 0.375
- upward_moment: float32 [1024, 256], P('dp'), may hold values from -10 to 10
- upward_square: float32 [1024, 256], P('dp'), may hold values from 11.9808 to 46.08
- upward_gram: float32 [256, 256], replicated, as said below
- upward_basis: float32 [256, 256], replicated, as said below
- lateral_weight: float32 [128, 256], replicated, may hold values from -0.5 to 0.5
- lateral_moment: float32 [128, 256], replicated, may hold values from -20 to 20
- lateral_square: float32 [128, 256], replicated, may hold values from 55.296 to 216.576
- lateral_gram: float32 [256, 256], replicated, as said below
- lateral_basis: float32 [256, 256], replicated, as said below
- merging_weight: float32 [4608, 64], P('dp'), may hold values from -0.09375 to 0.09375
- merging_moment: float32 [4608, 64], P('dp'), may hold values from -64 to 64
- merging_square: float32 [4608, 64], P('dp'), may hold values from 599.04 to 2442.24
- merging_gram: float32 [64, 64], replicated, as said below
- merging_basis: float32 [64, 64], replicated, as said below
- heads_weight: float32 [64, 70], replicated, may hold values from -0.75 to 0.75
- heads_moment: float32 [64, 70], replicated, may hold values from -128 to 128
- heads_square: float32 [64, 70], replicated, may hold values from 2442.24 to 9676.8
- heads_gram: float32 [70, 70], replicated, as said below
- heads_basis: float32 [70, 70], replicated, as said below
Outputs:
- head_maps: float32 [256, 180, 70], P('dp', 'stream')
- feats_grad: float32 [256, 180, 128], P('dp', 'stream')
- vector_renewed: float32 [1734], replicated
- vector_momentum: float32 [1734], replicated
- vector_variance: float32 [1734], replicated
- down_renewed: float32 [1152, 256], P('dp')
- down_momentum: float32 [1152, 256], P('dp')
- down_variance: float32 [1152, 256], P('dp')
- down_gramian: float32 [256, 256], replicated
- down_rotation: float32 [256, 256], replicated
- upward_renewed: float32 [1024, 256], P('dp')
- upward_momentum: float32 [1024, 256], P('dp')
- upward_variance: float32 [1024, 256], P('dp')
- upward_gramian: float32 [256, 256], replicated
- upward_rotation: float32 [256, 256], replicated
- lateral_renewed: float32 [128, 256], replicated
- lateral_momentum: float32 [128, 256], replicated
- lateral_variance: float32 [128, 256], replicated
- lateral_gramian: float32 [256, 256], replicated
- lateral_rotation: float32 [256, 256], replicated
- merging_renewed: float32 [4608, 64], P('dp')
- merging_momentum: float32 [4608, 64], P('dp')
- merging_variance: float32 [4608, 64], P('dp')
- merging_gramian: float32 [64, 64], replicated
- merging_rotation: float32 [64, 64], replicated
- heads_renewed: float32 [64, 70], replicated
- heads_momentum: float32 [64, 70], replicated
- heads_variance: float32 [64, 70], replicated
- heads_gramian: float32 [70, 70], replicated
- heads_rotation: float32 [70, 70], replicated
The draws below stay inside these ranges and needn't reach their ends.
Inputs may be any that keep to these rules, and one draw needn't show every extreme that they name: 1 marks an occupied pixel. `down_gram`: symmetric. `upward_gram`: symmetric. `lateral_gram`: symmetric. `merging_gram`: symmetric. `heads_gram`: symmetric. `down_basis`: orthogonal. `upward_basis`: orthogonal. `lateral_basis`: orthogonal. `merging_basis`: orthogonal. `heads_basis`: orthogonal.
All inputs are finite; a program needn't handle non-finite values.
Results may differ from the reference program's by a relative error of at most 0.0003.
Values sent between devices are 32-bit elements; how exact they have to be, the bound alone decides.
No kernel may reach another device: no remote copies, remote signals or barrier semaphores. Data moves between devices by JAX's collectives and lax.ppermute only.
A program may use at most 128 MiB of HBM per device.

```python
import math
import jax
import jax.numpy as jnp
from jax import lax

C0 = 128
C1 = 256
C2 = 64
CH = 70
COLS = 180
SCENE_ROWS = 180
STEP = 10
ROWS = 256
NVEC = 1734


def draw_occupied(key, part):
    row_index = jnp.arange(ROWS)[:, None]
    col_index = jnp.arange(COLS)[None, :]
    row_weight = (250 * (ROWS - 1) + 750 * row_index) // (ROWS - 1)
    col_weight = (250 * (COLS - 1) + 750 * col_index) // (COLS - 1)
    chance = 50 + row_weight * col_weight * 900 // 1000000
    ticket = jax.random.randint(key, (ROWS, COLS), 0, 1000)
    return (ticket < chance).astype(jnp.int32)


def gram_draw(key, order, magnitude, salt):
    first_key, second_key = jax.random.split(jax.random.fold_in(key, salt))
    diagonal = magnitude * jnp.exp(jax.random.uniform(first_key, (order,), jnp.float32, 0.0, math.log(4.0)))
    noise = jax.random.uniform(second_key, (order, order), jnp.float32, -1.0, 1.0)
    symmetric = 0.5 * (noise + noise.T)
    identity = (jnp.arange(order)[:, None] == jnp.arange(order)[None, :]).astype(jnp.float32)
    return identity * diagonal[None, :] + (1.0 - identity) * symmetric * (magnitude / order)


def basis_draw(key, order, salt):
    first_key, second_key = jax.random.split(jax.random.fold_in(key, salt))
    position = jnp.arange(order).astype(jnp.float32)
    table = jnp.cos(math.pi * (position[:, None] + 0.5) * position[None, :] / order) * math.sqrt(2.0 / order)
    table = jnp.where(position[None, :] == 0.0, table / math.sqrt(2.0), table)
    shuffle = jax.random.permutation(first_key, order)
    signs = (2 * jax.random.randint(second_key, (order,), 0, 2) - 1).astype(jnp.float32)
    return table[:, shuffle] * signs[None, :]


def draw_down_gram(key, part):
    return gram_draw(key, C1, 0.0144 * 9 * C0 * ROWS * COLS, 101)


def draw_upward_gram(key, part):
    return gram_draw(key, C1, 0.0049 * 4 * C1 * ROWS * COLS, 202)


def draw_lateral_gram(key, part):
    return gram_draw(key, C1, 0.0225 * C0 * ROWS * COLS, 303)


def draw_merging_gram(key, part):
    return gram_draw(key, C2, 0.25 * 18 * C1 * ROWS * COLS, 404)


def draw_heads_gram(key, part):
    return gram_draw(key, CH, 1.0 * C2 * ROWS * COLS, 505)


def draw_down_basis(key, part):
    return basis_draw(key, C1, 611)


def draw_upward_basis(key, part):
    return basis_draw(key, C1, 722)


def draw_lateral_basis(key, part):
    return basis_draw(key, C1, 833)


def draw_merging_basis(key, part):
    return basis_draw(key, C2, 944)


def draw_heads_basis(key, part):
    return basis_draw(key, CH, 1055)


def steps_of(rng, shape, cuts, least, largest):
    def one(dim, parts):
        draws = jax.random.uniform(jax.random.fold_in(jax.random.fold_in(rng, 6), dim), (parts,), jnp.float32, least / len(cuts), largest / len(cuts))
        return jnp.repeat(jnp.exp(draws), shape[dim] // parts).reshape((-1,) + (1,) * (len(shape) - dim - 1))

    factor_of = one(*cuts[0])
    for cut in cuts[1:]:
        factor_of = factor_of * one(*cut)
    return factor_of


def centred(stream_key, shape, scale, bound, cuts=(), kind=jnp.bfloat16):
    factor_of = steps_of(stream_key, shape, cuts, -0.22, 0.18) if cuts else 1.0
    drawn = jax.random.normal(stream_key, shape, jnp.float32) * scale * factor_of
    return jnp.minimum(jnp.maximum(drawn, -bound), bound).astype(kind)


def setup_inputs(seed: int = 0) -> dict:
    keys = jax.random.split(jax.random.key(seed), 32)
    return {
        "feats": centred(keys[0], (ROWS, COLS, C0), 1.0, 6.0, ((0, 16), (1, 2)), jnp.float32),
        "occupied": draw_occupied(jax.random.fold_in(keys[31], 71), 0),
        "cotangent": centred(keys[2], (ROWS, COLS, CH), 1.0, 6.0, ((0, 16), (1, 2)), jnp.float32),
        "vector_params": jnp.clip(1.0 + 0.1 * jax.random.normal(keys[3], (NVEC,), jnp.float32), 0.5, 1.5),
        "vector_moment": centred(keys[4], (NVEC,), (0.033 * (ROWS * COLS) ** 0.5), 40.0, (), jnp.float32),
        "vector_square": jnp.clip(jnp.exp(jax.random.uniform(keys[5], (NVEC,), jnp.float32, math.log(216.576), math.log(875.52))), 216.576, 875.52),
        "down_weight": centred(keys[6], (9 * C0, C1), (9 * C0) ** -0.5, 0.1875, ((0, 16),), jnp.float32),
        "down_moment": centred(keys[7], (9 * C0, C1), (0.0133 * (ROWS * COLS) ** 0.5), 16.0, ((0, 16),), jnp.float32),
        "down_square": jnp.clip(jnp.exp(math.log(138.24) - 1.3730491 * jax.random.uniform(keys[8], (9 * C0, C1), jnp.float32) ** steps_of(keys[8], (9 * C0, C1), ((0, 16),), -0.2, 0.2)), 35.0208, 138.24),
        "down_gram": draw_down_gram(jax.random.fold_in(keys[31], 71), 0),
        "down_basis": draw_down_basis(jax.random.fold_in(keys[31], 71), 0),
        "upward_weight": centred(keys[11], (4 * C1, C1), C1 ** -0.5, 0.375, ((0, 16),), jnp.float32),
        "upward_moment": centred(keys[12], (4 * C1, C1), (0.0078 * (ROWS * COLS) ** 0.5), 10.0, ((0, 16),), jnp.float32),
        "upward_square": jnp.clip(jnp.exp(math.log(46.08) - 1.3470737 * jax.random.uniform(keys[13], (4 * C1, C1), jnp.float32) ** steps_of(keys[13], (4 * C1, C1), ((0, 16),), -0.2, 0.2)), 11.9808, 46.08),
        "upward_gram": draw_upward_gram(jax.random.fold_in(keys[31], 71), 0),
        "upward_basis": draw_upward_basis(jax.random.fold_in(keys[31], 71), 0),
        "lateral_weight": centred(keys[16], (C0, C1), C0 ** -0.5, 0.5, (), jnp.float32),
        "lateral_moment": centred(keys[17], (C0, C1), (0.0167 * (ROWS * COLS) ** 0.5), 20.0, (), jnp.float32),
        "lateral_square": jnp.clip(jnp.exp(jax.random.uniform(keys[18], (C0, C1), jnp.float32, math.log(55.296), math.log(216.576))), 55.296, 216.576),
        "lateral_gram": draw_lateral_gram(jax.random.fold_in(keys[31], 71), 0),
        "lateral_basis": draw_lateral_basis(jax.random.fold_in(keys[31], 71), 0),
        "merging_weight": centred(keys[21], (18 * C1, C2), (18 * C1) ** -0.5, 0.09375, ((0, 16),), jnp.float32),
        "merging_moment": centred(keys[22], (18 * C1, C2), (0.0555 * (ROWS * COLS) ** 0.5), 64.0, ((0, 16),), jnp.float32),
        "merging_square": jnp.clip(jnp.exp(math.log(2442.24) - 1.4053426 * jax.random.uniform(keys[23], (18 * C1, C2), jnp.float32) ** steps_of(keys[23], (18 * C1, C2), ((0, 16),), -0.2, 0.2)), 599.04, 2442.24),
        "merging_gram": draw_merging_gram(jax.random.fold_in(keys[31], 71), 0),
        "merging_basis": draw_merging_basis(jax.random.fold_in(keys[31], 71), 0),
        "heads_weight": centred(keys[26], (C2, CH), C2 ** -0.5, 0.75, (), jnp.float32),
        "heads_moment": centred(keys[27], (C2, CH), (0.111 * (ROWS * COLS) ** 0.5), 128.0, (), jnp.float32),
        "heads_square": jnp.clip(jnp.exp(jax.random.uniform(keys[28], (C2, CH), jnp.float32, math.log(2442.24), math.log(9676.8))), 2442.24, 9676.8),
        "heads_gram": draw_heads_gram(jax.random.fold_in(keys[31], 71), 0),
        "heads_basis": draw_heads_basis(jax.random.fold_in(keys[31], 71), 0),
    }


EPS_NORM = 1e-05
BETA_ONE = 0.9
BETA_TWO = 0.95
BETA_GRAM = 0.95
EPS_ADAM = 1e-08
DECAY = 0.01
VECTOR_RATE = 0.1
HIGHEST = lax.Precision.HIGHEST

@jax.custom_vjp
def low(v):
    return lax.optimization_barrier(v.astype(jnp.bfloat16)).astype(jnp.float32)

@jax.custom_vjp
def low_back(v):
    return v

def low_keep(v):
    return (low(v), None)

def low_pass(kept, grad):
    return (grad,)

def back_keep(v):
    return (v, None)

def back_low(kept, grad):
    return (low(grad),)
low.defvjp(low_keep, low_pass)
low_back.defvjp(back_keep, back_low)

def matmul(left, right):
    return jnp.dot(left.astype(jnp.float32), right.astype(jnp.float32), precision=HIGHEST, preferred_element_type=jnp.float32)

def keep_rows(global_rows, total_rows):
    wrapped = jnp.remainder(global_rows, total_rows)
    return ((wrapped + SCENE_ROWS // 2) % SCENE_ROWS != 0).astype(jnp.float32)

def split_vector(packed):
    widths = [C1] * 6 + [C2] * 2 + [CH]
    pieces = []
    offset = 0
    for extent in widths:
        pieces.append(packed[offset:offset + extent])
        offset = offset + extent
    return pieces

def assemble_quads(quads):
    paired = [jnp.stack(quads[parity], axis=2) for parity in range(2)]
    joined = jnp.stack(paired, axis=1)
    return joined.reshape(joined.shape[0] * 2, joined.shape[2] * 2, joined.shape[4])

def batch_norm(feature, norm_gain, norm_shift):
    pixels = feature.shape[0] * feature.shape[1]
    centre = lax.optimization_barrier(jnp.sum(feature, axis=(0, 1))) / pixels
    second = lax.optimization_barrier(jnp.sum(feature * feature, axis=(0, 1))) / pixels
    spread = lax.rsqrt(second - centre * centre + EPS_NORM)
    return jax.nn.silu(norm_gain * ((feature - centre) * spread) + norm_shift)

def forward(masked, packed, down_matrix, upward_matrix, lateral_matrix, merging_matrix, head_matrix):
    height, breadth, channels = masked.shape
    half_height, half_breadth = (height // 2, breadth // 2)
    gain_one, shift_one, gain_three, shift_three, gain_four, shift_four, gain_five, shift_five, head_bias = split_vector(packed)
    cyclic_rows = jnp.concatenate([masked[height - 1:], masked], axis=0)
    padded = jnp.pad(cyclic_rows, ((0, 0), (1, 0), (0, 0)))
    coarse_keep = keep_rows(2 * jnp.arange(half_height), height)[:, None, None]
    coarse = jnp.zeros((half_height, half_breadth, C1), jnp.float32)
    for row_tap in range(3):
        for col_tap in range(3):
            window = padded[row_tap:row_tap + height:2, col_tap:col_tap + breadth:2]
            offset = (3 * row_tap + col_tap) * channels
            contrib = matmul(window, down_matrix[offset:offset + channels])
            if row_tap == 0:
                contrib = contrib * coarse_keep
            coarse = coarse + contrib
    act_one = batch_norm(coarse, gain_one, shift_one)
    quads = [[matmul(act_one, upward_matrix[(2 * row_tap + col_tap) * C1:(2 * row_tap + col_tap + 1) * C1]) for col_tap in range(2)] for row_tap in range(2)]
    act_three = batch_norm(assemble_quads(quads), gain_three, shift_three)
    act_four = batch_norm(matmul(masked, lateral_matrix), gain_four, shift_four)
    joined = jnp.concatenate([act_three, act_four], axis=2)
    cyclic_joined = jnp.concatenate([joined[height - 1:], joined, joined[:1]], axis=0)
    framed = jnp.pad(cyclic_joined, ((0, 0), (1, 1), (0, 0)))[None]
    row_index = jnp.arange(height)
    row_keeps = [keep_rows(row_index, height)[:, None, None], None, keep_rows(row_index + 1, height)[:, None, None]]
    merged = jnp.zeros((height, breadth, C2), jnp.float32)
    for row_tap in range(3):
        stencil = merging_matrix[6 * row_tap * C1:6 * (row_tap + 1) * C1].reshape(1, 3, 2 * C1, C2)
        sweep = lax.conv_general_dilated(framed, stencil, (1, 1), 'VALID', dimension_numbers=('NHWC', 'HWIO', 'NHWC'), precision=HIGHEST)[0]
        contrib = sweep[row_tap:row_tap + height]
        if row_tap != 1:
            contrib = contrib * row_keeps[row_tap]
        merged = merged + contrib
    act_five = batch_norm(merged, gain_five, shift_five)
    return matmul(act_five, head_matrix) + head_bias

def adam_vector(params, moment, square, gradient):
    momentum = BETA_ONE * moment + (1.0 - BETA_ONE) * gradient
    variance = BETA_TWO * square + (1.0 - BETA_TWO) * gradient * gradient
    direction = momentum / (1.0 - BETA_ONE ** STEP) / (jnp.sqrt(variance / (1.0 - BETA_TWO ** STEP)) + EPS_ADAM)
    return (params - VECTOR_RATE * (direction + DECAY * params), momentum, variance)

def soap_step(weight, moment, square, gram_old, basis_old, gradient, step_rate):
    rotated = matmul(gradient, basis_old)
    momentum = BETA_ONE * moment + (1.0 - BETA_ONE) * rotated
    variance = BETA_TWO * square + (1.0 - BETA_TWO) * rotated * rotated
    direction = momentum / (1.0 - BETA_ONE ** STEP) / (jnp.sqrt(variance / (1.0 - BETA_TWO ** STEP)) + EPS_ADAM)
    renewed = weight - step_rate * (matmul(direction, basis_old.T) + DECAY * weight)
    gramian = BETA_GRAM * gram_old + (1.0 - BETA_GRAM) * matmul(gradient.T, gradient)
    product = matmul(gramian, basis_old)
    factor = jnp.linalg.cholesky(matmul(product.T, product))
    rotation = jax.scipy.linalg.solve_triangular(factor, product.T, lower=True).T
    return (renewed, momentum, variance, gramian, rotation)

def reference(feats, occupied, cotangent, vector_params, vector_moment, vector_square, down_weight, down_moment, down_square, down_gram, down_basis, upward_weight, upward_moment, upward_square, upward_gram, upward_basis, lateral_weight, lateral_moment, lateral_square, lateral_gram, lateral_basis, merging_weight, merging_moment, merging_square, merging_gram, merging_basis, heads_weight, heads_moment, heads_square, heads_gram, heads_basis):
    occupancy = occupied.astype(jnp.float32)[..., None]
    masked = feats * occupancy
    head_maps, pullback = jax.vjp(forward, masked, vector_params, down_weight, upward_weight, lateral_weight, merging_weight, heads_weight)
    grad_masked, grad_vector, grad_down, grad_upward, grad_lateral, grad_merging, grad_heads = pullback(cotangent)
    feats_grad = grad_masked * occupancy
    vector_renewed, vector_momentum, vector_variance = adam_vector(vector_params, vector_moment, vector_square, grad_vector)
    down_renewed, down_momentum, down_variance, down_gramian, down_rotation = soap_step(down_weight, down_moment, down_square, down_gram, down_basis, grad_down, 1.0 / math.sqrt(9 * C0))
    upward_renewed, upward_momentum, upward_variance, upward_gramian, upward_rotation = soap_step(upward_weight, upward_moment, upward_square, upward_gram, upward_basis, grad_upward, 1.0 / math.sqrt(C1))
    lateral_renewed, lateral_momentum, lateral_variance, lateral_gramian, lateral_rotation = soap_step(lateral_weight, lateral_moment, lateral_square, lateral_gram, lateral_basis, grad_lateral, 1.0 / math.sqrt(C0))
    merging_renewed, merging_momentum, merging_variance, merging_gramian, merging_rotation = soap_step(merging_weight, merging_moment, merging_square, merging_gram, merging_basis, grad_merging, 1.0 / math.sqrt(18 * C1))
    heads_renewed, heads_momentum, heads_variance, heads_gramian, heads_rotation = soap_step(heads_weight, heads_moment, heads_square, heads_gram, heads_basis, grad_heads, 1.0 / math.sqrt(C2))
    return (head_maps, feats_grad, vector_renewed, vector_momentum, vector_variance, down_renewed, down_momentum, down_variance, down_gramian, down_rotation, upward_renewed, upward_momentum, upward_variance, upward_gramian, upward_rotation, lateral_renewed, lateral_momentum, lateral_variance, lateral_gramian, lateral_rotation, merging_renewed, merging_momentum, merging_variance, merging_gramian, merging_rotation, heads_renewed, heads_momentum, heads_variance, heads_gramian, heads_rotation)
```

```python
import functools
import math

import jax
import jax.numpy as jnp
from jax import lax
from jax.experimental import pallas as pl
from jax.experimental.pallas import tpu as pltpu
from jax.sharding import PartitionSpec as P

C0 = 128
C1 = 256
C2 = 64
CH = 70
SCENE_ROWS = 180
STEP = 10


EPS_NORM = 1e-05
BETA_ONE = 0.9
BETA_TWO = 0.95
BETA_GRAM = 0.95
EPS_ADAM = 1e-08
DECAY = 0.01
VECTOR_RATE = 0.1
HIGHEST = lax.Precision.HIGHEST


F32=jnp.float32
def dot(a,b,ca,cb):
    return lax.dot_general(a,b,(((ca,),(cb,)),((),())),precision=HIGHEST,preferred_element_type=F32)
NB=32
def base_inverse(blocks):
    lane=lax.broadcasted_iota(jnp.int32,(NB,128),1); row=lax.broadcasted_iota(jnp.int32,(NB,128),0)
    eye=(lane==row+NB).astype(F32)
    xs=[jnp.concatenate([b,jnp.zeros((NB,128-NB),F32)],axis=1)+eye for b in blocks]
    for k in range(NB):
        nx=[]
        for x in xs:
            col=jnp.broadcast_to(x[:,k:k+1],(NB,128))
            piv=col[k:k+1,:]
            r=x[k:k+1,:]*(1.0/piv)
            nx.append(x-jnp.where(row>k,col,0.0)*r)
        xs=nx
    outs=[]
    for x in xs:
        d=jnp.sum(jnp.where(lane==row,x,0.0),axis=1,keepdims=True)
        y=x*lax.rsqrt(d)
        outs.append(y[:,NB:2*NB])
    return outs
def kern(ns,*refs):
    m=len(ns)
    gram=refs[0:m]; add=refs[m:2*m]; basis=refs[2*m:3*m]
    out_gram=refs[3*m:4*m]; out_rot=refs[4*m:5*m]
    aa=refs[5*m:6*m]; xx=refs[6*m:7*m]
    prods=[]
    for i,n in enumerate(ns):
        g=0.95*gram[i][...]+0.05*add[i][...]
        out_gram[i][...]=g
        p=dot(g,basis[i][...],1,0)
        out_rot[i][...]=p
        a=dot(p,p,0,0)
        npad=aa[i].shape[0]
        if npad!=n:
            r=lax.broadcasted_iota(jnp.int32,(npad,npad),0); c=lax.broadcasted_iota(jnp.int32,(npad,npad),1)
            aa[i][...]=((r==c)&(r>=n)).astype(F32)
            aa[i][0:n,0:n]=a
        else:
            aa[i][...]=a
        r=lax.broadcasted_iota(jnp.int32,(npad,npad),0); c=lax.broadcasted_iota(jnp.int32,(npad,npad),1)
        xx[i][...]=(r==c).astype(F32)
    for b in range(max(a.shape[0] for a in aa)//NB):
        s=b*NB
        live=[i for i in range(m) if s<aa[i].shape[0]]
        inv=base_inverse([aa[i][s:s+NB,s:s+NB] for i in live])
        for i,li in zip(live,inv):
            npad=aa[i].shape[0]
            e=s+NB
            y=dot(li,xx[i][s:e,:],1,0)
            xx[i][s:e,:]=y
            if e<npad:
                rpan=dot(li,aa[i][s:e,e:],1,0)
                cpan=dot(aa[i][e:,s:e],li,1,1)
                aa[i][e:,e:]=aa[i][e:,e:]-dot(cpan,rpan,1,0)
                xx[i][e:,:]=xx[i][e:,:]-dot(cpan,y,1,0)
    for i,n in enumerate(ns):
        out_rot[i][...]=dot(out_rot[i][...],xx[i][0:n,0:n],1,1)
def rotations(grams,adds,bases):
    ns=[g.shape[0] for g in grams]
    pads=[-(-n//NB)*NB for n in ns]
    outs=pl.pallas_call(functools.partial(kern,ns),
        out_shape=[jax.ShapeDtypeStruct((n,n),F32) for n in ns]*2,
        scratch_shapes=[pltpu.VMEM((p,p),F32) for p in pads]*2,
        compiler_params=pltpu.CompilerParams(vmem_limit_bytes=32<<20),
        name='rotate')(*grams,*adds,*bases)
    return outs[:len(ns)],outs[len(ns):]


def exchange(value):
    return lax.ppermute(value, "stream", [(0, 1), (1, 0)])


def everyone(value, axes):
    count = lax.axis_size(axes)
    copies = jnp.broadcast_to(value[None], (count,) + value.shape)
    return lax.all_to_all(copies, axes, 0, 0, tiled=True)


def sum_small(pieces):
    flat = jnp.concatenate([piece.reshape(-1) for piece in pieces])
    total = jnp.sum(everyone(flat, ("dp", "stream")), axis=0)
    out = []
    offset = 0
    for piece in pieces:
        out.append(total[offset : offset + piece.size].reshape(piece.shape))
        offset += piece.size
    return out


def join_halves(mine, axis):
    other = exchange(mine)
    first = lax.axis_index("stream") == 0
    return jnp.concatenate(
        [jnp.where(first, mine, other), jnp.where(first, other, mine)], axis=axis
    )


def own_half(value, axis, which):
    half = value.shape[axis] // 2
    return lax.dynamic_slice_in_dim(value, which * half, half, axis)


def gather_rows(shard, axis):
    mine = own_half(shard, axis, lax.axis_index("stream"))
    blocks = everyone(mine, "dp")
    if axis == 1:
        return join_halves(blocks.reshape(-1, mine.shape[1]), 1)
    joined = join_halves(blocks, 1)
    return joined.reshape(-1, shard.shape[1])


def scatter_half(full, axis):
    core = lax.axis_index("stream")
    count = lax.axis_size("dp")
    blocks = full.reshape((count, full.shape[0] // count) + full.shape[1:])
    mine = own_half(blocks, axis + 1, core) + exchange(own_half(blocks, axis + 1, 1 - core))
    return jnp.sum(lax.all_to_all(mine, "dp", 0, 0, tiled=True), axis=0)


def from_behind(block, axis, distance):
    devices = range(lax.axis_size(axis))
    route = [(i - distance, i) for i in devices if i - distance in devices]
    return lax.ppermute(block, axis, route)


def shifted(value, axis, steps):
    count = lax.axis_size(axis)
    pairs = [(source, (source + steps) % count) for source in range(count)]
    return lax.ppermute(value, axis, pairs)


def extended_2(shard, sides, width):
    for axis, dim in sides:
        count, length = (lax.axis_size(axis), shard.shape[dim])
        up = [(i, (i + 1) % count) for i in range(count)]
        down = [(j, i) for i, j in up]
        last = lax.slice_in_dim(shard, length - width, length, axis=dim)
        initial = lax.slice_in_dim(shard, 0, width, axis=dim)
        before = lax.ppermute(last, axis, up)
        after = lax.ppermute(initial, axis, down)
        shard = jnp.concatenate([before, shard, after], axis=dim)
    return shard


def matmul(left, right):
    return jnp.dot(left, right, precision=HIGHEST, preferred_element_type=jnp.float32)


def contract(left, right):
    return jnp.tensordot(left, right, axes=((0, 1), (0, 1)), precision=HIGHEST)


def back_product(upstream, matrix):
    return jnp.tensordot(upstream, matrix, axes=((2,), (1,)), precision=HIGHEST)


def gram_rows(gradient):
    return jnp.tensordot(gradient, gradient, axes=((0,), (0,)), precision=HIGHEST)


def contract_rows(left, right):
    return jnp.tensordot(left, right, axes=((0,), (0,)), precision=HIGHEST)


def all_halves(partial, axis):
    count = lax.axis_size("dp")
    blocks = partial.reshape((count, partial.shape[0] // count) + partial.shape[1:])
    mine = jnp.sum(lax.all_to_all(blocks, "dp", 0, 0, tiled=True), axis=0)
    return join_halves(everyone(mine, "dp").reshape(partial.shape), axis)


def keep_rows(global_rows, total_rows):
    wrapped = jnp.remainder(global_rows, total_rows)
    return ((wrapped + SCENE_ROWS // 2) % SCENE_ROWS != 0).astype(jnp.float32)


def split_vector(packed):
    widths = [C1] * 6 + [C2] * 2 + [CH]
    pieces = []
    offset = 0
    for extent in widths:
        pieces.append(packed[offset : offset + extent])
        offset = offset + extent
    return pieces


def assemble_quads(quads):
    paired = [jnp.stack(quads[parity], axis=2) for parity in range(2)]
    joined = jnp.stack(paired, axis=1)
    return joined.reshape(joined.shape[0] * 2, joined.shape[2] * 2, joined.shape[4])


def split_quads(feature):
    shaped = feature.reshape(feature.shape[0] // 2, 2, feature.shape[1] // 2, 2, feature.shape[2])
    return [[shaped[:, row_tap, :, col_tap] for col_tap in range(2)] for row_tap in range(2)]


def norm_forward(feature, norm_gain, norm_shift, pixels):
    totals = sum_small(
        (jnp.sum(feature, axis=(0, 1)), jnp.sum(feature * feature, axis=(0, 1)))
    )
    centre = totals[0] / pixels
    spread = lax.rsqrt(totals[1] / pixels - centre * centre + EPS_NORM)
    normed = (feature - centre) * spread
    return (jax.nn.silu(norm_gain * normed + norm_shift), normed, spread)


def norm_backward(upstream, normed, spread, norm_gain, norm_shift, pixels):
    hidden = norm_gain * normed + norm_shift
    sigmoid = jax.nn.sigmoid(hidden)
    grad_hidden = upstream * sigmoid * (1.0 + hidden * (1.0 - sigmoid))
    grad_gain, grad_shift = sum_small(
        (jnp.sum(grad_hidden * normed, axis=(0, 1)), jnp.sum(grad_hidden, axis=(0, 1)))
    )
    grad_feature = (
        norm_gain * spread * (grad_hidden - grad_shift / pixels - normed * (grad_gain / pixels))
    )
    return (grad_feature, grad_gain, grad_shift)


def adam_vector(params, moment, square, gradient):
    momentum = BETA_ONE * moment + (1.0 - BETA_ONE) * gradient
    variance = BETA_TWO * square + (1.0 - BETA_TWO) * gradient * gradient
    direction = (
        momentum / (1.0 - BETA_ONE**STEP) / (jnp.sqrt(variance / (1.0 - BETA_TWO**STEP)) + EPS_ADAM)
    )
    return (params - VECTOR_RATE * (direction + DECAY * params), momentum, variance)


def soap_step(weight, moment, square, basis_old, gradient, step_rate):
    rotated = matmul(gradient, basis_old)
    momentum = BETA_ONE * moment + (1.0 - BETA_ONE) * rotated
    variance = BETA_TWO * square + (1.0 - BETA_TWO) * rotated * rotated
    direction = (
        momentum / (1.0 - BETA_ONE**STEP) / (jnp.sqrt(variance / (1.0 - BETA_TWO**STEP)) + EPS_ADAM)
    )
    renewed = weight - step_rate * (matmul(direction, basis_old.T) + DECAY * weight)
    return (renewed, momentum, variance)


def local(
    feats,
    occupied,
    cotangent,
    vector_params,
    vector_moment,
    vector_square,
    down_weight,
    down_moment,
    down_square,
    down_gram,
    down_basis,
    upward_weight,
    upward_moment,
    upward_square,
    upward_gram,
    upward_basis,
    lateral_weight,
    lateral_moment,
    lateral_square,
    lateral_gram,
    lateral_basis,
    merging_weight,
    merging_moment,
    merging_square,
    merging_gram,
    merging_basis,
    heads_weight,
    heads_moment,
    heads_square,
    heads_gram,
    heads_basis,
):
    height, breadth, channels = feats.shape
    half_height, half_breadth = (height // 2, breadth // 2)
    total_rows = height * lax.axis_size("dp")
    fine_count = float(height * breadth * lax.axis_size("dp") * lax.axis_size("stream"))
    coarse_count = fine_count / 4.0
    first_row = lax.axis_index("dp") * height
    stream_index = lax.axis_index("stream")
    left_live = (stream_index != 0).astype(jnp.float32)
    right_live = (stream_index != lax.axis_size("stream") - 1).astype(jnp.float32)
    column_mask = jnp.concatenate(
        [left_live[None], jnp.ones((breadth,), jnp.float32), right_live[None]]
    )[None, :, None]
    down_full, upward_full, merging_full = (
        gather_rows(down_weight, 1),
        gather_rows(upward_weight, 1),
        gather_rows(merging_weight, 0),
    )
    (
        gain_one,
        shift_one,
        gain_three,
        shift_three,
        gain_four,
        shift_four,
        gain_five,
        shift_five,
        head_bias,
    ) = split_vector(vector_params)
    occupancy = occupied.astype(jnp.float32)[..., None]
    masked = feats * occupancy
    left_edge = from_behind(masked[:, breadth - 1 :], "stream", 1)
    widened = jnp.concatenate([left_edge, masked], axis=1)
    upper_edge = shifted(widened[height - 1 :], "dp", 1)
    padded = jnp.concatenate([upper_edge, widened], axis=0)
    coarse_keep = keep_rows(first_row + 2 * jnp.arange(half_height), total_rows)[:, None, None]
    windows = [
        [
            padded[row_tap : row_tap + height : 2, col_tap : col_tap + breadth : 2]
            for col_tap in range(3)
        ]
        for row_tap in range(3)
    ]
    coarse = jnp.zeros((half_height, half_breadth, C1), jnp.float32)
    for row_tap in range(3):
        for col_tap in range(3):
            offset = (3 * row_tap + col_tap) * channels
            contrib = matmul(windows[row_tap][col_tap], down_full[offset : offset + channels])
            if row_tap == 0:
                contrib = contrib * coarse_keep
            coarse = coarse + contrib
    act_one, normed_one, spread_one = norm_forward(coarse, gain_one, shift_one, coarse_count)
    quads = [
        [
            matmul(
                act_one,
                upward_full[(2 * row_tap + col_tap) * C1 : (2 * row_tap + col_tap + 1) * C1],
            )
            for col_tap in range(2)
        ]
        for row_tap in range(2)
    ]
    act_three, normed_three, spread_three = norm_forward(
        assemble_quads(quads), gain_three, shift_three, fine_count
    )
    act_four, normed_four, spread_four = norm_forward(
        matmul(masked, lateral_weight), gain_four, shift_four, fine_count
    )
    joined = jnp.concatenate([act_three, act_four], axis=2)
    framed = extended_2(joined, (("dp", 0), ("stream", 1)), 1) * column_mask
    row_index = first_row + jnp.arange(height)
    row_keeps = [
        keep_rows(row_index, total_rows)[:, None, None],
        None,
        keep_rows(row_index + 1, total_rows)[:, None, None],
    ]
    merged = jnp.zeros((height, breadth, C2), jnp.float32)
    for row_tap in range(3):
        for col_tap in range(3):
            offset = (3 * row_tap + col_tap) * 2 * C1
            contrib = matmul(
                framed[row_tap : row_tap + height, col_tap : col_tap + breadth],
                merging_full[offset : offset + 2 * C1],
            )
            if row_tap != 1:
                contrib = contrib * row_keeps[row_tap]
            merged = merged + contrib
    act_five, normed_five, spread_five = norm_forward(merged, gain_five, shift_five, fine_count)
    head_maps = matmul(act_five, heads_weight) + head_bias
    grad_heads = contract(act_five, cotangent)
    grad_bias = jnp.sum(cotangent, axis=(0, 1))
    grad_five = back_product(cotangent, heads_weight)
    grad_merged, gain_grad_five, shift_grad_five = norm_backward(
        grad_five, normed_five, spread_five, gain_five, shift_five, fine_count
    )
    grad_framed = extended_2(grad_merged, (("dp", 0), ("stream", 1)), 1) * column_mask
    frame_rows = first_row - 1 + jnp.arange(height + 2)
    frame_keeps = [
        keep_rows(frame_rows, total_rows)[:, None, None],
        None,
        keep_rows(frame_rows + 1, total_rows)[:, None, None],
    ]
    merging_parts = []
    grad_joined = jnp.zeros((height, breadth, 2 * C1), jnp.float32)
    for row_tap in range(3):
        if row_tap == 1:
            local_grad = grad_merged
            source_frame = grad_framed
        else:
            local_grad = grad_merged * row_keeps[row_tap]
            source_frame = grad_framed * frame_keeps[row_tap]
        for col_tap in range(3):
            offset = (3 * row_tap + col_tap) * 2 * C1
            merging_parts.append(
                contract(
                    framed[row_tap : row_tap + height, col_tap : col_tap + breadth], local_grad
                )
            )
            grad_joined = grad_joined + back_product(
                source_frame[
                    2 - row_tap : 2 - row_tap + height, 2 - col_tap : 2 - col_tap + breadth
                ],
                merging_full[offset : offset + 2 * C1],
            )
    grad_merging = jnp.concatenate(merging_parts, axis=0)
    grad_lateral_map, gain_grad_four, shift_grad_four = norm_backward(
        grad_joined[:, :, C1:], normed_four, spread_four, gain_four, shift_four, fine_count
    )
    grad_lateral = contract(masked, grad_lateral_map)
    grad_masked = back_product(grad_lateral_map, lateral_weight)
    grad_upsampled, gain_grad_three, shift_grad_three = norm_backward(
        grad_joined[:, :, :C1], normed_three, spread_three, gain_three, shift_three, fine_count
    )
    up_quads = split_quads(grad_upsampled)
    upward_parts = []
    grad_act_one = jnp.zeros((half_height, half_breadth, C1), jnp.float32)
    for row_tap in range(2):
        for col_tap in range(2):
            offset = (2 * row_tap + col_tap) * C1
            upward_parts.append(contract(act_one, up_quads[row_tap][col_tap]))
            grad_act_one = grad_act_one + back_product(
                up_quads[row_tap][col_tap], upward_full[offset : offset + C1]
            )
    grad_upward = jnp.concatenate(upward_parts, axis=0)
    grad_coarse, gain_grad_one, shift_grad_one = norm_backward(
        grad_act_one, normed_one, spread_one, gain_one, shift_one, coarse_count
    )
    down_parts = []
    for row_tap in range(3):
        local_grad = grad_coarse * coarse_keep if row_tap == 0 else grad_coarse
        for col_tap in range(3):
            down_parts.append(contract(windows[row_tap][col_tap], local_grad))
    grad_down = jnp.concatenate(down_parts, axis=0)
    right_edge = from_behind(grad_coarse[:, :1], "stream", -1)
    extended = jnp.concatenate([grad_coarse, right_edge], axis=1)
    lower_edge = shifted(extended[:1], "dp", -1)
    extended = jnp.concatenate([extended, lower_edge], axis=0)
    extended_keep = keep_rows(first_row + 2 * jnp.arange(half_height + 1), total_rows)[
        :, None, None
    ]
    parity_taps = [[1], [0, 2]]
    back_quads = []
    for row_parity in range(2):
        quad_row = []
        for col_parity in range(2):
            total_piece = jnp.zeros((half_height, half_breadth, channels), jnp.float32)
            for row_tap in parity_taps[row_parity]:
                for col_tap in parity_taps[col_parity]:
                    row_start = 1 if row_tap == 0 else 0
                    col_start = 1 if col_tap == 0 else 0
                    source = extended[
                        row_start : row_start + half_height, col_start : col_start + half_breadth
                    ]
                    if row_tap == 0:
                        source = source * extended_keep[1 : half_height + 1]
                    tap_offset = (3 * row_tap + col_tap) * channels
                    total_piece = total_piece + back_product(
                        source, down_full[tap_offset : tap_offset + channels]
                    )
            quad_row.append(total_piece)
        back_quads.append(quad_row)
    grad_masked = grad_masked + assemble_quads(back_quads)
    feats_grad = grad_masked * occupancy
    down_shard = join_halves(scatter_half(grad_down, 1), 1)
    upward_shard = join_halves(scatter_half(grad_upward, 1), 1)
    merging_shard = join_halves(scatter_half(grad_merging, 0), 0)
    core = lax.axis_index("stream")
    partial_down = contract_rows(down_shard, own_half(down_shard, 1, core))
    partial_upward = contract_rows(upward_shard, own_half(upward_shard, 1, core))
    gram_down = all_halves(partial_down, 1)
    gram_upward = all_halves(partial_upward, 1)
    total_lateral = join_halves(everyone(scatter_half(grad_lateral, 1), "dp").reshape(C0, C1 // 2), 1)
    total_heads, total_bias, gram_merging = sum_small(
        (grad_heads, grad_bias, gram_rows(merging_shard) * 0.5)
    )
    grad_vector = jnp.concatenate(
        [
            gain_grad_one,
            shift_grad_one,
            gain_grad_three,
            shift_grad_three,
            gain_grad_four,
            shift_grad_four,
            gain_grad_five,
            shift_grad_five,
            total_bias,
        ]
    )
    vector_renewed, vector_momentum, vector_variance = adam_vector(
        vector_params, vector_moment, vector_square, grad_vector
    )
    down_renewed, down_momentum, down_variance = soap_step(
        down_weight, down_moment, down_square, down_basis, down_shard, 1.0 / math.sqrt(9 * C0)
    )
    upward_renewed, upward_momentum, upward_variance = soap_step(
        upward_weight,
        upward_moment,
        upward_square,
        upward_basis,
        upward_shard,
        1.0 / math.sqrt(C1),
    )
    lateral_renewed, lateral_momentum, lateral_variance = soap_step(
        lateral_weight,
        lateral_moment,
        lateral_square,
        lateral_basis,
        total_lateral,
        1.0 / math.sqrt(C0),
    )
    merging_renewed, merging_momentum, merging_variance = soap_step(
        merging_weight,
        merging_moment,
        merging_square,
        merging_basis,
        merging_shard,
        1.0 / math.sqrt(18 * C1),
    )
    heads_renewed, heads_momentum, heads_variance = soap_step(
        heads_weight, heads_moment, heads_square, heads_basis, total_heads, 1.0 / math.sqrt(C2)
    )
    (
        (down_gramian, upward_gramian, lateral_gramian, merging_gramian, heads_gramian),
        (down_rotation, upward_rotation, lateral_rotation, merging_rotation, heads_rotation),
    ) = rotations(
        (down_gram, upward_gram, lateral_gram, merging_gram, heads_gram),
        (
            gram_down,
            gram_upward,
            gram_rows(total_lateral),
            gram_merging,
            gram_rows(total_heads),
        ),
        (down_basis, upward_basis, lateral_basis, merging_basis, heads_basis),
    )
    return (
        head_maps,
        feats_grad,
        vector_renewed,
        vector_momentum,
        vector_variance,
        down_renewed,
        down_momentum,
        down_variance,
        down_gramian,
        down_rotation,
        upward_renewed,
        upward_momentum,
        upward_variance,
        upward_gramian,
        upward_rotation,
        lateral_renewed,
        lateral_momentum,
        lateral_variance,
        lateral_gramian,
        lateral_rotation,
        merging_renewed,
        merging_momentum,
        merging_variance,
        merging_gramian,
        merging_rotation,
        heads_renewed,
        heads_momentum,
        heads_variance,
        heads_gramian,
        heads_rotation,
    )


def solution(mesh):
    in_specs = (
        P("dp", "stream", None),
        P("dp", "stream"),
        P("dp", "stream", None),
        P(),
        P(),
        P(),
        P("dp", None),
        P("dp", None),
        P("dp", None),
        P(),
        P(),
        P("dp", None),
        P("dp", None),
        P("dp", None),
        P(),
        P(),
        P(),
        P(),
        P(),
        P(),
        P(),
        P("dp", None),
        P("dp", None),
        P("dp", None),
        P(),
        P(),
        P(),
        P(),
        P(),
        P(),
        P(),
    )
    out_specs = (
        P("dp", "stream", None),
        P("dp", "stream", None),
        P(),
        P(),
        P(),
        P("dp", None),
        P("dp", None),
        P("dp", None),
        P(),
        P(),
        P("dp", None),
        P("dp", None),
        P("dp", None),
        P(),
        P(),
        P(),
        P(),
        P(),
        P(),
        P(),
        P("dp", None),
        P("dp", None),
        P("dp", None),
        P(),
        P(),
        P(),
        P(),
        P(),
        P(),
        P(),
    )
    return jax.shard_map(local, mesh=mesh, in_specs=in_specs, out_specs=out_specs, check_vma=False)
```

```python
import functools
import math

import jax
import jax.numpy as jnp
from jax import lax
from jax.experimental import pallas as pl
from jax.experimental.pallas import tpu as pltpu
from jax.sharding import PartitionSpec as P

C0 = 128
C1 = 256
C2 = 64
CH = 70
SCENE_ROWS = 180
STEP = 10


EPS_NORM = 1e-05
BETA_ONE = 0.9
BETA_TWO = 0.95
BETA_GRAM = 0.95
EPS_ADAM = 1e-08
DECAY = 0.01
VECTOR_RATE = 0.1
HIGHEST = lax.Precision.HIGHEST


F32 = jnp.float32
HIGH = lax.Precision.HIGH
RIM_UP, RIM_DOWN, RIM_LEFT, RIM_RIGHT = 3, 2, 3, 2
LEAD = 10


def product(left, right, over_left, over_right, precision=HIGH):
    dims = (((over_left,), (over_right,)), ((), ()))
    return lax.dot_general(
        left, right, dims, precision=precision, preferred_element_type=F32
    )


def stage(body, outs, args, scalars=(), scratch=(), name=None, flops=0, alias=None):
    vmem = pl.BlockSpec(memory_space=pltpu.VMEM)
    smem = pl.BlockSpec(memory_space=pltpu.SMEM)
    shapes = [jax.ShapeDtypeStruct(shape, F32) for shape in outs]
    moved = 4 * (sum(math.prod(s) for s in outs) + sum(a.size for a in args))
    return pl.pallas_call(
        body,
        out_shape=shapes,
        in_specs=[smem] * len(scalars) + [vmem] * len(args),
        out_specs=[vmem] * len(shapes),
        scratch_shapes=list(scratch),
        compiler_params=pltpu.CompilerParams(vmem_limit_bytes=56 << 20),
        cost_estimate=pl.CostEstimate(flops=3 * flops, transcendentals=0, bytes_accessed=moved),
        name=name,
    )(*scalars, *args)


def channel_sums(ref):
    return jnp.sum(ref[...], axis=0)


def spread_of(total, pixels):
    half = total.shape[1] // 2
    centre = total[:, :half] * (1.0 / pixels)
    second = total[:, half:] * (1.0 / pixels)
    return centre, lax.rsqrt(second - centre * centre + EPS_NORM)


def cols_between(count, lanes, first, past):
    col = lax.broadcasted_iota(jnp.int32, (count, lanes), 0)
    return (col >= first) & (col < past)


def row_total(value):
    return jnp.sum(value, axis=0, keepdims=True)


def send(ref, row):
    ref[...] = jnp.broadcast_to(row[None], ref.shape)


def pad_lateral(masked, up, down, left, right, lateral, grid, z_four, sums):
    height, breadth, channels = masked.shape
    grid[...] = jnp.zeros(grid.shape, F32)
    inner = slice(LEAD, LEAD + breadth)
    grid[0:RIM_UP, inner] = up[...]
    grid[RIM_UP : RIM_UP + height, inner] = masked[...]
    grid[RIM_UP + height :, inner] = down[...]
    grid[:, LEAD - RIM_LEFT : LEAD] = left[...]
    grid[:, LEAD + breadth : LEAD + breadth + RIM_RIGHT] = right[...]
    width = z_four.shape[1]
    own = cols_between(width, C1, 2, 2 + breadth)
    total = jnp.zeros((1, C1), F32)
    square = jnp.zeros((1, C1), F32)
    tile = 6
    for first in range(0, height + 2, tile):
        block = grid[2 + first : 2 + first + tile, LEAD - 2 : LEAD - 2 + width]
        made = product(block.reshape(tile * width, channels), lateral[...], 1, 0)
        made = made.reshape(tile, width, C1)
        z_four[first : first + tile] = made
        for row in range(tile):
            if 1 <= first + row <= height:
                kept = jnp.where(own, made[row], 0.0)
                total = total + row_total(kept)
                square = square + row_total(kept * kept)
    sums[...] = jnp.concatenate([total, square], axis=1)


def coarse_map(flags, grid, weight, sums_four, z_one, windows, sums, window_sums):
    rows, width = z_one.shape[0], z_one.shape[1]
    half_breadth = width - 3
    own = cols_between(width, C0, 1, 1 + half_breadth)
    seen = [jnp.zeros((1, C0), F32) for _ in range(9)]
    for i in range(rows):
        for a in range(3):
            for b in range(3):
                piece = grid[2 * i + a, pl.ds(LEAD - 3 + b, width, 2), :]
                if a == 0:
                    piece = piece * flags[i]
                tap = 3 * a + b
                windows[i, :, tap * C0 : (tap + 1) * C0] = piece
                if 1 <= i < rows - 1:
                    seen[tap] = seen[tap] + row_total(jnp.where(own, piece, 0.0))
    window_sums[...] = jnp.concatenate(seen, axis=1)
    made = product(windows[...].reshape(rows * width, 9 * C0), weight[...], 1, 0)
    z_one[...] = made.reshape(rows, width, C1)
    own = cols_between(width, C1, 1, 1 + half_breadth)
    total = jnp.zeros((1, C1), F32)
    square = jnp.zeros((1, C1), F32)
    for i in range(1, rows - 1):
        kept = jnp.where(own, z_one[i], 0.0)
        total = total + row_total(kept)
        square = square + row_total(kept * kept)
    send(sums, jnp.concatenate([total, square, sums_four[...]], axis=1))


def window_product(windows, other, halves):
    rows, width, depth = windows.shape
    inside = windows[1 : rows - 1].reshape((rows - 2) * width, depth)
    half_breadth = width - 3
    own = cols_between(width, C1, 1, 1 + half_breadth)
    kept = jnp.concatenate(
        [jnp.where(own, other[i], 0.0) for i in range(1, rows - 1)], axis=0
    )
    made = product(inside, kept, 0, 0)
    halves[0] = made[:, : C1 // 2]
    halves[1] = made[:, C1 // 2 :]


def upsample(pixels, z_one, total_one, gain, shift, weight, z_three, act_one, slope_one, sums):
    rows, width = z_one.shape[0], z_one.shape[1]
    half_breadth = width - 3
    centre, spread = spread_of(channel_sums(total_one)[:, : 2 * C1], pixels)
    for i in range(rows):
        hidden = (z_one[i] - centre) * spread * gain[...] + shift[...]
        sigmoid = lax.logistic(hidden)
        act_one[i] = hidden * sigmoid
        slope_one[i] = sigmoid * (1.0 + hidden * (1.0 - sigmoid))
    active = act_one[...].reshape(rows * width, C1)
    own = cols_between(width, C1, 1, 1 + half_breadth)
    total = jnp.zeros((1, C1), F32)
    square = jnp.zeros((1, C1), F32)
    half = C1 // 2
    for a in range(2):
        for b in range(2):
            tap = 2 * a + b
            made = product(active, weight[tap * C1 : (tap + 1) * C1], 1, 0)
            for i in range(rows):
                part = made[i * width : (i + 1) * width]
                place = 2 * i + a - 1
                if 0 <= place < 2 * rows - 2:
                    for k in range(2):
                        z_three[k, place, pl.ds(b, width, 2), :] = part[:, k * half : (k + 1) * half]
                if 1 <= i < rows - 1:
                    kept = jnp.where(own, part, 0.0)
                    total = total + row_total(kept)
                    square = square + row_total(kept * kept)
    send(sums, jnp.concatenate([total, square], axis=1))


def pack_merging(weight, packed):
    for a in range(3):
        pieces = [
            weight[(3 * a + b) * 2 * C1 : (3 * a + b + 1) * 2 * C1] for b in range(3)
        ]
        pieces.append(jnp.zeros((2 * C1, C2), F32))
        packed[:, a * 4 * C2 : (a + 1) * 4 * C2] = jnp.concatenate(pieces, axis=1)


def merge(
    pixels,
    flags,
    z_three,
    z_four,
    total_three,
    total_one,
    norms,
    packed,
    window_sums,
    merged,
    joined,
    slopes,
    sums,
    taps,
):
    rows, width = z_four.shape[0], z_four.shape[1]
    height = rows - 2
    breadth = width - 6
    sum_three = channel_sums(total_three)
    sum_four = channel_sums(total_one)[:, 2 * C1 :]
    centre_three, spread_three = spread_of(sum_three, pixels)
    centre_four, spread_four = spread_of(sum_four, pixels)
    centre = jnp.concatenate([centre_three, centre_four], axis=1)
    spread = jnp.concatenate([spread_three, spread_four], axis=1)
    scale = spread * norms[0:1]
    offset = norms[1:2] - centre * scale
    col = lax.broadcasted_iota(jnp.int32, (width, 2 * C1), 0)
    dead = ((col == 1) & (flags[30] == 0.0)) | ((col == 2 + breadth) & (flags[31] == 0.0))

    def activate(r, carry):
        raw = jnp.concatenate([z_three[0, r], z_three[1, r], z_four[r]], axis=1)
        hidden = raw * scale + offset
        sigmoid = lax.logistic(hidden)
        joined[r] = jnp.where(dead, 0.0, hidden * sigmoid)
        slopes[r] = sigmoid * (1.0 + hidden * (1.0 - sigmoid))
        return carry

    lax.fori_loop(0, rows, activate, 0)
    tile = 6

    def spread_taps(t, carry):
        r = pl.multiple_of(t * tile, tile)
        block = joined[pl.ds(r, tile)].reshape(tile * width, 2 * C1)
        taps[pl.ds(r, tile)] = product(block, packed[...], 1, 0).reshape(tile, width, 12 * C2)
        return carry

    lax.fori_loop(0, rows // tile, spread_taps, 0)
    own = cols_between(width, 2 * C2, 2, 2 + breadth)
    lane = lax.broadcasted_iota(jnp.int32, (width, 2 * C2), 1)
    total = jnp.zeros((1, 2 * C2), F32)
    square = jnp.zeros((1, 2 * C2), F32)
    for row in range(height):
        r = row + 1
        both = (
            taps[r - 1, :, 0 : 4 * C2] * flags[10 + r]
            + taps[r, :, 4 * C2 : 8 * C2]
            + taps[r + 1, :, 8 * C2 : 12 * C2] * flags[11 + r]
        )
        first, second = both[:, : 2 * C2], both[:, 2 * C2 :]
        out = (
            pltpu.roll(first, 1, 0)
            + pltpu.roll(first, C2, 1)
            + pltpu.roll(second, width - 1, 0)
        )
        out = jnp.where(own & (lane < C2), out, 0.0)
        merged[row] = out
        total = total + row_total(out)
        square = square + row_total(out * out)
    send(sums, jnp.concatenate([total, square, window_sums[...]], axis=1))


def heads(
    pixels,
    merged,
    total_five,
    norms,
    weight,
    bias,
    cotangent,
    maps,
    pairs,
    weight_grad,
    sums,
    active,
    upstream,
):
    height, width, _ = merged.shape
    breadth = width - 6
    centre, spread = spread_of(channel_sums(total_five)[:, : 4 * C2], pixels)
    own = cols_between(width, 2 * C2, 2, 2 + breadth)
    upstream[...] = jnp.zeros(upstream.shape, F32)
    for r in range(height):
        upstream[r, 2 : 2 + breadth, 0:CH] = cotangent[r]
    flat = upstream[...].reshape(height * width, 2 * C2)
    grad = product(flat, weight[...], 1, 1).reshape(height, width, 2 * C2)
    grad_gain = jnp.zeros((1, 2 * C2), F32)
    grad_shift = jnp.zeros((1, 2 * C2), F32)
    for r in range(height):
        normed = jnp.where(own, (merged[r] - centre) * spread, 0.0)
        hidden = norms[0:1] * normed + norms[1:2]
        sigmoid = lax.logistic(hidden)
        active[r] = hidden * sigmoid
        grad_hidden = grad[r] * sigmoid * (1.0 + hidden * (1.0 - sigmoid))
        pairs[r] = grad_hidden + pltpu.roll(normed, C2, 1)
        grad_gain = grad_gain + row_total(grad_hidden * normed)
        grad_shift = grad_shift + row_total(grad_hidden)
    send(sums, jnp.concatenate([grad_gain, grad_shift, row_total(flat)], axis=1))
    act = active[...].reshape(height * width, 2 * C2)
    made = product(act, weight[...], 1, 0).reshape(height, width, 2 * C2) + bias[...]
    for r in range(height):
        maps[r] = made[r, 2 : 2 + breadth, 0:CH]
    weight_grad[...] = product(act, flat, 0, 0)


def merged_gradient(
    pixels,
    flags,
    pairs,
    above,
    below,
    left,
    right,
    total_five,
    grads_five,
    norm_five,
    packed,
    z_three,
    z_four,
    slopes,
    total_three,
    total_one,
    grad_joined,
    columns,
    sums,
):
    height, width, _ = pairs.shape
    breadth = width - 6
    lanes = 2 * C2
    _, spread = spread_of(channel_sums(total_five)[:, : 4 * C2], pixels)
    gained = channel_sums(grads_five)
    scale = norm_five[0:1] * spread
    mean_gain = gained[:, :lanes] * (1.0 / pixels)
    mean_shift = gained[:, lanes : 2 * lanes] * (1.0 / pixels)
    col = lax.broadcasted_iota(jnp.int32, (width, lanes), 0)
    lane = lax.broadcasted_iota(jnp.int32, (width, lanes), 1)
    live = (
        ((col >= 2) & (col < 2 + breadth))
        | ((col == 1) & (flags[30] != 0.0))
        | ((col == 2 + breadth) & (flags[31] != 0.0))
    ) & (lane < C2)
    for r in range(height + 2):
        if r == 0:
            raw = above[0]
        elif r == height + 1:
            raw = below[0]
        else:
            raw = pairs[r - 1]
        raw = jnp.where(col == 1, left[r], jnp.where(col == 2 + breadth, right[r], raw))
        normed = pltpu.roll(raw, C2, 1)
        value = jnp.where(live, scale * (raw - mean_shift - normed * mean_gain), 0.0)
        columns[r, :, 0:lanes] = pltpu.roll(value, width - 1, 0) + pltpu.roll(value, C2, 1)
        columns[r, :, lanes:] = pltpu.roll(value, 1, 0)
    centre_three, spread_three = spread_of(channel_sums(total_three), pixels)
    centre_four, spread_four = spread_of(channel_sums(total_one)[:, 2 * C1 :], pixels)
    centre = jnp.concatenate([centre_three, centre_four], axis=1)
    spread = jnp.concatenate([spread_three, spread_four], axis=1)
    own = cols_between(width, 2 * C1, 2, 2 + breadth)
    tile = 4

    def gradient(t, carry):
        r = t * tile
        block = jnp.zeros((tile * width, 2 * C1), F32)
        for a in range(3):
            rows = []
            for k in range(tile):
                source = r + k + 2 - a
                row = columns[source]
                if a == 0:
                    row = row * flags[10 + source]
                if a == 2:
                    row = row * flags[11 + source]
                rows.append(row)
            block = block + product(
                jnp.concatenate(rows, axis=0), packed[:, a * 4 * C2 : (a + 1) * 4 * C2], 1, 1
            )
        gain_sum, shift_sum = carry
        for k in range(tile):
            grad = jnp.where(own, block[k * width : (k + 1) * width] * slopes[r + k + 1], 0.0)
            grad_joined[r + k] = grad
            raw = jnp.concatenate(
                [z_three[0, r + k + 1], z_three[1, r + k + 1], z_four[r + k + 1]], axis=1
            )
            normed = (raw - centre) * spread
            gain_sum = gain_sum + row_total(grad * normed)
            shift_sum = shift_sum + row_total(grad)
        return gain_sum, shift_sum

    empty = jnp.zeros((1, 2 * C1), F32)
    gain_sum, shift_sum = lax.fori_loop(0, height // tile, gradient, (empty, empty))
    send(sums, jnp.concatenate([gain_sum, shift_sum], axis=1))


def merging_product(flags, joined, columns, grads, shifted_rows):
    rows, width, _ = joined.shape
    height = rows - 2
    inside = joined[1 : rows - 1].reshape(height * width, 2 * C1)
    own = cols_between(width, 4 * C2, 2, width - 4)
    for a in range(3):
        for r in range(height):
            source = r + 2 - a
            row = columns[source]
            if a == 0:
                row = row * flags[10 + source]
            if a == 2:
                row = row * flags[11 + source]
            shifted_rows[r] = jnp.where(own, row, 0.0)
        made = product(inside, shifted_rows[...].reshape(height * width, 4 * C2), 0, 0)
        for b in range(3):
            grads[(3 * a + b) * 2 * C1 : (3 * a + b + 1) * 2 * C1] = made[:, b * C2 : (b + 1) * C2]


def coarse_gradient(
    pixels,
    coarse_pixels,
    grad_joined,
    z_three,
    total_three,
    grads_joined,
    gain_three,
    weight,
    z_one,
    total_one,
    slope_one,
    quads,
    grad_one,
    sums,
    fine,
):
    height, width = grad_joined.shape[0], grad_joined.shape[1]
    rows, half_width = z_one.shape[0], z_one.shape[1]
    half = C1 // 2
    centre, spread = spread_of(channel_sums(total_three), pixels)
    gained = channel_sums(grads_joined)
    scale = gain_three[...] * spread
    mean_gain = gained[:, :C1] * (1.0 / pixels)
    mean_shift = gained[:, 2 * C1 : 3 * C1] * (1.0 / pixels)
    own = cols_between(width, C1, 2, width - 4)

    def fill(r, carry):
        raw = jnp.concatenate([z_three[0, r + 1], z_three[1, r + 1]], axis=1)
        normed = (raw - centre) * spread
        value = scale * (grad_joined[r, :, 0:C1] - mean_shift - normed * mean_gain)
        value = jnp.where(own, value, 0.0)
        fine[0, r] = value[:, :half]
        fine[1, r] = value[:, half:]
        return carry

    lax.fori_loop(0, height, fill, 0)
    grad = jnp.zeros(((rows - 2) * half_width, C1), F32)
    for a in range(2):
        for b in range(2):
            tap = 2 * a + b
            for i in range(rows - 2):
                for k in range(2):
                    quads[tap, i, :, k * half : (k + 1) * half] = fine[
                        k, 2 * i + a, pl.ds(b, half_width, 2), :
                    ]
            flat = quads[tap].reshape((rows - 2) * half_width, C1)
            grad = grad + product(flat, weight[tap * C1 : (tap + 1) * C1], 1, 1)
    centre, spread = spread_of(channel_sums(total_one)[:, : 2 * C1], coarse_pixels)
    own = cols_between(half_width, C1, 1, half_width - 2)
    gain_sum = jnp.zeros((1, C1), F32)
    shift_sum = jnp.zeros((1, C1), F32)
    grad_one[0] = jnp.zeros((half_width, C1), F32)
    grad_one[rows - 1] = jnp.zeros((half_width, C1), F32)
    for i in range(1, rows - 1):
        value = grad[(i - 1) * half_width : i * half_width] * slope_one[i]
        value = jnp.where(own, value, 0.0)
        grad_one[i] = value
        gain_sum = gain_sum + row_total(value * ((z_one[i] - centre) * spread))
        shift_sum = shift_sum + row_total(value)
    send(sums, jnp.concatenate([gain_sum, shift_sum], axis=1))


def fine_products(
    pixels,
    grad_joined,
    z_four,
    total_one,
    grads_joined,
    gain_four,
    lateral,
    grid,
    act_one,
    quads,
    upward_halves,
    lateral_halves,
    grad_masked,
    fine,
):
    height, width = grad_joined.shape[0], grad_joined.shape[1]
    rows, half_width = act_one.shape[0], act_one.shape[1]
    half = C1 // 2
    centre, spread = spread_of(channel_sums(total_one)[:, 2 * C1 :], pixels)
    gained = channel_sums(grads_joined)
    scale = gain_four[...] * spread
    mean_gain = gained[:, C1 : 2 * C1] * (1.0 / pixels)
    mean_shift = gained[:, 3 * C1 :] * (1.0 / pixels)
    own = cols_between(width, C1, 2, width - 4)

    def fill(r, carry):
        normed = (z_four[r + 1] - centre) * spread
        value = scale * (grad_joined[r, :, C1:] - mean_shift - normed * mean_gain)
        fine[r] = jnp.where(own, value, 0.0)
        return carry

    lax.fori_loop(0, height, fill, 0)
    flat = fine[...].reshape(height * width, C1)
    source = grid[RIM_UP : RIM_UP + height, LEAD - 2 : LEAD - 2 + width]
    made = product(source.reshape(height * width, C0), flat, 0, 0)
    lateral_halves[0] = made[:, :half]
    lateral_halves[1] = made[:, half:]
    back = product(flat, lateral[...], 1, 1)
    grad_masked[...] = back.reshape(height, width, C0)
    inside = act_one[1 : rows - 1].reshape((rows - 2) * half_width, C1)
    for tap in range(4):
        other = quads[tap].reshape((rows - 2) * half_width, C1)
        made = product(inside, other, 0, 0)
        for k in range(2):
            upward_halves[k, tap * C1 : (tap + 1) * C1] = made[:, k * half : (k + 1) * half]


def input_gradient(
    coarse_pixels,
    flags,
    grad_one,
    below,
    right,
    z_one,
    total_one,
    grads_one,
    gain_one,
    weight,
    grad_masked,
    occupancy,
    out,
    taps,
    fine,
):
    rows, half_width = z_one.shape[0], z_one.shape[1]
    height, breadth = out.shape[0], out.shape[1]
    centre, spread = spread_of(channel_sums(total_one)[:, : 2 * C1], coarse_pixels)
    gained = channel_sums(grads_one)
    scale = gain_one[...] * spread
    mean_gain = gained[:, :C1] * (1.0 / coarse_pixels)
    mean_shift = gained[:, C1:] * (1.0 / coarse_pixels)
    col = lax.broadcasted_iota(jnp.int32, (half_width, C1), 0)
    edge = half_width - 2
    live = ((col >= 1) & (col < edge)) | ((col == edge) & (flags[31] != 0.0))
    parts = []
    for i in range(1, rows):
        raw = grad_one[i] if i < rows - 1 else below[0]
        raw = jnp.where(col == edge, right[i - 1], raw)
        normed = (z_one[i] - centre) * spread
        value = scale * (raw - mean_shift - normed * mean_gain)
        parts.append(jnp.where(live, value, 0.0))
    made = product(jnp.concatenate(parts, axis=0), weight[...], 1, 1)
    taps[...] = made.reshape(rows - 1, half_width, 9 * C0)

    def tap(a, b, i):
        value = taps[i, :, (3 * a + b) * C0 : (3 * a + b + 1) * C0]
        if b == 0:
            value = pltpu.roll(value, half_width - 1, 0)
        if a == 0:
            value = value * flags[i + 1]
        return value

    for i in range(rows - 2):
        fine[2 * i, pl.ds(0, half_width, 2), :] = tap(1, 1, i)
        fine[2 * i, pl.ds(1, half_width, 2), :] = tap(1, 2, i) + tap(1, 0, i)
        fine[2 * i + 1, pl.ds(0, half_width, 2), :] = tap(2, 1, i) + tap(0, 1, i + 1)
        fine[2 * i + 1, pl.ds(1, half_width, 2), :] = (
            tap(2, 2, i) + tap(2, 0, i) + tap(0, 2, i + 1) + tap(0, 0, i + 1)
        )
    for r in range(height):
        total = fine[r] + grad_masked[r]
        out[r] = total[2 : 2 + breadth] * occupancy[r]


def dot(a,b,ca,cb):
    return lax.dot_general(a,b,(((ca,),(cb,)),((),())),precision=HIGHEST,preferred_element_type=F32)
NB=32
def base_inverse(blocks):
    lane=lax.broadcasted_iota(jnp.int32,(NB,128),1); row=lax.broadcasted_iota(jnp.int32,(NB,128),0)
    eye=(lane==row+NB).astype(F32)
    xs=[jnp.concatenate([b,jnp.zeros((NB,128-NB),F32)],axis=1)+eye for b in blocks]
    for k in range(NB):
        nx=[]
        for x in xs:
            col=jnp.broadcast_to(x[:,k:k+1],(NB,128))
            piv=col[k:k+1,:]
            r=x[k:k+1,:]*(1.0/piv)
            nx.append(x-jnp.where(row>k,col,0.0)*r)
        xs=nx
    outs=[]
    for x in xs:
        d=jnp.sum(jnp.where(lane==row,x,0.0),axis=1,keepdims=True)
        y=x*lax.rsqrt(d)
        outs.append(y[:,NB:2*NB])
    return outs
def kern(ns,*refs):
    m=len(ns)
    gram=refs[0:m]; add=refs[m:2*m]; basis=refs[2*m:3*m]
    out_gram=refs[3*m:4*m]; out_rot=refs[4*m:5*m]
    aa=refs[5*m:6*m]; xx=refs[6*m:7*m]
    prods=[]
    for i,n in enumerate(ns):
        g=0.95*gram[i][...]+0.05*add[i][...]
        out_gram[i][...]=g
        p=dot(g,basis[i][...],1,0)
        out_rot[i][...]=p
        a=dot(p,p,0,0)
        npad=aa[i].shape[0]
        if npad!=n:
            r=lax.broadcasted_iota(jnp.int32,(npad,npad),0); c=lax.broadcasted_iota(jnp.int32,(npad,npad),1)
            aa[i][...]=((r==c)&(r>=n)).astype(F32)
            aa[i][0:n,0:n]=a
        else:
            aa[i][...]=a
        r=lax.broadcasted_iota(jnp.int32,(npad,npad),0); c=lax.broadcasted_iota(jnp.int32,(npad,npad),1)
        xx[i][...]=(r==c).astype(F32)
    for b in range(max(a.shape[0] for a in aa)//NB):
        s=b*NB
        live=[i for i in range(m) if s<aa[i].shape[0]]
        inv=base_inverse([aa[i][s:s+NB,s:s+NB] for i in live])
        for i,li in zip(live,inv):
            npad=aa[i].shape[0]
            e=s+NB
            y=dot(li,xx[i][s:e,:],1,0)
            xx[i][s:e,:]=y
            if e<npad:
                rpan=dot(li,aa[i][s:e,e:],1,0)
                cpan=dot(aa[i][e:,s:e],li,1,1)
                aa[i][e:,e:]=aa[i][e:,e:]-dot(cpan,rpan,1,0)
                xx[i][e:,:]=xx[i][e:,:]-dot(cpan,y,1,0)
    for i,n in enumerate(ns):
        out_rot[i][...]=dot(out_rot[i][...],xx[i][0:n,0:n],1,1)
def rotations(grams,adds,bases):
    ns=[g.shape[0] for g in grams]
    pads=[-(-n//NB)*NB for n in ns]
    outs=pl.pallas_call(functools.partial(kern,ns),
        out_shape=[jax.ShapeDtypeStruct((n,n),F32) for n in ns]*2,
        scratch_shapes=[pltpu.VMEM((p,p),F32) for p in pads]*2,
        compiler_params=pltpu.CompilerParams(vmem_limit_bytes=32<<20),
        name='rotate')(*grams,*adds,*bases)
    return outs[:len(ns)],outs[len(ns):]


def keep_rows(global_rows, total_rows):
    wrapped = jnp.remainder(global_rows, total_rows)
    return ((wrapped + SCENE_ROWS // 2) % SCENE_ROWS != 0).astype(jnp.float32)


def from_behind(block, axis, distance):
    devices = range(lax.axis_size(axis))
    route = [(i - distance, i) for i in devices if i - distance in devices]
    return lax.ppermute(block, axis, route)


def shifted(value, axis, steps):
    count = lax.axis_size(axis)
    pairs = [(source, (source + steps) % count) for source in range(count)]
    return lax.ppermute(value, axis, pairs)


def exchange(value):
    return lax.ppermute(value, "stream", [(0, 1), (1, 0)])


def to_all(rows):
    return lax.all_to_all(rows, ("dp", "stream"), 0, 0, tiled=True)


def everyone(value):
    count = lax.axis_size("dp")
    copies = jnp.broadcast_to(value[None], (count,) + value.shape)
    return lax.all_to_all(copies, "dp", 0, 0, tiled=True)


def in_order(mine, other):
    first = lax.axis_index("stream") == 0
    return jnp.where(first, mine, other), jnp.where(first, other, mine)


def join_lanes(mine):
    return jnp.concatenate(in_order(mine, exchange(mine)), axis=-1)


def pick(pair, axis, which):
    return lax.dynamic_index_in_dim(pair, which, axis, keepdims=False)


def scatter(pair):
    core = lax.axis_index("stream")
    mine = pick(pair, 0, core) + exchange(pick(pair, 0, 1 - core))
    return jnp.sum(lax.all_to_all(mine, "dp", 0, 0, tiled=True), axis=0)


def by_shard(halves):
    count = lax.axis_size("dp")
    short = -halves.shape[1] % count
    if short:
        halves = jnp.pad(halves, ((0, 0), (0, short), (0, 0)))
    return halves.reshape(2, count, halves.shape[1] // count, halves.shape[2])


def fold_rows(rows, count):
    parts = rows.reshape(count, 2, 2, rows.shape[0] // (4 * count), C2)
    return jnp.swapaxes(jnp.concatenate([parts[:, :, 0], parts[:, :, 1]], axis=-1), 0, 1)


def unfold_rows(first, second):
    both = jnp.stack([first, second], axis=1)
    parts = jnp.stack([both[..., :C2], both[..., C2:]], axis=2)
    return parts.reshape(-1, C2)


def lanes_of(row, width):
    return jnp.pad(row, (0, width - row.shape[0]))[None]


def adam_vector(params, moment, square, gradient):
    momentum = BETA_ONE * moment + (1.0 - BETA_ONE) * gradient
    variance = BETA_TWO * square + (1.0 - BETA_TWO) * gradient * gradient
    direction = (
        momentum / (1.0 - BETA_ONE**STEP) / (jnp.sqrt(variance / (1.0 - BETA_TWO**STEP)) + EPS_ADAM)
    )
    return (params - VECTOR_RATE * (direction + DECAY * params), momentum, variance)


def soap_body(rates, *refs):
    count = len(rates)
    ins, outs = refs[: 5 * count], refs[5 * count :]
    for i, rate in enumerate(rates):
        weight, moment, square, basis, gradient = (ref[...] for ref in ins[5 * i : 5 * i + 5])
        rotated = product(gradient, basis, 1, 0, HIGHEST)
        momentum = BETA_ONE * moment + (1.0 - BETA_ONE) * rotated
        variance = BETA_TWO * square + (1.0 - BETA_TWO) * rotated * rotated
        direction = momentum * (1.0 / (1.0 - BETA_ONE**STEP)) / (
            jnp.sqrt(variance * (1.0 / (1.0 - BETA_TWO**STEP))) + EPS_ADAM
        )
        turned = product(direction, basis, 1, 1, HIGHEST)
        outs[3 * i][...] = weight - rate * (turned + DECAY * weight)
        outs[3 * i + 1][...] = momentum
        outs[3 * i + 2][...] = variance


def soap_steps(rates, *groups):
    outs = [group[0].shape for group in groups for _ in range(3)]
    args = [array for group in groups for array in group]
    made = stage(functools.partial(soap_body, rates), outs, args, name="soap")
    return [made[3 * i : 3 * i + 3] for i in range(len(groups))]


def local(
    feats,
    occupied,
    cotangent,
    vector_params,
    vector_moment,
    vector_square,
    down_weight,
    down_moment,
    down_square,
    down_gram,
    down_basis,
    upward_weight,
    upward_moment,
    upward_square,
    upward_gram,
    upward_basis,
    lateral_weight,
    lateral_moment,
    lateral_square,
    lateral_gram,
    lateral_basis,
    merging_weight,
    merging_moment,
    merging_square,
    merging_gram,
    merging_basis,
    heads_weight,
    heads_moment,
    heads_square,
    heads_gram,
    heads_basis,
):
    height, breadth, _ = feats.shape
    half_height, half_breadth = height // 2, breadth // 2
    shards = lax.axis_size("dp")
    cores = lax.axis_size("stream")
    everybody = shards * cores
    total_rows = height * shards
    fine_count = float(height * breadth * everybody)
    coarse_count = fine_count / 4.0
    shard_index, core = lax.axis_index("dp"), lax.axis_index("stream")
    first_row = shard_index * height
    width, half_width = breadth + 6, half_breadth + 3
    rows, half_rows = height + 2, half_height + 2
    flags = jnp.concatenate(
        [
            keep_rows(first_row + 2 * jnp.arange(-1, half_height + 1), total_rows),
            keep_rows(first_row + jnp.arange(-1, height + 3), total_rows),
            (core != 0).astype(F32)[None],
            (core != cores - 1).astype(F32)[None],
        ]
    )
    gains = [vector_params[i * C1 : (i + 1) * C1] for i in range(6)]
    late = 6 * C1
    gain_five, shift_five = vector_params[late : late + C2], vector_params[late + C2 : late + 2 * C2]
    head_bias = vector_params[late + 2 * C2 :]
    wide = 2 * C2
    norm_fine = jnp.stack(
        [jnp.concatenate([gains[2], gains[4]]), jnp.concatenate([gains[3], gains[5]])]
    )
    norm_five = jnp.concatenate([lanes_of(gain_five, wide), lanes_of(shift_five, wide)])

    down_half = pick(down_weight.reshape(-1, 2, C1 // 2), 1, core)
    down_full = join_lanes(everyone(down_half).reshape(-1, C1 // 2))

    occupancy = occupied.astype(F32)[..., None]
    masked = feats * occupancy
    shown = jnp.broadcast_to(occupancy, feats.shape)
    up = shifted(masked[height - RIM_UP :], "dp", 1)
    down = shifted(masked[:RIM_DOWN], "dp", -1)
    edges = jnp.concatenate([up, masked, down], axis=0)
    left = from_behind(edges[:, breadth - RIM_LEFT :], "stream", 1)
    right = from_behind(edges[:, :RIM_RIGHT], "stream", -1)
    grid, z_four, sums_four = stage(
        pad_lateral,
        [
            (height + RIM_UP + RIM_DOWN, width + LEAD - 2, C0),
            (rows, width, C1),
            (1, 2 * C1),
        ],
        [masked, up, down, left, right, lateral_weight],
        name="pad_lateral",
    )

    z_one, windows, sums_one, window_sums = stage(
        coarse_map,
        [
            (half_rows, half_width, C1),
            (half_rows, half_width, 9 * C0),
            (everybody, 1, 4 * C1),
            (1, 9 * C0),
        ],
        [grid, down_full, sums_four],
        scalars=[flags],
        name="coarse",
    )
    total_one = to_all(sums_one)

    upward_half = pick(upward_weight.reshape(-1, 2, C1 // 2), 1, core)
    upward_full = join_lanes(everyone(upward_half).reshape(-1, C1 // 2))
    merging_half = pick(fold_rows(merging_weight, 1), 0, core)[0]
    merging_all = everyone(merging_half)
    merging_full = unfold_rows(*in_order(merging_all, exchange(merging_all)))
    (packed,) = stage(pack_merging, [(2 * C1, 12 * C2)], [merging_full], name="pack")

    (early_halves,) = stage(
        window_product, [(2, 9 * C0, C1 // 2)], [windows, z_one], name="window_one"
    )

    z_three, act_one, slope_one, sums_three = stage(
        functools.partial(upsample, coarse_count),
        [
            (2, rows, width, C1 // 2),
            (half_rows, half_width, C1),
            (half_rows, half_width, C1),
            (everybody, 1, 2 * C1),
        ],
        [z_one, total_one, gains[0][None], gains[1][None], upward_full],
        name="upsample",
    )
    total_three = to_all(sums_three)
    window_one = scatter(by_shard(early_halves))

    merged, joined, slopes, sums_five = stage(
        functools.partial(merge, fine_count),
        [
            (height, width, wide),
            (rows, width, 2 * C1),
            (rows, width, 2 * C1),
            (everybody, 1, 2 * wide + 9 * C0),
        ],
        [z_three, z_four, total_three, total_one, norm_fine, packed, window_sums],
        scalars=[flags],
        scratch=[pltpu.VMEM((rows, width, 12 * C2), F32)],
        name="merge",
    )
    total_five = to_all(sums_five)

    heads_padded = jnp.pad(heads_weight, ((0, wide - C2), (0, wide - CH)))
    head_maps, pairs, heads_grad, grad_sums_five = stage(
        functools.partial(heads, fine_count),
        [
            (height, breadth, CH),
            (height, width, wide),
            (wide, wide),
            (everybody, 1, 3 * wide),
        ],
        [merged, total_five, norm_five, heads_padded, lanes_of(head_bias, wide), cotangent],
        scratch=[pltpu.VMEM((height, width, wide), F32)] * 2,
        name="heads",
    )
    grads_five = to_all(grad_sums_five)
    above = shifted(pairs[height - 1 :], "dp", 1)
    below = shifted(pairs[:1], "dp", -1)
    rim = [
        jnp.concatenate([above[:, c : c + 1], pairs[:, c : c + 1], below[:, c : c + 1]], axis=0)
        for c in (1 + breadth, 2)
    ]
    left = from_behind(rim[0], "stream", 1)
    right = from_behind(rim[1], "stream", -1)

    grad_joined, columns, grad_sums = stage(
        functools.partial(merged_gradient, fine_count),
        [
            (height, width, 2 * C1),
            (rows, width, 4 * C2),
            (everybody, 1, 4 * C1),
        ],
        [
            pairs,
            above,
            below,
            left,
            right,
            total_five,
            grads_five,
            norm_five,
            packed,
            z_three,
            z_four,
            slopes,
            total_three,
            total_one,
        ],
        scalars=[flags],
        name="merged_gradient",
    )
    grads_joined = to_all(grad_sums)
    (merging_grad,) = stage(
        merging_product,
        [(18 * C1, C2)],
        [joined, columns],
        scalars=[flags],
        scratch=[pltpu.VMEM((height, width, 4 * C2), F32)],
        name="merging_product",
    )
    merging_part = scatter(fold_rows(merging_grad, shards))

    quads, grad_one, grad_sums_one = stage(
        functools.partial(coarse_gradient, fine_count, coarse_count),
        [
            (4, half_height, half_width, C1),
            (half_rows, half_width, C1),
            (everybody, 1, 2 * C1),
        ],
        [
            grad_joined,
            z_three,
            total_three,
            grads_joined,
            gains[2][None],
            upward_full,
            z_one,
            total_one,
            slope_one,
        ],
        scratch=[pltpu.VMEM((2, height, width, C1 // 2), F32)],
        name="coarse_gradient",
    )
    grads_one = to_all(grad_sums_one)
    (late_halves,) = stage(
        window_product, [(2, 9 * C0, C1 // 2)], [windows, grad_one], name="window_two"
    )
    window_two = scatter(by_shard(late_halves))

    upward_halves, lateral_halves, grad_masked = stage(
        functools.partial(fine_products, fine_count),
        [(2, 4 * C1, C1 // 2), (2, C0, C1 // 2), (height, width, C0)],
        [
            grad_joined,
            z_four,
            total_one,
            grads_joined,
            gains[4][None],
            lateral_weight,
            grid,
            act_one,
            quads,
        ],
        scratch=[pltpu.VMEM((height, width, C1), F32)],
        name="fine_products",
    )
    heads_halves = heads_grad[:C2].reshape(2, C2 // 2, wide)
    blocks = [by_shard(value) for value in (upward_halves, lateral_halves, heads_halves)]
    cuts = [0]
    for block in blocks:
        cuts.append(cuts[-1] + block.shape[2])
    part = scatter(jnp.concatenate(blocks, axis=2))
    upward_part, small_part = part[: cuts[1]], part[cuts[1] :]

    below = shifted(grad_one[1:2], "dp", -1)
    first_col = jnp.concatenate([grad_one[1 : half_rows - 1, 1:2], below[:, 1:2]], axis=0)
    right = from_behind(first_col, "stream", -1)
    (feats_grad,) = stage(
        functools.partial(input_gradient, coarse_count),
        [(height, breadth, C0)],
        [
            grad_one,
            below,
            right,
            z_one,
            total_one,
            grads_one,
            gains[0][None],
            down_full,
            grad_masked,
            shown,
        ],
        scalars=[flags],
        scratch=[
            pltpu.VMEM((half_rows - 1, half_width, 9 * C0), F32),
            pltpu.VMEM((height, width, C0), F32),
        ],
        name="input_gradient",
    )

    totals_one = jnp.sum(total_one[:, 0, : 2 * C1], axis=0)
    sums_back = jnp.sum(grads_one[:, 0], axis=0)
    centre = totals_one[:C1] / coarse_count
    spread = lax.rsqrt(totals_one[C1:] / coarse_count - centre * centre + EPS_NORM)
    mean_gain, mean_shift = sums_back[:C1] / coarse_count, sums_back[C1:] / coarse_count
    seen = jnp.sum(total_five[:, 0, 2 * wide :], axis=0).reshape(shards, -1)
    seen = lax.dynamic_index_in_dim(seen, shard_index, 0, keepdims=False)[:, None]
    column = core * (C1 // 2)

    def half_of(row):
        return lax.dynamic_slice_in_dim(row, column, C1 // 2, 0)[None]

    down_part = half_of(gains[0] * spread) * (
        window_two
        - seen * half_of(mean_shift)
        - (window_one - seen * half_of(centre)) * half_of(spread * mean_gain)
    )
    down_shard = join_lanes(down_part)
    upward_shard = join_lanes(upward_part)
    merging_shard = unfold_rows(*[v[None] for v in in_order(merging_part, exchange(merging_part))])

    def partial_gram(shard):
        return jnp.tensordot(shard, shard, axes=((0,), (0,)), precision=HIGHEST)

    def whole_gram(partials):
        pieces = [p.reshape(shards, -1) for p in partials]
        flat = jnp.concatenate(pieces, axis=1)
        return jnp.sum(lax.all_to_all(flat[:, None], "dp", 0, 0, tiled=True), axis=0)[0]

    early_sum = whole_gram([partial_gram(upward_shard), partial_gram(merging_shard)])
    lanes = C1 // 2
    early_all = everyone(jnp.concatenate([early_sum, small_part.reshape(-1)])[None])[:, 0]
    edge = C1 * C1 // shards
    gram_upward = early_all[:, :edge].reshape(C1, C1)
    gram_merging = early_all[:, edge : early_sum.shape[0]].reshape(C2, C2)
    small_all = early_all[:, early_sum.shape[0] :].reshape(shards, -1, lanes)
    small_first, small_second = in_order(small_all, exchange(small_all))
    split = cuts[2] - cuts[1]
    total_lateral = jnp.concatenate(
        [small_first[:, :split].reshape(-1, lanes), small_second[:, :split].reshape(-1, lanes)],
        axis=1,
    )
    total_heads = jnp.concatenate(
        [
            small_first[:, split:].reshape(-1, lanes)[: C2 // 2],
            small_second[:, split:].reshape(-1, lanes)[: C2 // 2],
        ],
        axis=0,
    )[:, :CH]
    down_parts = partial_gram(down_shard).reshape(shards, -1, C1)
    gram_part = jnp.sum(lax.all_to_all(down_parts, "dp", 0, 0, tiled=True), axis=0)
    gram_down = everyone(gram_part).reshape(C1, C1)

    sums_fine = jnp.sum(grads_joined[:, 0], axis=0)
    sums_late = jnp.sum(grads_five[:, 0], axis=0)
    grad_vector = jnp.concatenate(
        [
            sums_back,
            sums_fine[:C1],
            sums_fine[2 * C1 : 3 * C1],
            sums_fine[C1 : 2 * C1],
            sums_fine[3 * C1 :],
            sums_late[:C2],
            sums_late[wide : wide + C2],
            sums_late[2 * wide : 2 * wide + CH],
        ]
    )
    vector_renewed, vector_momentum, vector_variance = adam_vector(
        vector_params, vector_moment, vector_square, grad_vector
    )
    (
        (upward_renewed, upward_momentum, upward_variance),
        (lateral_renewed, lateral_momentum, lateral_variance),
        (merging_renewed, merging_momentum, merging_variance),
        (heads_renewed, heads_momentum, heads_variance),
    ) = soap_steps(
        (1.0 / math.sqrt(C1), 1.0 / math.sqrt(C0), 1.0 / math.sqrt(18 * C1), 1.0 / math.sqrt(C2)),
        (upward_weight, upward_moment, upward_square, upward_basis, upward_shard),
        (lateral_weight, lateral_moment, lateral_square, lateral_basis, total_lateral),
        (merging_weight, merging_moment, merging_square, merging_basis, merging_shard),
        (heads_weight, heads_moment, heads_square, heads_basis, total_heads),
    )
    ((down_renewed, down_momentum, down_variance),) = soap_steps(
        (1.0 / math.sqrt(9 * C0),),
        (down_weight, down_moment, down_square, down_basis, down_shard),
    )
    (
        (down_gramian, upward_gramian, lateral_gramian, merging_gramian, heads_gramian),
        (down_rotation, upward_rotation, lateral_rotation, merging_rotation, heads_rotation),
    ) = rotations(
        (down_gram, upward_gram, lateral_gram, merging_gram, heads_gram),
        (
            gram_down,
            gram_upward,
            partial_gram(total_lateral),
            gram_merging,
            partial_gram(total_heads),
        ),
        (down_basis, upward_basis, lateral_basis, merging_basis, heads_basis),
    )
    return (
        head_maps,
        feats_grad,
        vector_renewed,
        vector_momentum,
        vector_variance,
        down_renewed,
        down_momentum,
        down_variance,
        down_gramian,
        down_rotation,
        upward_renewed,
        upward_momentum,
        upward_variance,
        upward_gramian,
        upward_rotation,
        lateral_renewed,
        lateral_momentum,
        lateral_variance,
        lateral_gramian,
        lateral_rotation,
        merging_renewed,
        merging_momentum,
        merging_variance,
        merging_gramian,
        merging_rotation,
        heads_renewed,
        heads_momentum,
        heads_variance,
        heads_gramian,
        heads_rotation,
    )


def solution(mesh):
    in_specs = (
        P("dp", "stream", None),
        P("dp", "stream"),
        P("dp", "stream", None),
        P(),
        P(),
        P(),
        P("dp", None),
        P("dp", None),
        P("dp", None),
        P(),
        P(),
        P("dp", None),
        P("dp", None),
        P("dp", None),
        P(),
        P(),
        P(),
        P(),
        P(),
        P(),
        P(),
        P("dp", None),
        P("dp", None),
        P("dp", None),
        P(),
        P(),
        P(),
        P(),
        P(),
        P(),
        P(),
    )
    out_specs = (
        P("dp", "stream", None),
        P("dp", "stream", None),
        P(),
        P(),
        P(),
        P("dp", None),
        P("dp", None),
        P("dp", None),
        P(),
        P(),
        P("dp", None),
        P("dp", None),
        P("dp", None),
        P(),
        P(),
        P(),
        P(),
        P(),
        P(),
        P(),
        P("dp", None),
        P("dp", None),
        P("dp", None),
        P(),
        P(),
        P(),
        P(),
        P(),
        P(),
        P(),
    )
    return jax.shard_map(local, mesh=mesh, in_specs=in_specs, out_specs=out_specs, check_vma=False)
```

```python
import functools
import math

import jax
import jax.numpy as jnp
from jax import lax
from jax.experimental import pallas as pl
from jax.experimental.pallas import tpu as pltpu
from jax.sharding import PartitionSpec as P

C0 = 128
C1 = 256
C2 = 64
CH = 70
SCENE_ROWS = 180
STEP = 10


EPS_NORM = 1e-05
BETA_ONE = 0.9
BETA_TWO = 0.95
BETA_GRAM = 0.95
EPS_ADAM = 1e-08
DECAY = 0.01
VECTOR_RATE = 0.1
HIGHEST = lax.Precision.HIGHEST


F32 = jnp.float32
HIGH = lax.Precision.HIGH
RIM_UP, RIM_DOWN, RIM_LEFT, RIM_RIGHT = 3, 2, 3, 2
LEAD = 10
NEAR = 4


def product(left, right, over_left, over_right, precision=HIGH):
    dims = (((over_left,), (over_right,)), ((), ()))
    return lax.dot_general(
        left, right, dims, precision=precision, preferred_element_type=F32
    )


def stage(body, outs, args, scalars=(), scratch=(), name=None):
    vmem = pl.BlockSpec(memory_space=pltpu.VMEM)
    smem = pl.BlockSpec(memory_space=pltpu.SMEM)
    shapes = [jax.ShapeDtypeStruct(shape, F32) for shape in outs]
    return pl.pallas_call(
        body,
        out_shape=shapes,
        in_specs=[smem] * len(scalars) + [vmem] * len(args),
        out_specs=[vmem] * len(shapes),
        scratch_shapes=list(scratch),
        compiler_params=pltpu.CompilerParams(vmem_limit_bytes=56 << 20),
        name=name,
    )(*scalars, *args)


def channel_sums(ref):
    return jnp.sum(ref[...], axis=0)


def spread_of(total, pixels):
    half = total.shape[1] // 2
    centre = total[:, :half] * (1.0 / pixels)
    second = total[:, half:] * (1.0 / pixels)
    return centre, lax.rsqrt(second - centre * centre + EPS_NORM)


def cols_between(count, lanes, first, past):
    col = lax.broadcasted_iota(jnp.int32, (count, lanes), 0)
    return (col >= first) & (col < past)


def row_total(value):
    return jnp.sum(value, axis=0, keepdims=True)


def send(ref, row):
    ref[...] = jnp.broadcast_to(row[None], ref.shape)


def pad_lateral(masked, up, down, left, right, lateral, grid, z_four, sums):
    height, breadth, channels = masked.shape
    grid[...] = jnp.zeros(grid.shape, F32)
    inner = slice(LEAD, LEAD + breadth)
    grid[0:RIM_UP, inner] = up[...]
    grid[RIM_UP : RIM_UP + height, inner] = masked[...]
    grid[RIM_UP + height :, inner] = down[...]
    grid[:, LEAD - RIM_LEFT : LEAD] = left[...]
    grid[:, LEAD + breadth : LEAD + breadth + RIM_RIGHT] = right[...]
    width = z_four.shape[1]
    own = cols_between(width, C1, 2, 2 + breadth)
    total = jnp.zeros((1, C1), F32)
    square = jnp.zeros((1, C1), F32)
    tile = 6
    for first in range(0, height + 2, tile):
        block = grid[2 + first : 2 + first + tile, LEAD - 2 : LEAD - 2 + width]
        made = product(block.reshape(tile * width, channels), lateral[...], 1, 0)
        made = made.reshape(tile, width, C1)
        z_four[first : first + tile] = made
        for row in range(tile):
            if 1 <= first + row <= height:
                kept = jnp.where(own, made[row], 0.0)
                total = total + row_total(kept)
                square = square + row_total(kept * kept)
    sums[...] = jnp.concatenate([total, square], axis=1)


def coarse_map(flags, grid, weight, sums_four, z_one, windows, sums):
    rows, width = z_one.shape[0], z_one.shape[1]
    half_breadth = width - 3
    for i in range(rows):
        for a in range(3):
            for b in range(3):
                piece = grid[2 * i + a, pl.ds(LEAD - 3 + b, width, 2), :]
                if a == 0:
                    piece = piece * flags[i]
                tap = 3 * a + b
                windows[i, :, tap * C0 : (tap + 1) * C0] = piece
    made = product(windows[...].reshape(rows * width, 9 * C0), weight[...], 1, 0)
    z_one[...] = made.reshape(rows, width, C1)
    own = cols_between(width, C1, 1, 1 + half_breadth)
    total = jnp.zeros((1, C1), F32)
    square = jnp.zeros((1, C1), F32)
    for i in range(1, rows - 1):
        kept = jnp.where(own, z_one[i], 0.0)
        total = total + row_total(kept)
        square = square + row_total(kept * kept)
    send(sums, jnp.concatenate([total, square, sums_four[...]], axis=1))


def window_halves(
    coarse_pixels, windows, grad_one, z_one, total_one, grads_one, gain_one, halves
):
    args = (windows, grad_one, z_one, total_one, grads_one, gain_one)
    made = multiply_windows(coarse_pixels, *args)
    halves[0] = made[:, : C1 // 2]
    halves[1] = made[:, C1 // 2 :]


def window_product(
    coarse_pixels, flags, slots, windows, grad_one, z_one, total_one, grads_one, gain_one, mine, other
):
    args = (windows, grad_one, z_one, total_one, grads_one, gain_one)
    made = multiply_windows(coarse_pixels, *args)
    shards = mine.shape[0] * mine.shape[1]
    by_slot(made, mine, other, slots, flags[30] == 0.0, shards, 0)


def multiply_windows(coarse_pixels, windows, grad_one, z_one, total_one, grads_one, gain_one):
    rows, width, depth = windows.shape
    centre, spread = spread_of(channel_sums(total_one)[:, : 2 * C1], coarse_pixels)
    gained = channel_sums(grads_one)
    scale = gain_one[...] * spread
    mean_gain = gained[:, :C1] * (1.0 / coarse_pixels)
    mean_shift = gained[:, C1:] * (1.0 / coarse_pixels)
    own = cols_between(width, C1, 1, width - 2)
    parts = []
    for i in range(1, rows - 1):
        normed = (z_one[i] - centre) * spread
        value = scale * (grad_one[i] - mean_shift - normed * mean_gain)
        parts.append(jnp.where(own, value, 0.0))
    inside = windows[1 : rows - 1].reshape((rows - 2) * width, depth)
    return product(inside, jnp.concatenate(parts, axis=0), 0, 0)


def upsample(pixels, z_one, total_one, gain, shift, weight, z_three, act_one, slope_one, sums):
    rows, width = z_one.shape[0], z_one.shape[1]
    half_breadth = width - 3
    centre, spread = spread_of(channel_sums(total_one)[:, : 2 * C1], pixels)
    for i in range(rows):
        hidden = (z_one[i] - centre) * spread * gain[...] + shift[...]
        sigmoid = lax.logistic(hidden)
        act_one[i] = hidden * sigmoid
        slope_one[i] = sigmoid * (1.0 + hidden * (1.0 - sigmoid))
    active = act_one[...].reshape(rows * width, C1)
    own = cols_between(width, C1, 1, 1 + half_breadth)
    total = jnp.zeros((1, C1), F32)
    square = jnp.zeros((1, C1), F32)
    half = C1 // 2
    for a in range(2):
        for b in range(2):
            tap = 2 * a + b
            made = product(active, weight[tap * C1 : (tap + 1) * C1], 1, 0)
            for i in range(rows):
                part = made[i * width : (i + 1) * width]
                place = 2 * i + a - 1
                if 0 <= place < 2 * rows - 2:
                    for k in range(2):
                        z_three[k, place, pl.ds(b, width, 2), :] = part[:, k * half : (k + 1) * half]
                if 1 <= i < rows - 1:
                    kept = jnp.where(own, part, 0.0)
                    total = total + row_total(kept)
                    square = square + row_total(kept * kept)
    send(sums, jnp.concatenate([total, square], axis=1))


def pack_merging(weight, packed):
    for a in range(3):
        pieces = [
            weight[(3 * a + b) * 2 * C1 : (3 * a + b + 1) * 2 * C1] for b in range(3)
        ]
        pieces.append(jnp.zeros((2 * C1, C2), F32))
        packed[:, a * 4 * C2 : (a + 1) * 4 * C2] = jnp.concatenate(pieces, axis=1)


def arrange(first, rows, place, pieces, swapped, out):
    near, far, _, lanes = pieces.shape
    front = place[near * far] == 0
    for low in range(near):
        for high in range(far):
            at = pl.ds(pl.multiple_of(place[low * far + high] * rows, 8), rows)
            mine = pieces[low, high, first : first + rows]
            other = swapped[low, high, first : first + rows]
            out[at, 0:lanes] = jnp.where(front, mine, other)
            out[at, lanes:] = jnp.where(front, other, mine)


def arrange_merging(first, place, pieces, swapped, packed, weight):
    near, far, last, _ = pieces.shape
    rows = last - first
    front = place[near * far] == 0
    for low in range(near):
        for high in range(far):
            mine, other = pieces[low, high, first:], swapped[low, high, first:]
            values = (jnp.where(front, mine, other), jnp.where(front, other, mine))
            for core in range(2):
                for side in range(2):
                    start = (place[low * far + high] * 4 + 2 * core + side) * rows
                    at = pl.ds(pl.multiple_of(start, 8), rows)
                    weight[at, :] = values[core][:, side * C2 : (side + 1) * C2]
    pack_merging(weight, packed)


def merge(
    pixels,
    flags,
    z_three,
    z_four,
    total_three,
    total_one,
    norms,
    packed,
    merged,
    joined,
    slopes,
    sums,
    taps,
):
    rows, width = z_four.shape[0], z_four.shape[1]
    height = rows - 2
    breadth = width - 6
    sum_three = channel_sums(total_three)
    sum_four = channel_sums(total_one)[:, 2 * C1 :]
    centre_three, spread_three = spread_of(sum_three, pixels)
    centre_four, spread_four = spread_of(sum_four, pixels)
    centre = jnp.concatenate([centre_three, centre_four], axis=1)
    spread = jnp.concatenate([spread_three, spread_four], axis=1)
    scale = spread * norms[0:1]
    offset = norms[1:2] - centre * scale
    col = lax.broadcasted_iota(jnp.int32, (width, 2 * C1), 0)
    dead = ((col == 1) & (flags[30] == 0.0)) | ((col == 2 + breadth) & (flags[31] == 0.0))

    def activate(r, carry):
        raw = jnp.concatenate([z_three[0, r], z_three[1, r], z_four[r]], axis=1)
        hidden = raw * scale + offset
        sigmoid = lax.logistic(hidden)
        joined[r] = jnp.where(dead, 0.0, hidden * sigmoid)
        slopes[r] = sigmoid * (1.0 + hidden * (1.0 - sigmoid))
        return carry

    lax.fori_loop(0, rows, activate, 0)
    tile = 6

    def spread_taps(t, carry):
        r = pl.multiple_of(t * tile, tile)
        block = joined[pl.ds(r, tile)].reshape(tile * width, 2 * C1)
        taps[pl.ds(r, tile)] = product(block, packed[...], 1, 0).reshape(tile, width, 12 * C2)
        return carry

    lax.fori_loop(0, rows // tile, spread_taps, 0)
    own = cols_between(width, 2 * C2, 2, 2 + breadth)
    lane = lax.broadcasted_iota(jnp.int32, (width, 2 * C2), 1)
    total = jnp.zeros((1, 2 * C2), F32)
    square = jnp.zeros((1, 2 * C2), F32)
    for row in range(height):
        r = row + 1
        both = (
            taps[r - 1, :, 0 : 4 * C2] * flags[10 + r]
            + taps[r, :, 4 * C2 : 8 * C2]
            + taps[r + 1, :, 8 * C2 : 12 * C2] * flags[11 + r]
        )
        first, second = both[:, : 2 * C2], both[:, 2 * C2 :]
        out = (
            pltpu.roll(first, 1, 0)
            + pltpu.roll(first, C2, 1)
            + pltpu.roll(second, width - 1, 0)
        )
        out = jnp.where(own & (lane < C2), out, 0.0)
        merged[row] = out
        total = total + row_total(out)
        square = square + row_total(out * out)
    send(sums, jnp.concatenate([total, square], axis=1))


def heads(
    pixels,
    merged,
    total_five,
    norms,
    weight,
    bias,
    cotangent,
    maps,
    pairs,
    weight_grad,
    sums,
    active,
    upstream,
):
    height, width, _ = merged.shape
    breadth = width - 6
    centre, spread = spread_of(channel_sums(total_five)[:, : 4 * C2], pixels)
    own = cols_between(width, 2 * C2, 2, 2 + breadth)
    upstream[...] = jnp.zeros(upstream.shape, F32)
    for r in range(height):
        upstream[r, 2 : 2 + breadth, 0:CH] = cotangent[r]
    flat = upstream[...].reshape(height * width, 2 * C2)
    grad = product(flat, weight[...], 1, 1).reshape(height, width, 2 * C2)
    grad_gain = jnp.zeros((1, 2 * C2), F32)
    grad_shift = jnp.zeros((1, 2 * C2), F32)
    for r in range(height):
        normed = jnp.where(own, (merged[r] - centre) * spread, 0.0)
        hidden = norms[0:1] * normed + norms[1:2]
        sigmoid = lax.logistic(hidden)
        active[r] = hidden * sigmoid
        grad_hidden = grad[r] * sigmoid * (1.0 + hidden * (1.0 - sigmoid))
        pairs[r] = grad_hidden + pltpu.roll(normed, C2, 1)
        grad_gain = grad_gain + row_total(grad_hidden * normed)
        grad_shift = grad_shift + row_total(grad_hidden)
    send(sums, jnp.concatenate([grad_gain, grad_shift, row_total(flat)], axis=1))
    act = active[...].reshape(height * width, 2 * C2)
    made = product(act, weight[...], 1, 0).reshape(height, width, 2 * C2) + bias[...]
    for r in range(height):
        maps[r] = made[r, 2 : 2 + breadth, 0:CH]
    weight_grad[...] = product(act, flat, 0, 0)


def merged_gradient(
    pixels,
    flags,
    pairs,
    above,
    below,
    left,
    right,
    total_five,
    grads_five,
    norm_five,
    packed,
    z_three,
    z_four,
    slopes,
    total_three,
    total_one,
    grad_joined,
    columns,
    sums,
):
    height, width, _ = pairs.shape
    breadth = width - 6
    lanes = 2 * C2
    _, spread = spread_of(channel_sums(total_five)[:, : 4 * C2], pixels)
    gained = channel_sums(grads_five)
    scale = norm_five[0:1] * spread
    mean_gain = gained[:, :lanes] * (1.0 / pixels)
    mean_shift = gained[:, lanes : 2 * lanes] * (1.0 / pixels)
    col = lax.broadcasted_iota(jnp.int32, (width, lanes), 0)
    lane = lax.broadcasted_iota(jnp.int32, (width, lanes), 1)
    live = (
        ((col >= 2) & (col < 2 + breadth))
        | ((col == 1) & (flags[30] != 0.0))
        | ((col == 2 + breadth) & (flags[31] != 0.0))
    ) & (lane < C2)
    for r in range(height + 2):
        if r == 0:
            raw = above[0]
        elif r == height + 1:
            raw = below[0]
        else:
            raw = pairs[r - 1]
        raw = jnp.where(col == 1, left[r], jnp.where(col == 2 + breadth, right[r], raw))
        normed = pltpu.roll(raw, C2, 1)
        value = jnp.where(live, scale * (raw - mean_shift - normed * mean_gain), 0.0)
        columns[r, :, 0:lanes] = pltpu.roll(value, width - 1, 0) + pltpu.roll(value, C2, 1)
        columns[r, :, lanes:] = pltpu.roll(value, 1, 0)
    centre_three, spread_three = spread_of(channel_sums(total_three), pixels)
    centre_four, spread_four = spread_of(channel_sums(total_one)[:, 2 * C1 :], pixels)
    centre = jnp.concatenate([centre_three, centre_four], axis=1)
    spread = jnp.concatenate([spread_three, spread_four], axis=1)
    own = cols_between(width, 2 * C1, 2, 2 + breadth)
    tile = 4

    def gradient(t, carry):
        r = t * tile
        block = jnp.zeros((tile * width, 2 * C1), F32)
        for a in range(3):
            rows = []
            for k in range(tile):
                source = r + k + 2 - a
                row = columns[source]
                if a == 0:
                    row = row * flags[10 + source]
                if a == 2:
                    row = row * flags[11 + source]
                rows.append(row)
            block = block + product(
                jnp.concatenate(rows, axis=0), packed[:, a * 4 * C2 : (a + 1) * 4 * C2], 1, 1
            )
        gain_sum, shift_sum = carry
        for k in range(tile):
            grad = jnp.where(own, block[k * width : (k + 1) * width] * slopes[r + k + 1], 0.0)
            grad_joined[r + k] = grad
            raw = jnp.concatenate(
                [z_three[0, r + k + 1], z_three[1, r + k + 1], z_four[r + k + 1]], axis=1
            )
            normed = (raw - centre) * spread
            gain_sum = gain_sum + row_total(grad * normed)
            shift_sum = shift_sum + row_total(grad)
        return gain_sum, shift_sum

    empty = jnp.zeros((1, 2 * C1), F32)
    gain_sum, shift_sum = lax.fori_loop(0, height // tile, gradient, (empty, empty))
    send(sums, jnp.concatenate([gain_sum, shift_sum], axis=1))


def by_slot(value, mine, other, slots, front, shards, first):
    rows = value.shape[0] // shards
    half = value.shape[1] // 2
    for shard in range(shards):
        piece = value[shard * rows : (shard + 1) * rows]
        low, high = piece[:, :half], piece[:, half:]
        place = slots[shard % NEAR], shard // NEAR, slice(first, first + rows)
        mine[place] = jnp.where(front, low, high)
        other[place] = jnp.where(front, high, low)


def merging_product(flags, slots, joined, columns, mine, other, grads, shifted_rows):
    multiply_merging(flags, joined, columns, grads, shifted_rows)
    front = flags[30] == 0.0
    near, far, rows, _ = mine.shape
    for shard in range(near * far):
        start = 4 * rows * shard
        runs = [grads[start + i * rows : start + (i + 1) * rows] for i in range(4)]
        first = jnp.concatenate(runs[:2], axis=1)
        second = jnp.concatenate(runs[2:], axis=1)
        place = slots[shard % near], shard // near
        mine[place] = jnp.where(front, first, second)
        other[place] = jnp.where(front, second, first)


def multiply_merging(flags, joined, columns, grads, shifted_rows):
    rows, width, _ = joined.shape
    height = rows - 2
    inside = joined[1 : rows - 1].reshape(height * width, 2 * C1)
    own = cols_between(width, 4 * C2, 2, width - 4)
    for a in range(3):
        for r in range(height):
            source = r + 2 - a
            row = columns[source]
            if a == 0:
                row = row * flags[10 + source]
            if a == 2:
                row = row * flags[11 + source]
            shifted_rows[r] = jnp.where(own, row, 0.0)
        made = product(inside, shifted_rows[...].reshape(height * width, 4 * C2), 0, 0)
        for b in range(3):
            grads[(3 * a + b) * 2 * C1 : (3 * a + b + 1) * 2 * C1] = made[:, b * C2 : (b + 1) * C2]


def coarse_gradient(
    pixels,
    coarse_pixels,
    grad_joined,
    z_three,
    total_three,
    grads_joined,
    gain_three,
    weight,
    z_one,
    total_one,
    slope_one,
    quads,
    grad_one,
    sums,
    fine,
):
    height, width = grad_joined.shape[0], grad_joined.shape[1]
    rows, half_width = z_one.shape[0], z_one.shape[1]
    half = C1 // 2
    centre, spread = spread_of(channel_sums(total_three), pixels)
    gained = channel_sums(grads_joined)
    scale = gain_three[...] * spread
    mean_gain = gained[:, :C1] * (1.0 / pixels)
    mean_shift = gained[:, 2 * C1 : 3 * C1] * (1.0 / pixels)
    own = cols_between(width, C1, 2, width - 4)

    def fill(r, carry):
        raw = jnp.concatenate([z_three[0, r + 1], z_three[1, r + 1]], axis=1)
        normed = (raw - centre) * spread
        value = scale * (grad_joined[r, :, 0:C1] - mean_shift - normed * mean_gain)
        value = jnp.where(own, value, 0.0)
        fine[0, r] = value[:, :half]
        fine[1, r] = value[:, half:]
        return carry

    lax.fori_loop(0, height, fill, 0)
    grad = jnp.zeros(((rows - 2) * half_width, C1), F32)
    for a in range(2):
        for b in range(2):
            tap = 2 * a + b
            for i in range(rows - 2):
                for k in range(2):
                    quads[tap, i, :, k * half : (k + 1) * half] = fine[
                        k, 2 * i + a, pl.ds(b, half_width, 2), :
                    ]
            flat = quads[tap].reshape((rows - 2) * half_width, C1)
            grad = grad + product(flat, weight[tap * C1 : (tap + 1) * C1], 1, 1)
    centre, spread = spread_of(channel_sums(total_one)[:, : 2 * C1], coarse_pixels)
    own = cols_between(half_width, C1, 1, half_width - 2)
    gain_sum = jnp.zeros((1, C1), F32)
    shift_sum = jnp.zeros((1, C1), F32)
    grad_one[0] = jnp.zeros((half_width, C1), F32)
    grad_one[rows - 1] = jnp.zeros((half_width, C1), F32)
    for i in range(1, rows - 1):
        value = grad[(i - 1) * half_width : i * half_width] * slope_one[i]
        value = jnp.where(own, value, 0.0)
        grad_one[i] = value
        gain_sum = gain_sum + row_total(value * ((z_one[i] - centre) * spread))
        shift_sum = shift_sum + row_total(value)
    send(sums, jnp.concatenate([gain_sum, shift_sum], axis=1))


def lateral_gradient(pixels, grad_joined, z_four, total_one, grads_joined, gain_four, fine):
    height, width = grad_joined.shape[0], grad_joined.shape[1]
    centre, spread = spread_of(channel_sums(total_one)[:, 2 * C1 :], pixels)
    gained = channel_sums(grads_joined)
    scale = gain_four[...] * spread
    mean_gain = gained[:, C1 : 2 * C1] * (1.0 / pixels)
    mean_shift = gained[:, 3 * C1 :] * (1.0 / pixels)
    own = cols_between(width, C1, 2, width - 4)

    def fill(r, carry):
        normed = (z_four[r + 1] - centre) * spread
        value = scale * (grad_joined[r, :, C1:] - mean_shift - normed * mean_gain)
        fine[r] = jnp.where(own, value, 0.0)
        return carry

    lax.fori_loop(0, height, fill, 0)


def fine_halves(
    pixels,
    grad_joined,
    z_four,
    total_one,
    grads_joined,
    gain_four,
    grid,
    act_one,
    quads,
    upward_halves,
    lateral_halves,
    fine,
):
    height, width = grad_joined.shape[0], grad_joined.shape[1]
    rows, half_width = act_one.shape[0], act_one.shape[1]
    half = C1 // 2
    lateral_gradient(pixels, grad_joined, z_four, total_one, grads_joined, gain_four, fine)
    flat = fine[...].reshape(height * width, C1)
    source = grid[RIM_UP : RIM_UP + height, LEAD - 2 : LEAD - 2 + width]
    made = product(source.reshape(height * width, C0), flat, 0, 0)
    lateral_halves[0] = made[:, :half]
    lateral_halves[1] = made[:, half:]
    inside = act_one[1 : rows - 1].reshape((rows - 2) * half_width, C1)
    for tap in range(4):
        made = product(inside, quads[tap].reshape((rows - 2) * half_width, C1), 0, 0)
        for side in range(2):
            upward_halves[side, tap * C1 : (tap + 1) * C1] = made[
                :, side * half : (side + 1) * half
            ]


def fine_products(
    pixels,
    flags,
    slots,
    grad_joined,
    z_four,
    total_one,
    grads_joined,
    gain_four,
    grid,
    act_one,
    quads,
    heads_grad,
    mine,
    other,
    fine,
):
    height, width = grad_joined.shape[0], grad_joined.shape[1]
    rows, half_width = act_one.shape[0], act_one.shape[1]
    shards = mine.shape[0] * mine.shape[1]
    front = flags[30] == 0.0
    lateral_gradient(pixels, grad_joined, z_four, total_one, grads_joined, gain_four, fine)
    inside = act_one[1 : rows - 1].reshape((rows - 2) * half_width, C1)
    parts = [
        product(inside, quads[tap].reshape((rows - 2) * half_width, C1), 0, 0)
        for tap in range(4)
    ]
    by_slot(jnp.concatenate(parts, axis=0), mine, other, slots, front, shards, 0)
    flat = fine[...].reshape(height * width, C1)
    source = grid[RIM_UP : RIM_UP + height, LEAD - 2 : LEAD - 2 + width]
    made = product(source.reshape(height * width, C0), flat, 0, 0)
    first = 4 * C1 // shards
    by_slot(made, mine, other, slots, front, shards, first)
    first += C0 // shards
    both = jnp.concatenate([heads_grad[0 : C2 // 2], heads_grad[C2 // 2 : C2]], axis=1)
    by_slot(both, mine, other, slots, front, shards, first)


def input_gradient(
    pixels,
    coarse_pixels,
    flags,
    grad_one,
    below,
    right,
    z_one,
    total_one,
    grads_one,
    gain_one,
    weight,
    grad_joined,
    z_four,
    grads_joined,
    gain_four,
    lateral,
    occupancy,
    out,
    taps,
    fine,
    wide_fine,
):
    lateral_gradient(
        pixels, grad_joined, z_four, total_one, grads_joined, gain_four, wide_fine
    )
    flat = wide_fine[...].reshape(-1, C1)
    grad_masked = product(flat, lateral[...], 1, 1).reshape(fine.shape)
    rows, half_width = z_one.shape[0], z_one.shape[1]
    height, breadth = out.shape[0], out.shape[1]
    centre, spread = spread_of(channel_sums(total_one)[:, : 2 * C1], coarse_pixels)
    gained = channel_sums(grads_one)
    scale = gain_one[...] * spread
    mean_gain = gained[:, :C1] * (1.0 / coarse_pixels)
    mean_shift = gained[:, C1:] * (1.0 / coarse_pixels)
    col = lax.broadcasted_iota(jnp.int32, (half_width, C1), 0)
    edge = half_width - 2
    live = ((col >= 1) & (col < edge)) | ((col == edge) & (flags[31] != 0.0))
    parts = []
    for i in range(1, rows):
        raw = grad_one[i] if i < rows - 1 else below[0]
        raw = jnp.where(col == edge, right[i - 1], raw)
        normed = (z_one[i] - centre) * spread
        value = scale * (raw - mean_shift - normed * mean_gain)
        parts.append(jnp.where(live, value, 0.0))
    made = product(jnp.concatenate(parts, axis=0), weight[...], 1, 1)
    taps[...] = made.reshape(rows - 1, half_width, 9 * C0)

    def tap(a, b, i):
        value = taps[i, :, (3 * a + b) * C0 : (3 * a + b + 1) * C0]
        if b == 0:
            value = pltpu.roll(value, half_width - 1, 0)
        if a == 0:
            value = value * flags[i + 1]
        return value

    for i in range(rows - 2):
        fine[2 * i, pl.ds(0, half_width, 2), :] = tap(1, 1, i)
        fine[2 * i, pl.ds(1, half_width, 2), :] = tap(1, 2, i) + tap(1, 0, i)
        fine[2 * i + 1, pl.ds(0, half_width, 2), :] = tap(2, 1, i) + tap(0, 1, i + 1)
        fine[2 * i + 1, pl.ds(1, half_width, 2), :] = (
            tap(2, 2, i) + tap(2, 0, i) + tap(0, 2, i + 1) + tap(0, 0, i + 1)
        )
    for r in range(height):
        total = fine[r] + grad_masked[r]
        out[r] = total[2 : 2 + breadth] * occupancy[r]


def dot(a,b,ca,cb):
    return lax.dot_general(a,b,(((ca,),(cb,)),((),())),precision=HIGHEST,preferred_element_type=F32)
NB=64
W=8
def base_inverse(blocks):
    lane=lax.broadcasted_iota(jnp.int32,(8,128),1); row=lax.broadcasted_iota(jnp.int32,(8,128),0)
    T=NB//8
    xs=[]
    for b in blocks:
        tiles=[]
        for t in range(T):
            pad=jnp.zeros((8,128-NB),F32)
            tiles.append(jnp.concatenate([b[8*t:8*t+8],pad],axis=1)+(lane==row+(NB+8*t)).astype(F32))
        xs.append(tiles)
    for g in range(0,NB,W):
        own=g//8
        cols=[[{t:jnp.broadcast_to(x[t][:,g+j:g+j+1],(8,128)) for t in range(own,T)} for j in range(W)] for x in xs]
        for j in range(W):
            k=(g+j)%8
            for m in range(len(xs)):
                c=cols[m][j]
                inv=1.0/c[own][k:k+1,:]
                rest=[(xs[m],xs[m][own][k:k+1,:])]+[(cols[m][u],cols[m][u][own][k:k+1,:]) for u in range(j+1,W)]
                for t in range(own,T):
                    f=(jnp.where(row>k,c[t],0.0) if t==own else c[t])*inv
                    for target,pivot_row in rest:
                        target[t]=target[t]-f*pivot_row
    outs=[]
    for x in xs:
        done=[]
        for t in range(T):
            d=jnp.sum(jnp.where(lane==row+8*t,x[t],0.0),axis=1,keepdims=True)
            done.append((x[t]*lax.rsqrt(d))[:,NB:2*NB])
        outs.append(jnp.concatenate(done,axis=0))
    return outs
def kern(ns,*refs):
    m=len(ns)
    gram=refs[0:m]; add=refs[m:2*m]; basis=refs[2*m:3*m]
    out_gram=refs[3*m:4*m]; out_rot=refs[4*m:5*m]
    aa=refs[5*m:6*m]; xx=refs[6*m:7*m]
    prods=[]
    for i,n in enumerate(ns):
        g=0.95*gram[i][...]+0.05*add[i][...]
        out_gram[i][...]=g
        p=dot(g,basis[i][...],1,0)
        out_rot[i][...]=p
        a=dot(p,p,0,0)
        npad=aa[i].shape[0]
        if npad!=n:
            r=lax.broadcasted_iota(jnp.int32,(npad,npad),0); c=lax.broadcasted_iota(jnp.int32,(npad,npad),1)
            aa[i][...]=((r==c)&(r>=n)).astype(F32)
            aa[i][0:n,0:n]=a
        else:
            aa[i][...]=a
        r=lax.broadcasted_iota(jnp.int32,(npad,npad),0); c=lax.broadcasted_iota(jnp.int32,(npad,npad),1)
        xx[i][...]=(r==c).astype(F32)
    for b in range(max(a.shape[0] for a in aa)//NB):
        s=b*NB
        live=[i for i in range(m) if s<aa[i].shape[0]]
        inv=base_inverse([aa[i][s:s+NB,s:s+NB] for i in live])
        for i,li in zip(live,inv):
            npad=aa[i].shape[0]
            e=s+NB
            y=dot(li,xx[i][s:e,:],1,0)
            xx[i][s:e,:]=y
            if e<npad:
                rpan=dot(li,aa[i][s:e,e:],1,0)
                cpan=dot(aa[i][e:,s:e],li,1,1)
                aa[i][e:,e:]=aa[i][e:,e:]-dot(cpan,rpan,1,0)
                xx[i][e:,:]=xx[i][e:,:]-dot(cpan,y,1,0)
    for i,n in enumerate(ns):
        out_rot[i][...]=dot(out_rot[i][...],xx[i][0:n,0:n],1,1)


def keep_rows(global_rows, total_rows):
    wrapped = jnp.remainder(global_rows, total_rows)
    return ((wrapped + SCENE_ROWS // 2) % SCENE_ROWS != 0).astype(jnp.float32)


def from_behind(block, axis, distance):
    devices = range(lax.axis_size(axis))
    route = [(i - distance, i) for i in devices if i - distance in devices]
    return lax.ppermute(block, axis, route)


def shifted(value, axis, steps):
    count = lax.axis_size(axis)
    pairs = [(source, (source + steps) % count) for source in range(count)]
    return lax.ppermute(value, axis, pairs)


def after(value, *others):
    return lax.optimization_barrier((value,) + others)[0]


def exchange(value):
    return lax.ppermute(value, "stream", [(0, 1), (1, 0)])


def to_all(rows):
    return lax.all_to_all(rows, ("dp", "stream"), 0, 0, tiled=True)


def everyone(value):
    count = lax.axis_size("dp")
    copies = jnp.broadcast_to(value[None], (count,) + value.shape)
    return lax.all_to_all(copies, "dp", 0, 0, tiled=True)


def far_groups():
    far = lax.axis_size("dp") // NEAR
    return [[low + NEAR * high for high in range(far)] for low in range(NEAR)]


def across(value, low):
    count = lax.axis_size("dp")
    return lax.ppermute(value, "dp", [(i, i ^ low) for i in range(count)])


def gather_pieces(value, *first):
    count = lax.axis_size("dp")
    far = count // NEAR
    if far <= NEAR:
        held = [value] + [shifted(value, "dp", NEAR * step) for step in range(1, far)]
        column = jnp.stack(held)
    else:
        copies = jnp.broadcast_to(value[None], (far,) + value.shape)
        column = lax.all_to_all(
            copies, "dp", 0, 0, axis_index_groups=far_groups(), tiled=True
        )
    column = after(column, *first)
    return jnp.stack([column] + [across(column, low) for low in range(1, NEAR)])


def by_low(value):
    low = lax.axis_index("dp") % NEAR
    pairs = value.reshape((2, 2) + value.shape[1:])
    pairs = jnp.where(low % 2 == 1, lax.rev(pairs, (1,)), pairs)
    pairs = jnp.where(low // 2 == 1, lax.rev(pairs, (0,)), pairs)
    return pairs.reshape(value.shape)


def by_index(pieces):
    far = pieces.shape[1]
    pieces = by_low(pieces)
    if far <= NEAR:
        back = lax.rev(pieces, (1,))
        start = (-1 - lax.axis_index("dp") // NEAR) % far
        pieces = lax.dynamic_slice_in_dim(jnp.concatenate([back, back], axis=1), start, far, 1)
    return jnp.swapaxes(pieces, 0, 1).reshape((NEAR * far,) + pieces.shape[2:])


def gather_order():
    count = lax.axis_size("dp")
    far = count // NEAR
    index = lax.axis_index("dp")
    low = (index % NEAR) ^ jnp.arange(NEAR)
    high = (index // NEAR - jnp.arange(far)) % far if far <= NEAR else jnp.arange(far)
    return (high[None, :] * NEAR + low[:, None]).reshape(-1).astype(jnp.int32)


def chip_sums(mine, other):
    return [mine[step] + other[step] for step in range(NEAR)]


def near_sum(sums):
    total = sums[0]
    for step in range(1, NEAR):
        total = total + across(sums[step], step)
    return total


def slotted(pair):
    core = lax.axis_index("stream")
    shape = (lax.axis_size("dp") // NEAR, NEAR) + pair.shape[2:]
    parts = (pick(pair, 0, which).reshape(shape) for which in (core, 1 - core))
    return [by_low(jnp.swapaxes(part, 0, 1)) for part in parts]


def far_sum(column):
    moved = lax.all_to_all(column, "dp", 0, 0, axis_index_groups=far_groups(), tiled=True)
    return moved


def in_order(mine, other):
    first = lax.axis_index("stream") == 0
    return jnp.where(first, mine, other), jnp.where(first, other, mine)


def pick(pair, axis, which):
    return lax.dynamic_index_in_dim(pair, which, axis, keepdims=False)


def by_shard(halves):
    count = lax.axis_size("dp")
    short = -halves.shape[1] % count
    if short:
        halves = jnp.pad(halves, ((0, 0), (0, short), (0, 0)))
    return halves.reshape(2, count, halves.shape[1] // count, halves.shape[2])


def fold_rows(rows, count):
    parts = rows.reshape(count, 2, 2, rows.shape[0] // (4 * count), C2)
    return jnp.swapaxes(jnp.concatenate([parts[:, :, 0], parts[:, :, 1]], axis=-1), 0, 1)


def unfold_rows(first, second):
    both = jnp.stack([first, second], axis=1)
    parts = jnp.stack([both[..., :C2], both[..., C2:]], axis=2)
    return parts.reshape(-1, C2)


def arranged(place, pieces, swapped, first=0, past=None):
    past = pieces.shape[2] if past is None else past
    count, rows = pieces.shape[0] * pieces.shape[1], past - first
    if rows % 8 == 0:
        body = functools.partial(arrange, first, rows)
        outs = [(count * rows, 2 * pieces.shape[3])]
        return stage(body, outs, [pieces, swapped], scalars=[place], name="arrange")[0]
    both = in_order(pieces[:, :, first:past], swapped[:, :, first:past])
    both = [by_index(part) for part in both]
    return jnp.concatenate([part.reshape(count * rows, -1) for part in both], axis=1)


def packed_merging(place, pieces, swapped, first, moment):
    count, rows = pieces.shape[0] * pieces.shape[1], pieces.shape[2] - first
    if rows % 8 == 0:
        return stage(
            functools.partial(arrange_merging, first),
            [(2 * C1, 12 * C2)],
            [after(pieces, moment), swapped],
            scalars=[place],
            scratch=[pltpu.VMEM((18 * C1, C2), F32)],
            name="pack",
        )[0]
    both = in_order(pieces[:, :, first:], swapped[:, :, first:])
    both = [by_index(part) for part in both]
    return stage(pack_merging, [(2 * C1, 12 * C2)], [unfold_rows(*both)], name="pack")[0]


def lanes_of(row, width):
    return jnp.pad(row, (0, width - row.shape[0]))[None]


def adam_vector(params, moment, square, gradient):
    momentum = BETA_ONE * moment + (1.0 - BETA_ONE) * gradient
    variance = BETA_TWO * square + (1.0 - BETA_TWO) * gradient * gradient
    direction = (
        momentum / (1.0 - BETA_ONE**STEP) / (jnp.sqrt(variance / (1.0 - BETA_TWO**STEP)) + EPS_ADAM)
    )
    return (params - VECTOR_RATE * (direction + DECAY * params), momentum, variance)


def soap_one(rate, flipped, weight, moment, square, basis, gradient, outs):
    if flipped:
        rotated = product(basis, gradient, 0, 1, HIGHEST)
    else:
        rotated = product(gradient, basis, 1, 0, HIGHEST)
    momentum = BETA_ONE * moment[...] + (1.0 - BETA_ONE) * rotated
    variance = BETA_TWO * square[...] + (1.0 - BETA_TWO) * rotated * rotated
    direction = momentum * (1.0 / (1.0 - BETA_ONE**STEP)) / (
        jnp.sqrt(variance * (1.0 / (1.0 - BETA_TWO**STEP))) + EPS_ADAM
    )
    if flipped:
        turned = product(basis, direction, 1, 0, HIGHEST)
    else:
        turned = product(direction, basis, 1, 1, HIGHEST)
    old = weight[...]
    outs[0][...] = old - rate * (turned + DECAY * old)
    outs[1][...] = momentum
    outs[2][...] = variance


def soap_shards(rates, *refs):
    count = len(rates)
    for i, (rate, flipped) in enumerate(rates):
        group = refs[5 * i : 5 * i + 3]
        outs = refs[5 * count + 3 * i : 5 * count + 3 * i + 3]
        basis, gradient = refs[5 * i + 3][...], refs[5 * i + 4][...]
        soap_one(rate, flipped, *group, basis, gradient, outs)


def close(rates, *refs):
    grams, bases, adds = refs[0:5], refs[5:10], refs[10:15]
    lateral, head = refs[15:18], refs[18:21]
    outs, lateral_outs, head_outs = refs[21:31], refs[31:34], refs[34:37]
    lateral_gram, head_gram = refs[37:39]
    total_lateral, total_heads = adds[2][...], adds[4][...]
    lateral_gram[...] = product(total_lateral, total_lateral, 0, 0, HIGHEST)
    head_gram[...] = product(total_heads, total_heads, 0, 0, HIGHEST)
    sums = (adds[0], adds[1], lateral_gram, adds[3], head_gram)
    kern([C1, C1, C1, C2, CH], *grams, *sums, *bases, *outs, *refs[39:])
    soap_one(rates[0], False, *lateral, bases[2][...], total_lateral, lateral_outs)
    soap_one(rates[1], False, *head, bases[4][...], total_heads, head_outs)


def close_parts(rates, cuts, flags, mine, other, *refs):
    shards = mine.shape[0]
    front = flags[30] == 0.0
    down, upward, lateral, merging, head = adds = refs[-5:]
    half = C1 // 2
    count = C1 // shards
    small = cuts[0] - 2 * count
    for d in range(shards):
        first = jnp.where(front, mine[d], other[d])
        second = jnp.where(front, other[d], mine[d])
        for side in range(2):
            rows, lanes = slice(side * count, (side + 1) * count), slice(side * half, (side + 1) * half)
            down[d * count : (d + 1) * count, lanes] = first[rows]
            upward[d * count : (d + 1) * count, lanes] = second[rows]
        merging[d * small : (d + 1) * small] = second[2 * count : cuts[0], 0:C2]
        rows = cuts[1] - cuts[0]
        lateral[d * rows : (d + 1) * rows, 0:half] = first[cuts[0] : cuts[1]]
        lateral[d * rows : (d + 1) * rows, half:] = second[cuts[0] : cuts[1]]
        rows = cuts[2] - cuts[1]
        head[d * rows : (d + 1) * rows] = first[cuts[1] : cuts[2], 0:CH]
        start = C2 // 2 + d * rows
        head[start : start + rows] = second[cuts[1] : cuts[2], 0:CH]
    close(rates, *refs[:10], *adds, *refs[10:-5])


def assembled(final, other, gram_rows, small):
    final_first, final_second = in_order(final, other)
    shards, half, wide = final.shape[0], C1 // 2, 2 * C2

    def square_of(value):
        count = C1 // shards
        return jnp.concatenate(
            [value[:, k * count : (k + 1) * count].reshape(C1, half) for k in range(2)], axis=1
        )

    gram_down = square_of(final_first)
    gram_upward = square_of(final_second)
    gram_merging = final_second[:, 2 * (C1 // shards) : gram_rows].reshape(-1, wide)[:C2, :C2]
    total_lateral = jnp.concatenate(
        [v[:, gram_rows : gram_rows + small].reshape(C0, half) for v in (final_first, final_second)],
        axis=1,
    )
    total_heads = jnp.concatenate(
        [
            v[:, gram_rows + small :].reshape(-1, wide)[: C2 // 2]
            for v in (final_first, final_second)
        ],
        axis=0,
    )[:, :CH]
    return gram_down, gram_upward, total_lateral, gram_merging, total_heads


def local(
    feats,
    occupied,
    cotangent,
    vector_params,
    vector_moment,
    vector_square,
    down_weight,
    down_moment,
    down_square,
    down_gram,
    down_basis,
    upward_weight,
    upward_moment,
    upward_square,
    upward_gram,
    upward_basis,
    lateral_weight,
    lateral_moment,
    lateral_square,
    lateral_gram,
    lateral_basis,
    merging_weight,
    merging_moment,
    merging_square,
    merging_gram,
    merging_basis,
    heads_weight,
    heads_moment,
    heads_square,
    heads_gram,
    heads_basis,
):
    height, breadth, _ = feats.shape
    half_height, half_breadth = height // 2, breadth // 2
    shards = lax.axis_size("dp")
    cores = lax.axis_size("stream")
    everybody = shards * cores
    total_rows = height * shards
    fine_count = float(height * breadth * everybody)
    coarse_count = fine_count / 4.0
    shard_index, core = lax.axis_index("dp"), lax.axis_index("stream")
    first_row = shard_index * height
    width, half_width = breadth + 6, half_breadth + 3
    rows, half_rows = height + 2, half_height + 2
    flags = jnp.concatenate(
        [
            keep_rows(first_row + 2 * jnp.arange(-1, half_height + 1), total_rows),
            keep_rows(first_row + jnp.arange(-1, height + 3), total_rows),
            (core != 0).astype(F32)[None],
            (core != cores - 1).astype(F32)[None],
        ]
    )
    gains = [vector_params[i * C1 : (i + 1) * C1] for i in range(6)]
    late = 6 * C1
    gain_five, shift_five = vector_params[late : late + C2], vector_params[late + C2 : late + 2 * C2]
    head_bias = vector_params[late + 2 * C2 :]
    wide = 2 * C2
    norm_fine = jnp.stack(
        [jnp.concatenate([gains[2], gains[4]]), jnp.concatenate([gains[3], gains[5]])]
    )
    norm_five = jnp.concatenate([lanes_of(gain_five, wide), lanes_of(shift_five, wide)])

    half = C1 // 2
    weight_halves = [
        pick(w.reshape(-1, 2, half), 1, core) for w in (down_weight, upward_weight)
    ]
    weight_halves.append(pick(fold_rows(merging_weight, 1)[:, 0], 0, core))
    place = jnp.concatenate([gather_order(), core[None].astype(jnp.int32)])
    occupancy = occupied.astype(F32)[..., None]
    masked = feats * occupancy
    shown = jnp.broadcast_to(occupancy, feats.shape)
    up = shifted(masked[height - RIM_UP :], "dp", 1)
    down = shifted(masked[:RIM_DOWN], "dp", -1)
    edges = jnp.concatenate([up, masked, down], axis=0)
    gathered = gather_pieces(jnp.concatenate(weight_halves, axis=0), up, down)
    left = from_behind(edges[:, breadth - RIM_LEFT :], "stream", 1)
    right = from_behind(edges[:, :RIM_RIGHT], "stream", -1)
    grid, z_four, sums_four = stage(
        pad_lateral,
        [
            (height + RIM_UP + RIM_DOWN, width + LEAD - 2, C0),
            (rows, width, C1),
            (1, 2 * C1),
        ],
        [masked, up, down, left, right, lateral_weight],
        name="pad_lateral",
    )

    swapped = exchange(after(gathered, grid))
    bounds = [0]
    for part in weight_halves:
        bounds.append(bounds[-1] + part.shape[0])
    down_full = arranged(place, gathered, swapped, 0, bounds[1])
    z_one, windows, sums_one = stage(
        coarse_map,
        [
            (half_rows, half_width, C1),
            (half_rows, half_width, 9 * C0),
            (everybody, 1, 4 * C1),
        ],
        [grid, down_full, sums_four],
        scalars=[flags],
        name="coarse",
    )
    upward_full = arranged(place, after(gathered, z_one), swapped, bounds[1], bounds[2])
    total_one = after(to_all(sums_one), upward_full)

    z_three, act_one, slope_one, sums_three = stage(
        functools.partial(upsample, coarse_count),
        [
            (2, rows, width, C1 // 2),
            (half_rows, half_width, C1),
            (half_rows, half_width, C1),
            (everybody, 1, 2 * C1),
        ],
        [z_one, total_one, gains[0][None], gains[1][None], upward_full],
        name="upsample",
    )
    packed = packed_merging(place, gathered, swapped, bounds[2], sums_three)
    total_three = after(to_all(sums_three), packed)

    merged, joined, slopes, sums_five = stage(
        functools.partial(merge, fine_count),
        [
            (height, width, wide),
            (rows, width, 2 * C1),
            (rows, width, 2 * C1),
            (everybody, 1, 2 * wide),
        ],
        [z_three, z_four, total_three, total_one, norm_fine, packed],
        scalars=[flags],
        scratch=[pltpu.VMEM((rows, width, 12 * C2), F32)],
        name="merge",
    )
    total_five = to_all(sums_five)

    heads_padded = jnp.pad(heads_weight, ((0, wide - C2), (0, wide - CH)))
    head_maps, pairs, heads_grad, grad_sums_five = stage(
        functools.partial(heads, fine_count),
        [
            (height, breadth, CH),
            (height, width, wide),
            (wide, wide),
            (everybody, 1, 3 * wide),
        ],
        [merged, total_five, norm_five, heads_padded, lanes_of(head_bias, wide), cotangent],
        scratch=[pltpu.VMEM((height, width, wide), F32)] * 2,
        name="heads",
    )
    grads_five = to_all(grad_sums_five)
    above = shifted(pairs[height - 1 :], "dp", 1)
    below = shifted(pairs[:1], "dp", -1)
    rim = [
        jnp.concatenate([above[:, c : c + 1], pairs[:, c : c + 1], below[:, c : c + 1]], axis=0)
        for c in (1 + breadth, 2)
    ]
    left = from_behind(rim[0], "stream", 1)
    right = from_behind(rim[1], "stream", -1)

    grad_joined, columns, grad_sums = stage(
        functools.partial(merged_gradient, fine_count),
        [
            (height, width, 2 * C1),
            (rows, width, 4 * C2),
            (everybody, 1, 4 * C1),
        ],
        [
            pairs,
            above,
            below,
            left,
            right,
            total_five,
            grads_five,
            norm_five,
            packed,
            z_three,
            z_four,
            slopes,
            total_three,
            total_one,
        ],
        scalars=[flags],
        name="merged_gradient",
    )
    far = shards // NEAR
    slots = jnp.arange(NEAR, dtype=jnp.int32) ^ (shard_index % NEAR).astype(jnp.int32)
    quarter = 18 * C1 // (4 * shards)
    shifted_rows = pltpu.VMEM((height, width, 4 * C2), F32)
    aligned = quarter % 8 == 0
    if aligned:
        merging_grads = stage(
            merging_product,
            [(NEAR, far, quarter, wide)] * 2,
            [joined, columns],
            scalars=[flags, slots],
            scratch=[pltpu.VMEM((18 * C1, C2), F32), shifted_rows],
            name="merging_product",
        )
    else:
        (merging_grad,) = stage(
            multiply_merging,
            [(18 * C1, C2)],
            [joined, columns],
            scalars=[flags],
            scratch=[shifted_rows],
            name="merging_product",
        )
        merging_grads = slotted(fold_rows(merging_grad, shards))
    merging_grad = merging_grads[0]
    grads_joined = after(to_all(grad_sums), merging_grad)

    quads, grad_one, grad_sums_one = stage(
        functools.partial(coarse_gradient, fine_count, coarse_count),
        [
            (4, half_height, half_width, C1),
            (half_rows, half_width, C1),
            (everybody, 1, 2 * C1),
        ],
        [
            grad_joined,
            z_three,
            total_three,
            grads_joined,
            gains[2][None],
            upward_full,
            z_one,
            total_one,
            slope_one,
        ],
        scratch=[pltpu.VMEM((2, height, width, C1 // 2), F32)],
        name="coarse_gradient",
    )
    late_rows = [4 * C1 // shards, C0 // shards, -(-C2 // (2 * shards))]
    late_args = [
        grad_joined,
        z_four,
        total_one,
        grads_joined,
        gains[4][None],
        grid,
        act_one,
        quads,
        heads_grad,
    ]
    fine_scratch = pltpu.VMEM((height, width, C1), F32)
    if aligned:
        late_grads = stage(
            functools.partial(fine_products, fine_count),
            [(NEAR, far, sum(late_rows), half)] * 2,
            late_args,
            scalars=[flags, slots],
            scratch=[fine_scratch],
            name="fine_products",
        )
    else:
        late_halves = stage(
            functools.partial(fine_halves, fine_count),
            [(2, 4 * C1, half), (2, C0, half)],
            late_args[:-1],
            scratch=[fine_scratch],
            name="fine_products",
        )
        heads_halves = heads_grad[:C2].reshape(2, C2 // 2, wide)
        blocks = [by_shard(value) for value in (*late_halves, heads_halves)]
        late_grads = slotted(jnp.concatenate(blocks, axis=2))
    grads_one = after(to_all(grad_sums_one), late_grads[0])
    down_args = [windows, grad_one, z_one, total_one, grads_one, gains[0][None]]
    if aligned:
        down_grads = stage(
            functools.partial(window_product, coarse_count),
            [(NEAR, far, 9 * C0 // shards, half)] * 2,
            down_args,
            scalars=[flags, slots],
            name="window_product",
        )
    else:
        (halves,) = stage(
            functools.partial(window_halves, coarse_count),
            [(2, 9 * C0, half)],
            down_args,
            name="window_product",
        )
        down_grads = slotted(by_shard(halves))
    down_sums = chip_sums(down_grads[0], exchange(down_grads[1]))
    merging_other = exchange(after(merging_grads[1], down_grads[0]))
    late_other = exchange(after(late_grads[1], down_grads[0]))
    merging_sums = chip_sums(after(merging_grads[0], *down_sums), merging_other)
    late_sums = chip_sums(after(late_grads[0], *down_sums), late_other)
    down_mine, merging_mine, late_mine = map(near_sum, (down_sums, merging_sums, late_sums))
    received = far_sum(down_mine)
    rest = jnp.concatenate([merging_mine, late_mine], axis=1)
    rest_received = far_sum(after(rest, received))
    cuts = [0]
    for count in (down_mine.shape[1], merging_mine.shape[1], *late_rows):
        cuts.append(cuts[-1] + count)

    sums_back = jnp.sum(grads_one[:, 0], axis=0)
    part = jnp.concatenate([jnp.sum(received, axis=0), jnp.sum(rest_received, axis=0)], axis=0)
    swapped = exchange(part[: cuts[3]])
    first_part, second_part = in_order(part[: cuts[3]], swapped)
    down_shard = jnp.concatenate([first_part[: cuts[1]], second_part[: cuts[1]]], axis=1)
    merging_shard = unfold_rows(first_part[None, cuts[1] : cuts[2]], second_part[None, cuts[1] : cuts[2]])
    upward_shard = jnp.concatenate([first_part[cuts[2] :], second_part[cuts[2] :]], axis=1)

    def partial_gram(shard):
        return jnp.tensordot(shard, shard, axes=((0,), (0,)), precision=HIGHEST)

    def lane_rows(gram):
        count = gram.shape[0] // shards
        return jnp.concatenate(
            [
                gram[:, k * half : (k + 1) * half].reshape(shards, count, half)
                for k in range(C1 // half)
            ],
            axis=1,
        )

    shard_groups = [
        (down_weight, down_moment, down_square, down_basis, down_shard),
        (upward_weight, upward_moment, upward_square, upward_basis, upward_shard),
        (merging_weight.T, merging_moment.T, merging_square.T, merging_basis, merging_shard),
    ]
    stepped = stage(
        functools.partial(
            soap_shards,
            (
                (1.0 / math.sqrt(9 * C0), False),
                (1.0 / math.sqrt(C1), False),
                (1.0 / math.sqrt(18 * C1), True),
            ),
        ),
        [group[0].shape for group in shard_groups for _ in range(3)],
        [array for group in shard_groups for array in group],
        name="soap",
    )
    down_renewed, down_momentum, down_variance = stepped[:3]
    upward_renewed, upward_momentum, upward_variance = stepped[3:6]
    merging_renewed, merging_momentum, merging_variance = (value.T for value in stepped[6:])
    gram_two = jnp.pad(partial_gram(merging_shard), ((0, -C2 % shards), (0, wide - C2)))
    gram_two = gram_two.reshape(shards, -1, wide)
    firsts = jnp.pad(lane_rows(partial_gram(down_shard)), ((0, 0), (0, gram_two.shape[1]), (0, 0)))
    seconds = jnp.concatenate([lane_rows(partial_gram(upward_shard)), gram_two], axis=1)
    parts = jnp.where(core == 0, firsts, seconds)
    edge_one = after(grad_one, parts)
    below = shifted(edge_one[1:2], "dp", -1)
    first_col = jnp.concatenate([edge_one[1 : half_rows - 1, 1:2], below[:, 1:2]], axis=0)
    right = from_behind(first_col, "stream", -1)
    gram_parts = after(lax.all_to_all(parts, "dp", 0, 0, tiled=True), *stepped, right)
    gram_sum = jnp.sum(gram_parts, axis=0)
    (feats_grad,) = stage(
        functools.partial(input_gradient, fine_count, coarse_count),
        [(height, breadth, C0)],
        [
            grad_one,
            below,
            right,
            z_one,
            total_one,
            after(grads_one, gram_sum),
            gains[0][None],
            down_full,
            grad_joined,
            z_four,
            grads_joined,
            gains[4][None],
            lateral_weight,
            shown,
        ],
        scalars=[flags],
        scratch=[
            pltpu.VMEM((half_rows - 1, half_width, 9 * C0), F32),
            pltpu.VMEM((height, width, C0), F32),
            fine_scratch,
        ],
        name="input_gradient",
    )
    gram_rows = gram_sum.shape[0]
    final = everyone(jnp.concatenate([gram_sum, part[cuts[3] :]], axis=0))
    final = after(final, feats_grad)
    final_other = exchange(final)
    grams = (down_gram, upward_gram, lateral_gram, merging_gram, heads_gram)
    bases = (down_basis, upward_basis, lateral_basis, merging_basis, heads_basis)
    orders = [C1, C1, C1, C2, CH]
    padded = [-(-n // NB) * NB for n in orders]
    close_args = [
        *grams,
        *bases,
        lateral_weight,
        lateral_moment,
        lateral_square,
        heads_weight,
        heads_moment,
        heads_square,
    ]
    close_outs = [(n, n) for n in orders] * 2 + [(C0, C1)] * 3 + [(C2, CH)] * 3
    close_scratch = [pltpu.VMEM((n, n), F32) for n in (C1, CH)]
    close_scratch += [pltpu.VMEM((n, n), F32) for n in padded] * 2
    rates = (1.0 / math.sqrt(C0), 1.0 / math.sqrt(C2))
    add_shapes = [(C1, C1), (C1, C1), (C0, C1), (C2, C2), (C2, CH)]
    if aligned:
        ends = (gram_rows, gram_rows + late_rows[1], gram_rows + sum(late_rows[1:]))
        closed = stage(
            functools.partial(close_parts, rates, ends),
            close_outs,
            [final, final_other, *close_args],
            scalars=[flags],
            scratch=close_scratch + [pltpu.VMEM(shape, F32) for shape in add_shapes],
            name="close",
        )
    else:
        adds = assembled(final, final_other, gram_rows, late_rows[1])
        closed = stage(
            functools.partial(close, rates),
            close_outs,
            [*close_args[:10], *adds, *close_args[10:]],
            scratch=close_scratch,
            name="close",
        )
    down_gramian, upward_gramian, lateral_gramian, merging_gramian, heads_gramian = closed[:5]
    down_rotation, upward_rotation, lateral_rotation, merging_rotation, heads_rotation = closed[5:10]
    lateral_renewed, lateral_momentum, lateral_variance = closed[10:13]
    heads_renewed, heads_momentum, heads_variance = closed[13:]

    sums_fine = jnp.sum(grads_joined[:, 0], axis=0)
    sums_late = jnp.sum(grads_five[:, 0], axis=0)
    grad_vector = jnp.concatenate(
        [
            sums_back,
            sums_fine[:C1],
            sums_fine[2 * C1 : 3 * C1],
            sums_fine[C1 : 2 * C1],
            sums_fine[3 * C1 :],
            sums_late[:C2],
            sums_late[wide : wide + C2],
            sums_late[2 * wide : 2 * wide + CH],
        ]
    )
    vector_renewed, vector_momentum, vector_variance = adam_vector(
        vector_params, vector_moment, vector_square, grad_vector
    )
    return (
        head_maps,
        feats_grad,
        vector_renewed,
        vector_momentum,
        vector_variance,
        down_renewed,
        down_momentum,
        down_variance,
        down_gramian,
        down_rotation,
        upward_renewed,
        upward_momentum,
        upward_variance,
        upward_gramian,
        upward_rotation,
        lateral_renewed,
        lateral_momentum,
        lateral_variance,
        lateral_gramian,
        lateral_rotation,
        merging_renewed,
        merging_momentum,
        merging_variance,
        merging_gramian,
        merging_rotation,
        heads_renewed,
        heads_momentum,
        heads_variance,
        heads_gramian,
        heads_rotation,
    )


def solution(mesh):
    in_specs = (
        P("dp", "stream", None),
        P("dp", "stream"),
        P("dp", "stream", None),
        P(),
        P(),
        P(),
        P("dp", None),
        P("dp", None),
        P("dp", None),
        P(),
        P(),
        P("dp", None),
        P("dp", None),
        P("dp", None),
        P(),
        P(),
        P(),
        P(),
        P(),
        P(),
        P(),
        P("dp", None),
        P("dp", None),
        P("dp", None),
        P(),
        P(),
        P(),
        P(),
        P(),
        P(),
        P(),
    )
    out_specs = (
        P("dp", "stream", None),
        P("dp", "stream", None),
        P(),
        P(),
        P(),
        P("dp", None),
        P("dp", None),
        P("dp", None),
        P(),
        P(),
        P("dp", None),
        P("dp", None),
        P("dp", None),
        P(),
        P(),
        P(),
        P(),
        P(),
        P(),
        P(),
        P("dp", None),
        P("dp", None),
        P("dp", None),
        P(),
        P(),
        P(),
        P(),
        P(),
        P(),
        P(),
    )
    return jax.shard_map(local, mesh=mesh, in_specs=in_specs, out_specs=out_specs, check_vma=False)
```

```python
import functools
import math

import jax
import jax.numpy as jnp
from jax import lax
from jax.experimental import pallas as pl
from jax.experimental.pallas import tpu as pltpu
from jax.sharding import PartitionSpec as P

C0 = 128
C1 = 256
C2 = 64
CH = 70
SCENE_ROWS = 180
STEP = 10


EPS_NORM = 1e-05
BETA_ONE = 0.9
BETA_TWO = 0.95
BETA_GRAM = 0.95
EPS_ADAM = 1e-08
DECAY = 0.01
VECTOR_RATE = 0.1
HIGHEST = lax.Precision.HIGHEST


F32 = jnp.float32
HIGH = lax.Precision.HIGH
RIM_UP, RIM_DOWN, RIM_LEFT, RIM_RIGHT = 3, 2, 3, 2
LEAD = 10
NEAR = 4


def product(left, right, over_left, over_right, precision=HIGH):
    dims = (((over_left,), (over_right,)), ((), ()))
    return lax.dot_general(
        left, right, dims, precision=precision, preferred_element_type=F32
    )


def stage(body, outs, args, scalars=(), scratch=(), name=None, far_args=(), far_outs=()):
    vmem = pl.BlockSpec(memory_space=pltpu.VMEM)
    smem = pl.BlockSpec(memory_space=pltpu.SMEM)
    away = pl.BlockSpec(memory_space=pl.ANY)
    shapes = [jax.ShapeDtypeStruct(shape, F32) for shape in outs]
    return pl.pallas_call(
        body,
        out_shape=shapes,
        in_specs=[smem] * len(scalars)
        + [away if i in far_args else vmem for i in range(len(args))],
        out_specs=[away if i in far_outs else vmem for i in range(len(shapes))],
        scratch_shapes=list(scratch),
        compiler_params=pltpu.CompilerParams(vmem_limit_bytes=56 << 20),
        name=name,
    )(*scalars, *args)


def channel_sums(ref):
    return jnp.sum(ref[...], axis=0)


def spread_of(total, pixels):
    half = total.shape[1] // 2
    centre = total[:, :half] * (1.0 / pixels)
    second = total[:, half:] * (1.0 / pixels)
    return centre, lax.rsqrt(second - centre * centre + EPS_NORM)


def cols_between(count, lanes, first, past):
    col = lax.broadcasted_iota(jnp.int32, (count, lanes), 0)
    return (col >= first) & (col < past)


def row_total(value):
    return jnp.sum(value, axis=0, keepdims=True)


def send(ref, row):
    ref[...] = jnp.broadcast_to(row[None], ref.shape)


def pad_lateral(masked, up, down, left, right, lateral, grid, z_four, sums):
    height, breadth, channels = masked.shape
    grid[...] = jnp.zeros(grid.shape, F32)
    inner = slice(LEAD, LEAD + breadth)
    grid[0:RIM_UP, inner] = up[...]
    grid[RIM_UP : RIM_UP + height, inner] = masked[...]
    grid[RIM_UP + height :, inner] = down[...]
    grid[:, LEAD - RIM_LEFT : LEAD] = left[...]
    grid[:, LEAD + breadth : LEAD + breadth + RIM_RIGHT] = right[...]
    width = z_four.shape[1]
    own = cols_between(width, C1, 2, 2 + breadth)
    total = jnp.zeros((1, C1), F32)
    square = jnp.zeros((1, C1), F32)
    tile = 6
    for first in range(0, height + 2, tile):
        block = grid[2 + first : 2 + first + tile, LEAD - 2 : LEAD - 2 + width]
        made = product(block.reshape(tile * width, channels), lateral[...], 1, 0)
        made = made.reshape(tile, width, C1)
        z_four[first : first + tile] = made
        for row in range(tile):
            if 1 <= first + row <= height:
                kept = jnp.where(own, made[row], 0.0)
                total = total + row_total(kept)
                square = square + row_total(kept * kept)
    sums[...] = jnp.concatenate([total, square], axis=1)


def coarse_arranged(
    flags, place, grid, pieces_far, swapped_far, sums_four, z_one, windows, sums, weight, *scratch
):
    pieces, swapped, arrived = scratch
    rows = pieces.shape[2]
    copies = [
        start_copy(pieces_far.at[:, :, pl.ds(0, rows)], pieces, arrived.at[0]),
        start_copy(swapped_far.at[:, :, pl.ds(0, rows)], swapped, arrived.at[1]),
    ]
    build_windows(flags, grid, windows, z_one.shape[1])
    for copy in copies:
        copy.wait()
    arrange(0, rows, place, pieces, swapped, weight)
    multiply_map(weight, sums_four, z_one, windows, sums)


def coarse_map(flags, grid, weight, sums_four, z_one, windows, sums):
    build_windows(flags, grid, windows, z_one.shape[1])
    multiply_map(weight, sums_four, z_one, windows, sums)


def build_windows(flags, grid, windows, width):
    for i in range(windows.shape[0]):
        for a in range(3):
            for b in range(3):
                piece = grid[2 * i + a, pl.ds(LEAD - 3 + b, width, 2), :]
                if a == 0:
                    piece = piece * flags[i]
                tap = 3 * a + b
                windows[i, :, tap * C0 : (tap + 1) * C0] = piece


def multiply_map(weight, sums_four, z_one, windows, sums):
    rows, width = z_one.shape[0], z_one.shape[1]
    half_breadth = width - 3
    made = product(windows[...].reshape(rows * width, 9 * C0), weight[...], 1, 0)
    z_one[...] = made.reshape(rows, width, C1)
    own = cols_between(width, C1, 1, 1 + half_breadth)
    total = jnp.zeros((1, C1), F32)
    square = jnp.zeros((1, C1), F32)
    for i in range(1, rows - 1):
        kept = jnp.where(own, z_one[i], 0.0)
        total = total + row_total(kept)
        square = square + row_total(kept * kept)
    send(sums, jnp.concatenate([total, square, sums_four[...]], axis=1))


def window_halves(
    coarse_pixels, windows, grad_one, z_one, total_one, grads_one, gain_one, halves
):
    args = (windows, grad_one, z_one, total_one, grads_one, gain_one)
    made = multiply_windows(coarse_pixels, *args)
    halves[0] = made[:, : C1 // 2]
    halves[1] = made[:, C1 // 2 :]


def window_product(
    coarse_pixels, flags, slots, windows, grad_one, z_one, total_one, grads_one, gain_one, mine, other
):
    args = (windows, grad_one, z_one, total_one, grads_one, gain_one)
    made = multiply_windows(coarse_pixels, *args)
    shards = mine.shape[0] * mine.shape[1]
    by_slot(made, mine, other, slots, flags[30] == 0.0, shards, 0)


def multiply_windows(coarse_pixels, windows, grad_one, z_one, total_one, grads_one, gain_one):
    rows, width, depth = windows.shape
    centre, spread = spread_of(channel_sums(total_one)[:, : 2 * C1], coarse_pixels)
    gained = channel_sums(grads_one)
    scale = gain_one[...] * spread
    mean_gain = gained[:, :C1] * (1.0 / coarse_pixels)
    mean_shift = gained[:, C1:] * (1.0 / coarse_pixels)
    own = cols_between(width, C1, 1, width - 2)
    parts = []
    for i in range(1, rows - 1):
        normed = (z_one[i] - centre) * spread
        value = scale * (grad_one[i] - mean_shift - normed * mean_gain)
        parts.append(jnp.where(own, value, 0.0))
    inside = windows[1 : rows - 1].reshape((rows - 2) * width, depth)
    return product(inside, jnp.concatenate(parts, axis=0), 0, 0)


def upsample(pixels, z_one, total_one, gain, shift, weight, z_three, act_one, slope_one, sums):
    rows, width = z_one.shape[0], z_one.shape[1]
    half_breadth = width - 3
    centre, spread = spread_of(channel_sums(total_one)[:, : 2 * C1], pixels)
    for i in range(rows):
        hidden = (z_one[i] - centre) * spread * gain[...] + shift[...]
        sigmoid = lax.logistic(hidden)
        act_one[i] = hidden * sigmoid
        slope_one[i] = sigmoid * (1.0 + hidden * (1.0 - sigmoid))
    active = act_one[...].reshape(rows * width, C1)
    own = cols_between(width, C1, 1, 1 + half_breadth)
    total = jnp.zeros((1, C1), F32)
    square = jnp.zeros((1, C1), F32)
    half = C1 // 2
    for a in range(2):
        for b in range(2):
            tap = 2 * a + b
            made = product(active, weight[tap * C1 : (tap + 1) * C1], 1, 0)
            for i in range(rows):
                part = made[i * width : (i + 1) * width]
                place = 2 * i + a - 1
                if 0 <= place < 2 * rows - 2:
                    for k in range(2):
                        z_three[k, place, pl.ds(b, width, 2), :] = part[:, k * half : (k + 1) * half]
                if 1 <= i < rows - 1:
                    kept = jnp.where(own, part, 0.0)
                    total = total + row_total(kept)
                    square = square + row_total(kept * kept)
    send(sums, jnp.concatenate([total, square], axis=1))


def pack_merging(weight, packed):
    for a in range(3):
        pieces = [
            weight[(3 * a + b) * 2 * C1 : (3 * a + b + 1) * 2 * C1] for b in range(3)
        ]
        pieces.append(jnp.zeros((2 * C1, C2), F32))
        packed[:, a * 4 * C2 : (a + 1) * 4 * C2] = jnp.concatenate(pieces, axis=1)


def arrange(first, rows, place, pieces, swapped, out):
    near, far, _, lanes = pieces.shape
    front = place[near * far] == 0
    for low in range(near):
        for high in range(far):
            at = pl.ds(pl.multiple_of(place[low * far + high] * rows, 8), rows)
            mine = pieces[low, high, first : first + rows]
            other = swapped[low, high, first : first + rows]
            out[at, 0:lanes] = jnp.where(front, mine, other)
            out[at, lanes:] = jnp.where(front, other, mine)


def arrange_merging(first, place, pieces, swapped, packed, weight):
    near, far, last, _ = pieces.shape
    rows = last - first
    front = place[near * far] == 0
    for low in range(near):
        for high in range(far):
            mine, other = pieces[low, high, first:], swapped[low, high, first:]
            values = (jnp.where(front, mine, other), jnp.where(front, other, mine))
            for core in range(2):
                for side in range(2):
                    start = (place[low * far + high] * 4 + 2 * core + side) * rows
                    at = pl.ds(pl.multiple_of(start, 8), rows)
                    weight[at, :] = values[core][:, side * C2 : (side + 1) * C2]
    pack_merging(weight, packed)


def start_copy(source, target, semaphore):
    copy = pltpu.make_async_copy(source, target, semaphore)
    copy.start()
    return copy


def merge(
    pixels,
    flags,
    z_three_far,
    z_four_far,
    total_three,
    total_one,
    norms,
    packed_far,
    merged,
    joined_far,
    slopes_far,
    sums,
    taps,
    z_three,
    z_four,
    packed,
    joined,
    slopes,
    arrived,
    left,
):
    rows, width = z_four.shape[0], z_four.shape[1]
    height = rows - 2
    breadth = width - 6
    tile = 6
    firsts = list(range(0, rows, tile))
    coming = []
    for t, r in enumerate(firsts):
        part = pl.ds(r, tile)
        coming.append(
            [
                start_copy(z_three_far.at[:, part], z_three.at[:, part], arrived.at[2 * t]),
                start_copy(z_four_far.at[part], z_four.at[part], arrived.at[2 * t + 1]),
            ]
        )
    weight_copy = start_copy(packed_far, packed, arrived.at[2 * len(firsts)])
    sum_three = channel_sums(total_three)
    sum_four = channel_sums(total_one)[:, 2 * C1 :]
    centre_three, spread_three = spread_of(sum_three, pixels)
    centre_four, spread_four = spread_of(sum_four, pixels)
    centre = jnp.concatenate([centre_three, centre_four], axis=1)
    spread = jnp.concatenate([spread_three, spread_four], axis=1)
    scale = spread * norms[0:1]
    offset = norms[1:2] - centre * scale
    col = lax.broadcasted_iota(jnp.int32, (width, 2 * C1), 0)
    dead = ((col == 1) & (flags[30] == 0.0)) | ((col == 2 + breadth) & (flags[31] == 0.0))

    def activate(r, carry):
        raw = jnp.concatenate([z_three[0, r], z_three[1, r], z_four[r]], axis=1)
        hidden = raw * scale + offset
        sigmoid = lax.logistic(hidden)
        joined[r] = jnp.where(dead, 0.0, hidden * sigmoid)
        slopes[r] = sigmoid * (1.0 + hidden * (1.0 - sigmoid))
        return carry

    going = []
    for t, r in enumerate(firsts):
        for copy in coming[t]:
            copy.wait()
        lax.fori_loop(r, r + tile, activate, 0)
        part = pl.ds(r, tile)
        going.append(start_copy(joined.at[part], joined_far.at[part], left.at[2 * t]))
        going.append(start_copy(slopes.at[part], slopes_far.at[part], left.at[2 * t + 1]))
    weight_copy.wait()

    def spread_taps(t, carry):
        r = pl.multiple_of(t * tile, tile)
        block = joined[pl.ds(r, tile)].reshape(tile * width, 2 * C1)
        taps[pl.ds(r, tile)] = product(block, packed[...], 1, 0).reshape(tile, width, 12 * C2)
        return carry

    lax.fori_loop(0, rows // tile, spread_taps, 0)
    own = cols_between(width, 2 * C2, 2, 2 + breadth)
    lane = lax.broadcasted_iota(jnp.int32, (width, 2 * C2), 1)
    total = jnp.zeros((1, 2 * C2), F32)
    square = jnp.zeros((1, 2 * C2), F32)
    for row in range(height):
        r = row + 1
        both = (
            taps[r - 1, :, 0 : 4 * C2] * flags[10 + r]
            + taps[r, :, 4 * C2 : 8 * C2]
            + taps[r + 1, :, 8 * C2 : 12 * C2] * flags[11 + r]
        )
        first, second = both[:, : 2 * C2], both[:, 2 * C2 :]
        out = (
            pltpu.roll(first, 1, 0)
            + pltpu.roll(first, C2, 1)
            + pltpu.roll(second, width - 1, 0)
        )
        out = jnp.where(own & (lane < C2), out, 0.0)
        merged[row] = out
        total = total + row_total(out)
        square = square + row_total(out * out)
    send(sums, jnp.concatenate([total, square], axis=1))
    for copy in going:
        copy.wait()


def heads(
    pixels,
    flags,
    merged,
    total_five,
    norms,
    weight,
    bias,
    cotangent,
    maps,
    pairs,
    last_row,
    first_row,
    edge,
    weight_grad,
    sums,
    active,
    upstream,
):
    height, width, _ = merged.shape
    breadth = width - 6
    centre, spread = spread_of(channel_sums(total_five)[:, : 4 * C2], pixels)
    own = cols_between(width, 2 * C2, 2, 2 + breadth)
    upstream[...] = jnp.zeros(upstream.shape, F32)
    for r in range(height):
        upstream[r, 2 : 2 + breadth, 0:CH] = cotangent[r]
    flat = upstream[...].reshape(height * width, 2 * C2)
    grad = product(flat, weight[...], 1, 1).reshape(height, width, 2 * C2)
    grad_gain = jnp.zeros((1, 2 * C2), F32)
    grad_shift = jnp.zeros((1, 2 * C2), F32)
    for r in range(height):
        normed = jnp.where(own, (merged[r] - centre) * spread, 0.0)
        hidden = norms[0:1] * normed + norms[1:2]
        sigmoid = lax.logistic(hidden)
        active[r] = hidden * sigmoid
        grad_hidden = grad[r] * sigmoid * (1.0 + hidden * (1.0 - sigmoid))
        pair = grad_hidden + pltpu.roll(normed, C2, 1)
        pairs[r] = pair
        edge[r] = jnp.where(flags[30] == 0.0, pair[1 + breadth : 2 + breadth], pair[2:3])
        if r == 0:
            first_row[0] = pair
        if r == height - 1:
            last_row[0] = pair
        grad_gain = grad_gain + row_total(grad_hidden * normed)
        grad_shift = grad_shift + row_total(grad_hidden)
    send(sums, jnp.concatenate([grad_gain, grad_shift, row_total(flat)], axis=1))
    act = active[...].reshape(height * width, 2 * C2)
    made = product(act, weight[...], 1, 0).reshape(height, width, 2 * C2) + bias[...]
    for r in range(height):
        maps[r] = pltpu.roll(made[r], width - 2, 0).T[0:CH, 0:breadth]
    weight_grad[...] = product(act, flat, 0, 0)


def merged_gradient(
    pixels,
    flags,
    pairs,
    above,
    below,
    side,
    total_five,
    grads_five,
    norm_five,
    packed_far,
    z_three_far,
    z_four_far,
    slopes_far,
    total_three,
    total_one,
    grad_far,
    columns_far,
    sums,
    packed,
    z_three,
    z_four,
    slopes,
    grad_joined,
    columns,
    arrived,
    left_sems,
):
    height, width, _ = pairs.shape
    breadth = width - 6
    lanes = 2 * C2
    tile = 4
    weight_copy = start_copy(packed_far, packed, arrived.at[0])
    coming = []
    for t in range(height // tile):
        part = pl.ds(t * tile + 1, tile)
        coming.append(
            [
                start_copy(slopes_far.at[part], slopes.at[part], arrived.at[3 * t + 1]),
                start_copy(z_three_far.at[:, part], z_three.at[:, part], arrived.at[3 * t + 2]),
                start_copy(z_four_far.at[part], z_four.at[part], arrived.at[3 * t + 3]),
            ]
        )
    _, spread = spread_of(channel_sums(total_five)[:, : 4 * C2], pixels)
    gained = channel_sums(grads_five)
    scale = norm_five[0:1] * spread
    mean_gain = gained[:, :lanes] * (1.0 / pixels)
    mean_shift = gained[:, lanes : 2 * lanes] * (1.0 / pixels)
    col = lax.broadcasted_iota(jnp.int32, (width, lanes), 0)
    lane = lax.broadcasted_iota(jnp.int32, (width, lanes), 1)
    live = (
        ((col >= 2) & (col < 2 + breadth))
        | ((col == 1) & (flags[30] != 0.0))
        | ((col == 2 + breadth) & (flags[31] != 0.0))
    ) & (lane < C2)
    target = jnp.where(flags[30] == 0.0, 2 + breadth, 1)
    for r in range(height + 2):
        if r == 0:
            raw = above[0]
        elif r == height + 1:
            raw = below[0]
        else:
            raw = pairs[r - 1]
        raw = jnp.where(col == target, side[r], raw)
        normed = pltpu.roll(raw, C2, 1)
        value = jnp.where(live, scale * (raw - mean_shift - normed * mean_gain), 0.0)
        columns[r, :, 0:lanes] = pltpu.roll(value, width - 1, 0) + pltpu.roll(value, C2, 1)
        columns[r, :, lanes:] = pltpu.roll(value, 1, 0)
    going = [start_copy(columns, columns_far, left_sems.at[0])]
    centre_three, spread_three = spread_of(channel_sums(total_three), pixels)
    centre_four, spread_four = spread_of(channel_sums(total_one)[:, 2 * C1 :], pixels)
    centre = jnp.concatenate([centre_three, centre_four], axis=1)
    spread = jnp.concatenate([spread_three, spread_four], axis=1)
    own = cols_between(width, 2 * C1, 2, 2 + breadth)

    def gradient(t, carry):
        r = t * tile
        block = jnp.zeros((tile * width, 2 * C1), F32)
        for a in range(3):
            rows = []
            for k in range(tile):
                source = r + k + 2 - a
                row = columns[source]
                if a == 0:
                    row = row * flags[10 + source]
                if a == 2:
                    row = row * flags[11 + source]
                rows.append(row)
            block = block + product(
                jnp.concatenate(rows, axis=0), packed[:, a * 4 * C2 : (a + 1) * 4 * C2], 1, 1
            )
        gain_sum, shift_sum = carry
        for k in range(tile):
            grad = jnp.where(own, block[k * width : (k + 1) * width] * slopes[r + k + 1], 0.0)
            grad_joined[r + k] = grad
            raw = jnp.concatenate(
                [z_three[0, r + k + 1], z_three[1, r + k + 1], z_four[r + k + 1]], axis=1
            )
            normed = (raw - centre) * spread
            gain_sum = gain_sum + row_total(grad * normed)
            shift_sum = shift_sum + row_total(grad)
        return gain_sum, shift_sum

    empty = jnp.zeros((1, 2 * C1), F32)
    carry = (empty, empty)
    weight_copy.wait()
    for t in range(height // tile):
        for copy in coming[t]:
            copy.wait()
        carry = gradient(t, carry)
        part = pl.ds(t * tile, tile)
        going.append(start_copy(grad_joined.at[part], grad_far.at[part], left_sems.at[t + 1]))
    send(sums, jnp.concatenate(carry, axis=1))
    for copy in going:
        copy.wait()


def by_slot(value, mine, other, slots, front, shards, first):
    rows = value.shape[0] // shards
    half = value.shape[1] // 2
    for shard in range(shards):
        piece = value[shard * rows : (shard + 1) * rows]
        low, high = piece[:, :half], piece[:, half:]
        place = slots[shard % NEAR], shard // NEAR, slice(first, first + rows)
        mine[place] = jnp.where(front, low, high)
        other[place] = jnp.where(front, high, low)


def merging_product(flags, slots, joined, columns, mine, other, grads, shifted_rows):
    multiply_merging(flags, joined, columns, grads, shifted_rows)
    front = flags[30] == 0.0
    near, far, rows, _ = mine.shape
    for shard in range(near * far):
        start = 4 * rows * shard
        runs = [grads[start + i * rows : start + (i + 1) * rows] for i in range(4)]
        first = jnp.concatenate(runs[:2], axis=1)
        second = jnp.concatenate(runs[2:], axis=1)
        place = slots[shard % near], shard // near
        mine[place] = jnp.where(front, first, second)
        other[place] = jnp.where(front, second, first)


def multiply_merging(flags, joined, columns, grads, shifted_rows):
    rows, width, _ = joined.shape
    height = rows - 2
    inside = joined[1 : rows - 1].reshape(height * width, 2 * C1)
    own = cols_between(width, 4 * C2, 2, width - 4)
    for a in range(3):
        for r in range(height):
            source = r + 2 - a
            row = columns[source]
            if a == 0:
                row = row * flags[10 + source]
            if a == 2:
                row = row * flags[11 + source]
            shifted_rows[r] = jnp.where(own, row, 0.0)
        made = product(inside, shifted_rows[...].reshape(height * width, 4 * C2), 0, 0)
        for b in range(3):
            grads[(3 * a + b) * 2 * C1 : (3 * a + b + 1) * 2 * C1] = made[:, b * C2 : (b + 1) * C2]


def coarse_gradient(
    pixels,
    coarse_pixels,
    grad_joined,
    z_three,
    total_three,
    grads_joined,
    gain_three,
    weight,
    z_one,
    total_one,
    slope_one,
    quads,
    grad_one,
    sums,
    fine,
):
    height, width = grad_joined.shape[0], grad_joined.shape[1]
    rows, half_width = z_one.shape[0], z_one.shape[1]
    half = C1 // 2
    centre, spread = spread_of(channel_sums(total_three), pixels)
    gained = channel_sums(grads_joined)
    scale = gain_three[...] * spread
    mean_gain = gained[:, :C1] * (1.0 / pixels)
    mean_shift = gained[:, 2 * C1 : 3 * C1] * (1.0 / pixels)
    own = cols_between(width, C1, 2, width - 4)

    def fill(r, carry):
        raw = jnp.concatenate([z_three[0, r + 1], z_three[1, r + 1]], axis=1)
        normed = (raw - centre) * spread
        value = scale * (grad_joined[r, :, 0:C1] - mean_shift - normed * mean_gain)
        value = jnp.where(own, value, 0.0)
        fine[0, r] = value[:, :half]
        fine[1, r] = value[:, half:]
        return carry

    lax.fori_loop(0, height, fill, 0)
    grad = jnp.zeros(((rows - 2) * half_width, C1), F32)
    for a in range(2):
        for b in range(2):
            tap = 2 * a + b
            for i in range(rows - 2):
                for k in range(2):
                    quads[tap, i, :, k * half : (k + 1) * half] = fine[
                        k, 2 * i + a, pl.ds(b, half_width, 2), :
                    ]
            flat = quads[tap].reshape((rows - 2) * half_width, C1)
            grad = grad + product(flat, weight[tap * C1 : (tap + 1) * C1], 1, 1)
    centre, spread = spread_of(channel_sums(total_one)[:, : 2 * C1], coarse_pixels)
    own = cols_between(half_width, C1, 1, half_width - 2)
    gain_sum = jnp.zeros((1, C1), F32)
    shift_sum = jnp.zeros((1, C1), F32)
    grad_one[0] = jnp.zeros((half_width, C1), F32)
    grad_one[rows - 1] = jnp.zeros((half_width, C1), F32)
    for i in range(1, rows - 1):
        value = grad[(i - 1) * half_width : i * half_width] * slope_one[i]
        value = jnp.where(own, value, 0.0)
        grad_one[i] = value
        gain_sum = gain_sum + row_total(value * ((z_one[i] - centre) * spread))
        shift_sum = shift_sum + row_total(value)
    send(sums, jnp.concatenate([gain_sum, shift_sum], axis=1))


def lateral_gradient(pixels, grad_joined, z_four, total_one, grads_joined, gain_four, fine):
    height, width = grad_joined.shape[0], grad_joined.shape[1]
    centre, spread = spread_of(channel_sums(total_one)[:, 2 * C1 :], pixels)
    gained = channel_sums(grads_joined)
    scale = gain_four[...] * spread
    mean_gain = gained[:, C1 : 2 * C1] * (1.0 / pixels)
    mean_shift = gained[:, 3 * C1 :] * (1.0 / pixels)
    own = cols_between(width, C1, 2, width - 4)

    def fill(r, carry):
        normed = (z_four[r + 1] - centre) * spread
        value = scale * (grad_joined[r, :, C1:] - mean_shift - normed * mean_gain)
        fine[r] = jnp.where(own, value, 0.0)
        return carry

    lax.fori_loop(0, height, fill, 0)


def fine_halves(
    pixels,
    grad_joined,
    z_four,
    total_one,
    grads_joined,
    gain_four,
    grid,
    act_one,
    quads,
    upward_halves,
    lateral_halves,
    fine,
):
    height, width = grad_joined.shape[0], grad_joined.shape[1]
    rows, half_width = act_one.shape[0], act_one.shape[1]
    half = C1 // 2
    lateral_gradient(pixels, grad_joined, z_four, total_one, grads_joined, gain_four, fine)
    flat = fine[...].reshape(height * width, C1)
    source = grid[RIM_UP : RIM_UP + height, LEAD - 2 : LEAD - 2 + width]
    made = product(source.reshape(height * width, C0), flat, 0, 0)
    lateral_halves[0] = made[:, :half]
    lateral_halves[1] = made[:, half:]
    inside = act_one[1 : rows - 1].reshape((rows - 2) * half_width, C1)
    for tap in range(4):
        made = product(inside, quads[tap].reshape((rows - 2) * half_width, C1), 0, 0)
        for side in range(2):
            upward_halves[side, tap * C1 : (tap + 1) * C1] = made[
                :, side * half : (side + 1) * half
            ]


def fine_products(
    pixels,
    flags,
    slots,
    grad_joined,
    z_four,
    total_one,
    grads_joined,
    gain_four,
    grid,
    act_one,
    quads,
    heads_grad,
    merging_mine,
    merging_other,
    mine,
    other,
    fine,
):
    height, width = grad_joined.shape[0], grad_joined.shape[1]
    rows, half_width = act_one.shape[0], act_one.shape[1]
    shards = mine.shape[0] * mine.shape[1]
    front = flags[30] == 0.0
    lateral_gradient(pixels, grad_joined, z_four, total_one, grads_joined, gain_four, fine)
    inside = act_one[1 : rows - 1].reshape((rows - 2) * half_width, C1)
    parts = [
        product(inside, quads[tap].reshape((rows - 2) * half_width, C1), 0, 0)
        for tap in range(4)
    ]
    first = merging_mine.shape[2]
    mine[:, :, :first] = merging_mine[...]
    other[:, :, :first] = merging_other[...]
    by_slot(jnp.concatenate(parts, axis=0), mine, other, slots, front, shards, first)
    flat = fine[...].reshape(height * width, C1)
    source = grid[RIM_UP : RIM_UP + height, LEAD - 2 : LEAD - 2 + width]
    made = product(source.reshape(height * width, C0), flat, 0, 0)
    first += 4 * C1 // shards
    by_slot(made, mine, other, slots, front, shards, first)
    first += C0 // shards
    both = jnp.concatenate([heads_grad[0 : C2 // 2], heads_grad[C2 // 2 : C2]], axis=1)
    by_slot(both, mine, other, slots, front, shards, first)


def input_gradient(
    pixels,
    coarse_pixels,
    flags,
    grad_one,
    below,
    right,
    z_one,
    total_one,
    grads_one,
    gain_one,
    weight,
    grad_joined,
    z_four,
    grads_joined,
    gain_four,
    lateral,
    occupancy,
    out,
    taps,
    fine,
    wide_fine,
):
    lateral_gradient(
        pixels, grad_joined, z_four, total_one, grads_joined, gain_four, wide_fine
    )
    flat = wide_fine[...].reshape(-1, C1)
    grad_masked = product(flat, lateral[...], 1, 1).reshape(fine.shape)
    rows, half_width = z_one.shape[0], z_one.shape[1]
    height, breadth, _ = occupancy.shape
    centre, spread = spread_of(channel_sums(total_one)[:, : 2 * C1], coarse_pixels)
    gained = channel_sums(grads_one)
    scale = gain_one[...] * spread
    mean_gain = gained[:, :C1] * (1.0 / coarse_pixels)
    mean_shift = gained[:, C1:] * (1.0 / coarse_pixels)
    col = lax.broadcasted_iota(jnp.int32, (half_width, C1), 0)
    edge = half_width - 2
    live = ((col >= 1) & (col < edge)) | ((col == edge) & (flags[31] != 0.0))
    parts = []
    for i in range(1, rows):
        raw = grad_one[i] if i < rows - 1 else below[0]
        raw = jnp.where(col == edge, right[i - 1], raw)
        normed = (z_one[i] - centre) * spread
        value = scale * (raw - mean_shift - normed * mean_gain)
        parts.append(jnp.where(live, value, 0.0))
    made = product(jnp.concatenate(parts, axis=0), weight[...], 1, 1)
    taps[...] = made.reshape(rows - 1, half_width, 9 * C0)

    def tap(a, b, i):
        value = taps[i, :, (3 * a + b) * C0 : (3 * a + b + 1) * C0]
        if b == 0:
            value = pltpu.roll(value, half_width - 1, 0)
        if a == 0:
            value = value * flags[i + 1]
        return value

    for i in range(rows - 2):
        fine[2 * i, pl.ds(0, half_width, 2), :] = tap(1, 1, i)
        fine[2 * i, pl.ds(1, half_width, 2), :] = tap(1, 2, i) + tap(1, 0, i)
        fine[2 * i + 1, pl.ds(0, half_width, 2), :] = tap(2, 1, i) + tap(0, 1, i + 1)
        fine[2 * i + 1, pl.ds(1, half_width, 2), :] = (
            tap(2, 2, i) + tap(2, 0, i) + tap(0, 2, i + 1) + tap(0, 0, i + 1)
        )
    for r in range(height):
        total = fine[r] + grad_masked[r]
        out[pl.ds(r, breadth, height), :] = total[2 : 2 + breadth] * occupancy[r]


def dot(a,b,ca,cb):
    return lax.dot_general(a,b,(((ca,),(cb,)),((),())),precision=HIGHEST,preferred_element_type=F32)
NB=64
W=8
def base_inverse(blocks):
    lane=lax.broadcasted_iota(jnp.int32,(8,128),1); row=lax.broadcasted_iota(jnp.int32,(8,128),0)
    T=NB//8
    xs=[]
    for b in blocks:
        tiles=[]
        for t in range(T):
            pad=jnp.zeros((8,128-NB),F32)
            tiles.append(jnp.concatenate([b[8*t:8*t+8],pad],axis=1)+(lane==row+(NB+8*t)).astype(F32))
        xs.append(tiles)
    for g in range(0,NB,W):
        own=g//8
        cols=[[{t:jnp.broadcast_to(x[t][:,g+j:g+j+1],(8,128)) for t in range(own,T)} for j in range(W)] for x in xs]
        for j in range(W):
            k=(g+j)%8
            for m in range(len(xs)):
                c=cols[m][j]
                inv=1.0/c[own][k:k+1,:]
                rest=[(xs[m],xs[m][own][k:k+1,:])]+[(cols[m][u],cols[m][u][own][k:k+1,:]) for u in range(j+1,W)]
                for t in range(own,T):
                    f=(jnp.where(row>k,c[t],0.0) if t==own else c[t])*inv
                    for target,pivot_row in rest:
                        target[t]=target[t]-f*pivot_row
    outs=[]
    for x in xs:
        done=[]
        for t in range(T):
            d=jnp.sum(jnp.where(lane==row+8*t,x[t],0.0),axis=1,keepdims=True)
            done.append((x[t]*lax.rsqrt(d))[:,NB:2*NB])
        outs.append(jnp.concatenate(done,axis=0))
    return outs
def kern(ns,*refs):
    m=len(ns)
    gram=refs[0:m]; add=refs[m:2*m]; basis=refs[2*m:3*m]
    out_gram=refs[3*m:4*m]; out_rot=refs[4*m:5*m]
    both=refs[5*m:6*m]
    for i,n in enumerate(ns):
        g=0.95*gram[i][...]+0.05*add[i][...]
        out_gram[i][...]=g
        turned=dot(basis[i][...],g,0,0)
        a=dot(turned,turned,1,1)
        npad=both[i].shape[0]
        if npad!=n:
            r=lax.broadcasted_iota(jnp.int32,(npad,2*npad),0); c=lax.broadcasted_iota(jnp.int32,(npad,2*npad),1)
            both[i][...]=((r==c)&(r>=n)).astype(F32)
        both[i][0:n,0:n]=a
        both[i][0:n,npad:npad+n]=turned
    for b in range(max(a.shape[0] for a in both)//NB):
        s=b*NB
        live=[i for i in range(m) if s<both[i].shape[0]]
        inv=base_inverse([both[i][s:s+NB,s:s+NB] for i in live])
        for i,li in zip(live,inv):
            npad=both[i].shape[0]
            e=s+NB
            left=min(e//128*128,npad)
            panel=dot(li,both[i][s:e,left:],1,0)
            both[i][s:e,left:]=panel
            if e<npad:
                both[i][e:,left:]=both[i][e:,left:]-dot(panel[:,e-left:npad-left],panel,0,0)
    for i,n in enumerate(ns):
        npad=both[i].shape[0]
        out_rot[i][...]=both[i][:,npad:].T[0:n,0:n]


def keep_rows(global_rows, total_rows):
    wrapped = jnp.remainder(global_rows, total_rows)
    return ((wrapped + SCENE_ROWS // 2) % SCENE_ROWS != 0).astype(jnp.float32)


def from_behind(block, axis, distance):
    devices = range(lax.axis_size(axis))
    route = [(i - distance, i) for i in devices if i - distance in devices]
    return lax.ppermute(block, axis, route)


def shifted(value, axis, steps):
    count = lax.axis_size(axis)
    pairs = [(source, (source + steps) % count) for source in range(count)]
    return lax.ppermute(value, axis, pairs)


def after(value, *others):
    return lax.optimization_barrier((value,) + others)[0]


def exchange(value):
    return lax.ppermute(value, "stream", [(0, 1), (1, 0)])


def to_all(rows):
    return lax.all_to_all(rows, ("dp", "stream"), 0, 0, tiled=True)


def everyone(value):
    count = lax.axis_size("dp")
    copies = jnp.broadcast_to(value[None], (count,) + value.shape)
    return lax.all_to_all(copies, "dp", 0, 0, tiled=True)


def far_groups():
    far = lax.axis_size("dp") // NEAR
    return [[low + NEAR * high for high in range(far)] for low in range(NEAR)]


def across(value, low):
    count = lax.axis_size("dp")
    return lax.ppermute(value, "dp", [(i, i ^ low) for i in range(count)])


def gather_pieces(value, *first):
    count = lax.axis_size("dp")
    far = count // NEAR
    if far <= NEAR:
        held = [value] + [shifted(value, "dp", NEAR * step) for step in range(1, far)]
        column = jnp.stack(held)
    else:
        copies = jnp.broadcast_to(value[None], (far,) + value.shape)
        column = lax.all_to_all(
            copies, "dp", 0, 0, axis_index_groups=far_groups(), tiled=True
        )
    column = after(column, *first)
    return jnp.stack([column] + [across(column, low) for low in range(1, NEAR)])


def by_low(value):
    low = lax.axis_index("dp") % NEAR
    pairs = value.reshape((2, 2) + value.shape[1:])
    pairs = jnp.where(low % 2 == 1, lax.rev(pairs, (1,)), pairs)
    pairs = jnp.where(low // 2 == 1, lax.rev(pairs, (0,)), pairs)
    return pairs.reshape(value.shape)


def by_index(pieces):
    far = pieces.shape[1]
    pieces = by_low(pieces)
    if far <= NEAR:
        back = lax.rev(pieces, (1,))
        start = (-1 - lax.axis_index("dp") // NEAR) % far
        pieces = lax.dynamic_slice_in_dim(jnp.concatenate([back, back], axis=1), start, far, 1)
    return jnp.swapaxes(pieces, 0, 1).reshape((NEAR * far,) + pieces.shape[2:])


def gather_order():
    count = lax.axis_size("dp")
    far = count // NEAR
    index = lax.axis_index("dp")
    low = (index % NEAR) ^ jnp.arange(NEAR)
    high = (index // NEAR - jnp.arange(far)) % far if far <= NEAR else jnp.arange(far)
    return (high[None, :] * NEAR + low[:, None]).reshape(-1).astype(jnp.int32)


def chip_sums(mine, other):
    return [mine[step] + other[step] for step in range(NEAR)]


def near_sum(sums, *first):
    total = after(sums[0], *first)
    for step in range(1, NEAR):
        total = total + across(sums[step], step)
    return total


def slotted(pair):
    core = lax.axis_index("stream")
    shape = (lax.axis_size("dp") // NEAR, NEAR) + pair.shape[2:]
    parts = (pick(pair, 0, which).reshape(shape) for which in (core, 1 - core))
    return [by_low(jnp.swapaxes(part, 0, 1)) for part in parts]


def far_sum(column):
    moved = lax.all_to_all(column, "dp", 0, 0, axis_index_groups=far_groups(), tiled=True)
    return moved


def in_order(mine, other):
    first = lax.axis_index("stream") == 0
    return jnp.where(first, mine, other), jnp.where(first, other, mine)


def pick(pair, axis, which):
    return lax.dynamic_index_in_dim(pair, which, axis, keepdims=False)


def by_shard(halves):
    count = lax.axis_size("dp")
    short = -halves.shape[1] % count
    if short:
        halves = jnp.pad(halves, ((0, 0), (0, short), (0, 0)))
    return halves.reshape(2, count, halves.shape[1] // count, halves.shape[2])


def fold_rows(rows, count):
    parts = rows.reshape(count, 2, 2, rows.shape[0] // (4 * count), C2)
    return jnp.swapaxes(jnp.concatenate([parts[:, :, 0], parts[:, :, 1]], axis=-1), 0, 1)


def unfold_rows(first, second):
    both = jnp.stack([first, second], axis=1)
    parts = jnp.stack([both[..., :C2], both[..., C2:]], axis=2)
    return parts.reshape(-1, C2)


def arranged(place, pieces, swapped, first=0, past=None):
    past = pieces.shape[2] if past is None else past
    count, rows = pieces.shape[0] * pieces.shape[1], past - first
    if rows % 8 == 0:
        body = functools.partial(arrange, first, rows)
        outs = [(count * rows, 2 * pieces.shape[3])]
        return stage(body, outs, [pieces, swapped], scalars=[place], name="arrange")[0]
    both = in_order(pieces[:, :, first:past], swapped[:, :, first:past])
    both = [by_index(part) for part in both]
    return jnp.concatenate([part.reshape(count * rows, -1) for part in both], axis=1)


def packed_merging(place, pieces, swapped, first, moment):
    count, rows = pieces.shape[0] * pieces.shape[1], pieces.shape[2] - first
    if rows % 8 == 0:
        return stage(
            functools.partial(arrange_merging, first),
            [(2 * C1, 12 * C2)],
            [after(pieces, moment), swapped],
            scalars=[place],
            scratch=[pltpu.VMEM((18 * C1, C2), F32)],
            name="pack",
        )[0]
    both = in_order(pieces[:, :, first:], swapped[:, :, first:])
    both = [by_index(part) for part in both]
    return stage(pack_merging, [(2 * C1, 12 * C2)], [unfold_rows(*both)], name="pack")[0]


def lanes_of(row, width):
    return jnp.pad(row, (0, width - row.shape[0]))[None]


def adam_vector(params, moment, square, gradient):
    momentum = BETA_ONE * moment + (1.0 - BETA_ONE) * gradient
    variance = BETA_TWO * square + (1.0 - BETA_TWO) * gradient * gradient
    direction = (
        momentum / (1.0 - BETA_ONE**STEP) / (jnp.sqrt(variance / (1.0 - BETA_TWO**STEP)) + EPS_ADAM)
    )
    return (params - VECTOR_RATE * (direction + DECAY * params), momentum, variance)


def soap_one(rate, flipped, weight, moment, square, basis, gradient, outs):
    if flipped:
        rotated = product(basis, gradient, 0, 1, HIGHEST)
    else:
        rotated = product(gradient, basis, 1, 0, HIGHEST)
    momentum = BETA_ONE * moment[...] + (1.0 - BETA_ONE) * rotated
    variance = BETA_TWO * square[...] + (1.0 - BETA_TWO) * rotated * rotated
    direction = momentum * (1.0 / (1.0 - BETA_ONE**STEP)) / (
        jnp.sqrt(variance * (1.0 / (1.0 - BETA_TWO**STEP))) + EPS_ADAM
    )
    if flipped:
        turned = product(basis, direction, 1, 0, HIGHEST)
    else:
        turned = product(direction, basis, 1, 1, HIGHEST)
    old = weight[...]
    outs[0][...] = old - rate * (turned + DECAY * old)
    outs[1][...] = momentum
    outs[2][...] = variance


def soap_shards(rates, *refs):
    count = len(rates)
    for i, (rate, flipped) in enumerate(rates):
        group = refs[5 * i : 5 * i + 3]
        outs = refs[5 * count + 3 * i : 5 * count + 3 * i + 3]
        basis, gradient = refs[5 * i + 3][...], refs[5 * i + 4][...]
        soap_one(rate, flipped, *group, basis, gradient, outs)


def close(rates, *refs):
    grams, bases, adds = refs[0:5], refs[5:10], refs[10:15]
    lateral, head = refs[15:18], refs[18:21]
    outs, lateral_outs, head_outs = refs[21:31], refs[31:34], refs[34:37]
    lateral_gram, head_gram = refs[37:39]
    total_lateral, total_heads = adds[2][...], adds[4][...]
    lateral_gram[...] = product(total_lateral, total_lateral, 0, 0, HIGHEST)
    head_gram[...] = product(total_heads, total_heads, 0, 0, HIGHEST)
    sums = (adds[0], adds[1], lateral_gram, adds[3], head_gram)
    kern([C1, C1, C1, C2, CH], *grams, *sums, *bases, *outs, *refs[39:])
    soap_one(rates[0], False, *lateral, bases[2][...], total_lateral, lateral_outs)
    soap_one(rates[1], False, *head, bases[4][...], total_heads, head_outs)


def close_parts(rates, cuts, flags, mine, other, *refs):
    shards = mine.shape[0]
    front = flags[30] == 0.0
    down, upward, lateral, merging, head = adds = refs[-5:]
    half = C1 // 2
    count = C1 // shards
    small = cuts[0] - 2 * count
    for d in range(shards):
        first = jnp.where(front, mine[d], other[d])
        second = jnp.where(front, other[d], mine[d])
        for side in range(2):
            rows, lanes = slice(side * count, (side + 1) * count), slice(side * half, (side + 1) * half)
            down[d * count : (d + 1) * count, lanes] = first[rows]
            upward[d * count : (d + 1) * count, lanes] = second[rows]
        merging[d * small : (d + 1) * small] = second[2 * count : cuts[0], 0:C2]
        rows = cuts[1] - cuts[0]
        lateral[d * rows : (d + 1) * rows, 0:half] = first[cuts[0] : cuts[1]]
        lateral[d * rows : (d + 1) * rows, half:] = second[cuts[0] : cuts[1]]
        rows = cuts[2] - cuts[1]
        head[d * rows : (d + 1) * rows] = first[cuts[1] : cuts[2], 0:CH]
        start = C2 // 2 + d * rows
        head[start : start + rows] = second[cuts[1] : cuts[2], 0:CH]
    close(rates, *refs[:10], *adds, *refs[10:-5])


def partial_gram(shard):
    return jnp.tensordot(shard, shard, axes=((0,), (0,)), precision=HIGHEST)


def assembled(final, other, gram_rows, small):
    final_first, final_second = in_order(final, other)
    shards, half, wide = final.shape[0], C1 // 2, 2 * C2

    def square_of(value):
        count = C1 // shards
        return jnp.concatenate(
            [value[:, k * count : (k + 1) * count].reshape(C1, half) for k in range(2)], axis=1
        )

    gram_down = square_of(final_first)
    gram_upward = square_of(final_second)
    gram_merging = final_second[:, 2 * (C1 // shards) : gram_rows].reshape(-1, wide)[:C2, :C2]
    total_lateral = jnp.concatenate(
        [v[:, gram_rows : gram_rows + small].reshape(C0, half) for v in (final_first, final_second)],
        axis=1,
    )
    total_heads = jnp.concatenate(
        [
            v[:, gram_rows + small :].reshape(-1, wide)[: C2 // 2]
            for v in (final_first, final_second)
        ],
        axis=0,
    )[:, :CH]
    return gram_down, gram_upward, total_lateral, gram_merging, total_heads


def local(
    feats,
    occupied,
    cotangent,
    vector_params,
    vector_moment,
    vector_square,
    down_weight,
    down_moment,
    down_square,
    down_gram,
    down_basis,
    upward_weight,
    upward_moment,
    upward_square,
    upward_gram,
    upward_basis,
    lateral_weight,
    lateral_moment,
    lateral_square,
    lateral_gram,
    lateral_basis,
    merging_weight,
    merging_moment,
    merging_square,
    merging_gram,
    merging_basis,
    heads_weight,
    heads_moment,
    heads_square,
    heads_gram,
    heads_basis,
):
    height, breadth, _ = feats.shape
    half_height, half_breadth = height // 2, breadth // 2
    shards = lax.axis_size("dp")
    cores = lax.axis_size("stream")
    everybody = shards * cores
    total_rows = height * shards
    fine_count = float(height * breadth * everybody)
    coarse_count = fine_count / 4.0
    shard_index, core = lax.axis_index("dp"), lax.axis_index("stream")
    first_row = shard_index * height
    width, half_width = breadth + 6, half_breadth + 3
    rows, half_rows = height + 2, half_height + 2
    flags = jnp.concatenate(
        [
            keep_rows(first_row + 2 * jnp.arange(-1, half_height + 1), total_rows),
            keep_rows(first_row + jnp.arange(-1, height + 3), total_rows),
            (core != 0).astype(F32)[None],
            (core != cores - 1).astype(F32)[None],
        ]
    )
    gains = [vector_params[i * C1 : (i + 1) * C1] for i in range(6)]
    late = 6 * C1
    gain_five, shift_five = vector_params[late : late + C2], vector_params[late + C2 : late + 2 * C2]
    head_bias = vector_params[late + 2 * C2 :]
    wide = 2 * C2
    norm_fine = jnp.stack(
        [jnp.concatenate([gains[2], gains[4]]), jnp.concatenate([gains[3], gains[5]])]
    )
    norm_five = jnp.concatenate([lanes_of(gain_five, wide), lanes_of(shift_five, wide)])

    half = C1 // 2
    weight_halves = [
        lax.dynamic_slice_in_dim(w, core * half, half, 1) for w in (down_weight, upward_weight)
    ]
    quarter = merging_weight.shape[0] // 4
    runs = [
        lax.dynamic_slice_in_dim(merging_weight, (2 * core + i) * quarter, quarter, 0)
        for i in range(2)
    ]
    weight_halves.append(jnp.concatenate(runs, axis=1))
    place = jnp.concatenate([gather_order(), core[None].astype(jnp.int32)])
    occupancy = occupied.astype(F32)[..., None]
    masked = feats * occupancy
    shown = jnp.broadcast_to(occupancy, feats.shape)
    up = shifted(masked[height - RIM_UP :], "dp", 1)
    down = shifted(masked[:RIM_DOWN], "dp", -1)
    edges = jnp.concatenate([up, masked, down], axis=0)
    gathered = gather_pieces(jnp.concatenate(weight_halves, axis=0), up, down)
    left = from_behind(edges[:, breadth - RIM_LEFT :], "stream", 1)
    right = from_behind(edges[:, :RIM_RIGHT], "stream", -1)
    grid, z_four, sums_four = stage(
        pad_lateral,
        [
            (height + RIM_UP + RIM_DOWN, width + LEAD - 2, C0),
            (rows, width, C1),
            (1, 2 * C1),
        ],
        [masked, up, down, left, right, lateral_weight],
        name="pad_lateral",
    )

    swapped = exchange(after(gathered, grid))
    bounds = [0]
    for part in weight_halves:
        bounds.append(bounds[-1] + part.shape[0])
    map_outs = [
        (half_rows, half_width, C1),
        (half_rows, half_width, 9 * C0),
        (everybody, 1, 4 * C1),
    ]
    if bounds[1] % 8 == 0:
        part_shape = (NEAR, shards // NEAR, bounds[1], half)
        z_one, windows, sums_one, down_full = stage(
            coarse_arranged,
            [*map_outs, (9 * C0, C1)],
            [grid, gathered, swapped, sums_four],
            scalars=[flags, place],
            scratch=[pltpu.VMEM(part_shape, F32)] * 2 + [pltpu.SemaphoreType.DMA((2,))],
            name="coarse",
            far_args=(1, 2),
        )
    else:
        down_full = arranged(place, gathered, swapped, 0, bounds[1])
        z_one, windows, sums_one = stage(
            coarse_map, map_outs, [grid, down_full, sums_four], scalars=[flags], name="coarse"
        )
    upward_full = arranged(place, after(gathered, z_one), swapped, bounds[1], bounds[2])
    total_one = after(to_all(sums_one), upward_full)

    z_three, act_one, slope_one, sums_three = stage(
        functools.partial(upsample, coarse_count),
        [
            (2, rows, width, C1 // 2),
            (half_rows, half_width, C1),
            (half_rows, half_width, C1),
            (everybody, 1, 2 * C1),
        ],
        [z_one, total_one, gains[0][None], gains[1][None], upward_full],
        name="upsample",
    )
    packed = packed_merging(place, gathered, swapped, bounds[2], sums_three)
    total_three = after(to_all(sums_three), packed)

    merged, joined, slopes, sums_five = stage(
        functools.partial(merge, fine_count),
        [
            (height, width, wide),
            (rows, width, 2 * C1),
            (rows, width, 2 * C1),
            (everybody, 1, 2 * wide),
        ],
        [z_three, z_four, total_three, total_one, norm_fine, packed],
        scalars=[flags],
        scratch=[
            pltpu.VMEM((rows, width, 12 * C2), F32),
            pltpu.VMEM((2, rows, width, half), F32),
            pltpu.VMEM((rows, width, C1), F32),
            pltpu.VMEM((2 * C1, 12 * C2), F32),
            pltpu.VMEM((rows, width, 2 * C1), F32),
            pltpu.VMEM((rows, width, 2 * C1), F32),
            pltpu.SemaphoreType.DMA((rows // 3 + 1,)),
            pltpu.SemaphoreType.DMA((rows // 3,)),
        ],
        name="merge",
        far_args=(0, 1, 5),
        far_outs=(1, 2),
    )
    total_five = to_all(sums_five)

    heads_padded = jnp.pad(heads_weight, ((0, wide - C2), (0, wide - CH)))
    head_maps, pairs, last_row, first_row_pair, edge, heads_grad, grad_sums_five = stage(
        functools.partial(heads, fine_count),
        [
            (height, CH, breadth),
            (height, width, wide),
            (1, width, wide),
            (1, width, wide),
            (height, 1, wide),
            (wide, wide),
            (everybody, 1, 3 * wide),
        ],
        [merged, total_five, norm_five, heads_padded, lanes_of(head_bias, wide), cotangent],
        scalars=[flags],
        scratch=[pltpu.VMEM((height, width, wide), F32)] * 2,
        name="heads",
    )
    head_maps = jnp.swapaxes(head_maps, 1, 2)
    grads_five = to_all(grad_sums_five)
    above = shifted(last_row, "dp", 1)
    below = shifted(first_row_pair, "dp", -1)
    ends = [jnp.where(core == 0, v[:, 1 + breadth : 2 + breadth], v[:, 2:3]) for v in (above, below)]
    side = exchange(jnp.concatenate([ends[0], edge, ends[1]], axis=0))

    grad_joined, columns, grad_sums = stage(
        functools.partial(merged_gradient, fine_count),
        [
            (height, width, 2 * C1),
            (rows, width, 4 * C2),
            (everybody, 1, 4 * C1),
        ],
        [
            pairs,
            above,
            below,
            side,
            total_five,
            grads_five,
            norm_five,
            packed,
            z_three,
            z_four,
            slopes,
            total_three,
            total_one,
        ],
        scalars=[flags],
        scratch=[
            pltpu.VMEM((2 * C1, 12 * C2), F32),
            pltpu.VMEM((2, rows, width, half), F32),
            pltpu.VMEM((rows, width, C1), F32),
            pltpu.VMEM((rows, width, 2 * C1), F32),
            pltpu.VMEM((height, width, 2 * C1), F32),
            pltpu.VMEM((rows, width, 4 * C2), F32),
            pltpu.SemaphoreType.DMA((3 * height // 4 + 1,)),
            pltpu.SemaphoreType.DMA((height // 4 + 1,)),
        ],
        name="merged_gradient",
        far_args=(7, 8, 9, 10),
        far_outs=(0, 1),
    )
    far = shards // NEAR
    slots = jnp.arange(NEAR, dtype=jnp.int32) ^ (shard_index % NEAR).astype(jnp.int32)
    shifted_rows = pltpu.VMEM((height, width, 4 * C2), F32)
    aligned = quarter % 8 == 0
    if aligned:
        merging_grads = stage(
            merging_product,
            [(NEAR, far, quarter, wide)] * 2,
            [joined, columns],
            scalars=[flags, slots],
            scratch=[pltpu.VMEM((18 * C1, C2), F32), shifted_rows],
            name="merging_product",
        )
    else:
        (merging_grad,) = stage(
            multiply_merging,
            [(18 * C1, C2)],
            [joined, columns],
            scalars=[flags],
            scratch=[shifted_rows],
            name="merging_product",
        )
        merging_grads = slotted(fold_rows(merging_grad, shards))
    merging_grad = merging_grads[0]
    grads_joined = after(to_all(grad_sums), merging_grad)

    quads, grad_one, grad_sums_one = stage(
        functools.partial(coarse_gradient, fine_count, coarse_count),
        [
            (4, half_height, half_width, C1),
            (half_rows, half_width, C1),
            (everybody, 1, 2 * C1),
        ],
        [
            grad_joined,
            z_three,
            total_three,
            grads_joined,
            gains[2][None],
            upward_full,
            z_one,
            total_one,
            slope_one,
        ],
        scratch=[pltpu.VMEM((2, height, width, C1 // 2), F32)],
        name="coarse_gradient",
    )
    late_rows = [4 * C1 // shards, C0 // shards, -(-C2 // (2 * shards))]
    late_args = [
        grad_joined,
        z_four,
        total_one,
        grads_joined,
        gains[4][None],
        grid,
        act_one,
        quads,
        heads_grad,
    ]
    fine_scratch = pltpu.VMEM((height, width, C1), F32)
    if aligned:
        late_grads = stage(
            functools.partial(fine_products, fine_count),
            [(NEAR, far, quarter + sum(late_rows), half)] * 2,
            [*late_args, *merging_grads],
            scalars=[flags, slots],
            scratch=[fine_scratch],
            name="fine_products",
        )
    else:
        late_halves = stage(
            functools.partial(fine_halves, fine_count),
            [(2, 4 * C1, half), (2, C0, half)],
            late_args[:-1],
            scratch=[fine_scratch],
            name="fine_products",
        )
        heads_halves = heads_grad[:C2].reshape(2, C2 // 2, wide)
        blocks = [by_shard(value) for value in (*late_halves, heads_halves)]
        pairs_of = zip(merging_grads, slotted(jnp.concatenate(blocks, axis=2)))
        late_grads = [jnp.concatenate(pair, axis=2) for pair in pairs_of]
    grads_one = after(to_all(grad_sums_one), late_grads[0])
    down_args = [windows, grad_one, z_one, total_one, grads_one, gains[0][None]]
    if aligned:
        down_grads = stage(
            functools.partial(window_product, coarse_count),
            [(NEAR, far, 9 * C0 // shards, half)] * 2,
            down_args,
            scalars=[flags, slots],
            name="window_product",
        )
    else:
        (halves,) = stage(
            functools.partial(window_halves, coarse_count),
            [(2, 9 * C0, half)],
            down_args,
            name="window_product",
        )
        down_grads = slotted(by_shard(halves))
    down_sums = chip_sums(down_grads[0], exchange(down_grads[1]))
    rest_other = exchange(after(late_grads[1], down_grads[0]))
    rest_sums = chip_sums(after(late_grads[0], *down_sums), rest_other)
    down_mine = near_sum(down_sums)
    edge_one = after(grad_one, *rest_sums)
    below = shifted(edge_one[1:2], "dp", -1)
    first_col = jnp.concatenate([edge_one[1 : half_rows - 1, 1:2], below[:, 1:2]], axis=0)
    right = from_behind(first_col, "stream", -1)
    received = far_sum(after(down_mine, *rest_sums))
    rest = near_sum(rest_sums, received, right)
    rest_received = far_sum(rest)
    cuts = [0]
    for count in (quarter, *late_rows):
        cuts.append(cuts[-1] + count)

    sums_back = jnp.sum(grads_one[:, 0], axis=0)
    down_part = jnp.sum(received, axis=0)
    down_shard = jnp.concatenate(in_order(down_part, exchange(down_part)), axis=1)
    gram_one = partial_gram(down_shard)
    part = jnp.sum(after(rest_received, gram_one), axis=0)
    swapped = exchange(part[: cuts[2]])
    first_part, second_part = in_order(part[: cuts[2]], swapped)
    merging_shard = unfold_rows(first_part[None, : cuts[1]], second_part[None, : cuts[1]])
    upward_shard = jnp.concatenate([first_part[cuts[1] :], second_part[cuts[1] :]], axis=1)

    def lane_rows(gram):
        count = gram.shape[0] // shards
        return jnp.concatenate(
            [
                gram[:, k * half : (k + 1) * half].reshape(shards, count, half)
                for k in range(C1 // half)
            ],
            axis=1,
        )

    shard_groups = [
        (down_weight, down_moment, down_square, down_basis, down_shard),
        (upward_weight, upward_moment, upward_square, upward_basis, upward_shard),
        (merging_weight.T, merging_moment.T, merging_square.T, merging_basis, merging_shard),
    ]
    stepped = stage(
        functools.partial(
            soap_shards,
            (
                (1.0 / math.sqrt(9 * C0), False),
                (1.0 / math.sqrt(C1), False),
                (1.0 / math.sqrt(18 * C1), True),
            ),
        ),
        [group[0].shape for group in shard_groups for _ in range(3)],
        [array for group in shard_groups for array in group],
        name="soap",
    )
    down_renewed, down_momentum, down_variance = stepped[:3]
    upward_renewed, upward_momentum, upward_variance = stepped[3:6]
    merging_renewed, merging_momentum, merging_variance = (value.T for value in stepped[6:])
    gram_two = jnp.pad(partial_gram(merging_shard), ((0, -C2 % shards), (0, wide - C2)))
    gram_two = gram_two.reshape(shards, -1, wide)
    firsts = jnp.pad(lane_rows(gram_one), ((0, 0), (0, gram_two.shape[1]), (0, 0)))
    seconds = jnp.concatenate([lane_rows(partial_gram(upward_shard)), gram_two], axis=1)
    parts = jnp.where(core == 0, firsts, seconds)
    gram_parts = after(lax.all_to_all(parts, "dp", 0, 0, tiled=True), *stepped)
    gram_sum = jnp.sum(gram_parts, axis=0)
    (feats_grad,) = stage(
        functools.partial(input_gradient, fine_count, coarse_count),
        [(breadth * height, C0)],
        [
            grad_one,
            below,
            right,
            z_one,
            total_one,
            after(grads_one, gram_sum),
            gains[0][None],
            down_full,
            grad_joined,
            z_four,
            grads_joined,
            gains[4][None],
            lateral_weight,
            shown,
        ],
        scalars=[flags],
        scratch=[
            pltpu.VMEM((half_rows - 1, half_width, 9 * C0), F32),
            pltpu.VMEM((height, width, C0), F32),
            fine_scratch,
        ],
        name="input_gradient",
    )
    feats_grad = jnp.swapaxes(feats_grad.reshape(breadth, height, C0), 0, 1)
    gram_rows = gram_sum.shape[0]
    final = everyone(jnp.concatenate([gram_sum, part[cuts[2] :]], axis=0))
    final = after(final, feats_grad)
    final_other = exchange(final)
    grams = (down_gram, upward_gram, lateral_gram, merging_gram, heads_gram)
    bases = (down_basis, upward_basis, lateral_basis, merging_basis, heads_basis)
    orders = [C1, C1, C1, C2, CH]
    padded = [-(-n // NB) * NB for n in orders]
    close_args = [
        *grams,
        *bases,
        lateral_weight,
        lateral_moment,
        lateral_square,
        heads_weight,
        heads_moment,
        heads_square,
    ]
    close_outs = [(n, n) for n in orders] * 2 + [(C0, C1)] * 3 + [(C2, CH)] * 3
    close_scratch = [pltpu.VMEM((n, n), F32) for n in (C1, CH)]
    close_scratch += [pltpu.VMEM((n, 2 * n), F32) for n in padded]
    rates = (1.0 / math.sqrt(C0), 1.0 / math.sqrt(C2))
    add_shapes = [(C1, C1), (C1, C1), (C0, C1), (C2, C2), (C2, CH)]
    if aligned:
        ends = (gram_rows, gram_rows + late_rows[1], gram_rows + sum(late_rows[1:]))
        closed = stage(
            functools.partial(close_parts, rates, ends),
            close_outs,
            [final, final_other, *close_args],
            scalars=[flags],
            scratch=close_scratch + [pltpu.VMEM(shape, F32) for shape in add_shapes],
            name="close",
        )
    else:
        adds = assembled(final, final_other, gram_rows, late_rows[1])
        closed = stage(
            functools.partial(close, rates),
            close_outs,
            [*close_args[:10], *adds, *close_args[10:]],
            scratch=close_scratch,
            name="close",
        )
    down_gramian, upward_gramian, lateral_gramian, merging_gramian, heads_gramian = closed[:5]
    down_rotation, upward_rotation, lateral_rotation, merging_rotation, heads_rotation = closed[5:10]
    lateral_renewed, lateral_momentum, lateral_variance = closed[10:13]
    heads_renewed, heads_momentum, heads_variance = closed[13:]

    sums_fine = jnp.sum(grads_joined[:, 0], axis=0)
    sums_late = jnp.sum(grads_five[:, 0], axis=0)
    grad_vector = jnp.concatenate(
        [
            sums_back,
            sums_fine[:C1],
            sums_fine[2 * C1 : 3 * C1],
            sums_fine[C1 : 2 * C1],
            sums_fine[3 * C1 :],
            sums_late[:C2],
            sums_late[wide : wide + C2],
            sums_late[2 * wide : 2 * wide + CH],
        ]
    )
    vector_renewed, vector_momentum, vector_variance = adam_vector(
        vector_params, vector_moment, vector_square, grad_vector
    )
    return (
        head_maps,
        feats_grad,
        vector_renewed,
        vector_momentum,
        vector_variance,
        down_renewed,
        down_momentum,
        down_variance,
        down_gramian,
        down_rotation,
        upward_renewed,
        upward_momentum,
        upward_variance,
        upward_gramian,
        upward_rotation,
        lateral_renewed,
        lateral_momentum,
        lateral_variance,
        lateral_gramian,
        lateral_rotation,
        merging_renewed,
        merging_momentum,
        merging_variance,
        merging_gramian,
        merging_rotation,
        heads_renewed,
        heads_momentum,
        heads_variance,
        heads_gramian,
        heads_rotation,
    )


def solution(mesh):
    in_specs = (
        P("dp", "stream", None),
        P("dp", "stream"),
        P("dp", "stream", None),
        P(),
        P(),
        P(),
        P("dp", None),
        P("dp", None),
        P("dp", None),
        P(),
        P(),
        P("dp", None),
        P("dp", None),
        P("dp", None),
        P(),
        P(),
        P(),
        P(),
        P(),
        P(),
        P(),
        P("dp", None),
        P("dp", None),
        P("dp", None),
        P(),
        P(),
        P(),
        P(),
        P(),
        P(),
        P(),
    )
    out_specs = (
        P("dp", "stream", None),
        P("dp", "stream", None),
        P(),
        P(),
        P(),
        P("dp", None),
        P("dp", None),
        P("dp", None),
        P(),
        P(),
        P("dp", None),
        P("dp", None),
        P("dp", None),
        P(),
        P(),
        P(),
        P(),
        P(),
        P(),
        P(),
        P("dp", None),
        P("dp", None),
        P("dp", None),
        P(),
        P(),
        P(),
        P(),
        P(),
        P(),
        P(),
    )
    return jax.shard_map(local, mesh=mesh, in_specs=in_specs, out_specs=out_specs, check_vma=False)
```

```python
import functools
import math

import jax
import jax.numpy as jnp
from jax import lax
from jax.experimental import pallas as pl
from jax.experimental.pallas import tpu as pltpu
from jax.sharding import PartitionSpec as P

C0 = 128
C1 = 256
C2 = 64
CH = 70
SCENE_ROWS = 180
STEP = 10


EPS_NORM = 1e-05
BETA_ONE = 0.9
BETA_TWO = 0.95
BETA_GRAM = 0.95
EPS_ADAM = 1e-08
DECAY = 0.01
VECTOR_RATE = 0.1
HIGHEST = lax.Precision.HIGHEST


F32 = jnp.float32
HIGH = lax.Precision.HIGH
RIM_UP, RIM_DOWN, RIM_LEFT, RIM_RIGHT = 3, 2, 3, 2
LEAD = 10
NEAR = 4


def product(left, right, over_left, over_right, precision=HIGH):
    dims = (((over_left,), (over_right,)), ((), ()))
    return lax.dot_general(
        left, right, dims, precision=precision, preferred_element_type=F32
    )


def stage(body, outs, args, scalars=(), scratch=(), name=None, far_args=(), far_outs=()):
    vmem = pl.BlockSpec(memory_space=pltpu.VMEM)
    smem = pl.BlockSpec(memory_space=pltpu.SMEM)
    away = pl.BlockSpec(memory_space=pl.ANY)
    shapes = [jax.ShapeDtypeStruct(shape, F32) for shape in outs]
    return pl.pallas_call(
        body,
        out_shape=shapes,
        in_specs=[smem] * len(scalars)
        + [away if i in far_args else vmem for i in range(len(args))],
        out_specs=[away if i in far_outs else vmem for i in range(len(shapes))],
        scratch_shapes=list(scratch),
        compiler_params=pltpu.CompilerParams(vmem_limit_bytes=56 << 20),
        name=name,
    )(*scalars, *args)


def channel_sums(ref):
    return jnp.sum(ref[...], axis=0)


def spread_of(total, pixels):
    half = total.shape[1] // 2
    centre = total[:, :half] * (1.0 / pixels)
    second = total[:, half:] * (1.0 / pixels)
    return centre, lax.rsqrt(second - centre * centre + EPS_NORM)


def cols_between(count, lanes, first, past):
    col = lax.broadcasted_iota(jnp.int32, (count, lanes), 0)
    return (col >= first) & (col < past)


def row_total(value):
    return jnp.sum(value, axis=0, keepdims=True)


def send(ref, row):
    ref[...] = jnp.broadcast_to(row[None], ref.shape)


def pad_lateral(masked, up, down, left, right, lateral, grid, z_four, sums):
    height, breadth, channels = masked.shape
    grid[...] = jnp.zeros(grid.shape, F32)
    inner = slice(LEAD, LEAD + breadth)
    grid[0:RIM_UP, inner] = up[...]
    grid[RIM_UP : RIM_UP + height, inner] = masked[...]
    grid[RIM_UP + height :, inner] = down[...]
    grid[:, LEAD - RIM_LEFT : LEAD] = left[...]
    grid[:, LEAD + breadth : LEAD + breadth + RIM_RIGHT] = right[...]
    width = z_four.shape[1]
    own = cols_between(width, C1, 2, 2 + breadth)
    total = jnp.zeros((1, C1), F32)
    square = jnp.zeros((1, C1), F32)
    tile = 6
    for first in range(0, height + 2, tile):
        block = grid[2 + first : 2 + first + tile, LEAD - 2 : LEAD - 2 + width]
        made = product(block.reshape(tile * width, channels), lateral[...], 1, 0)
        made = made.reshape(tile, width, C1)
        z_four[first : first + tile] = made
        for row in range(tile):
            if 1 <= first + row <= height:
                kept = jnp.where(own, made[row], 0.0)
                total = total + row_total(kept)
                square = square + row_total(kept * kept)
    sums[...] = jnp.concatenate([total, square], axis=1)


def coarse_arranged(
    flags, place, grid, pieces_far, swapped_far, sums_four, z_one, windows, sums, weight, *scratch
):
    pieces, swapped, arrived = scratch
    rows = pieces.shape[2]
    copies = [
        start_copy(pieces_far.at[:, :, pl.ds(0, rows)], pieces, arrived.at[0]),
        start_copy(swapped_far.at[:, :, pl.ds(0, rows)], swapped, arrived.at[1]),
    ]
    build_windows(flags, grid, windows, z_one.shape[1])
    for copy in copies:
        copy.wait()
    arrange(0, rows, place, pieces, swapped, weight)
    multiply_map(weight, sums_four, z_one, windows, sums)


def coarse_map(flags, grid, weight, sums_four, z_one, windows, sums):
    build_windows(flags, grid, windows, z_one.shape[1])
    multiply_map(weight, sums_four, z_one, windows, sums)


def build_windows(flags, grid, windows, width):
    for i in range(windows.shape[0]):
        for a in range(3):
            for b in range(3):
                piece = grid[2 * i + a, pl.ds(LEAD - 3 + b, width, 2), :]
                if a == 0:
                    piece = piece * flags[i]
                tap = 3 * a + b
                windows[i, :, tap * C0 : (tap + 1) * C0] = piece


def multiply_map(weight, sums_four, z_one, windows, sums):
    rows, width = z_one.shape[0], z_one.shape[1]
    half_breadth = width - 3
    made = product(windows[...].reshape(rows * width, 9 * C0), weight[...], 1, 0)
    z_one[...] = made.reshape(rows, width, C1)
    own = cols_between(width, C1, 1, 1 + half_breadth)
    total = jnp.zeros((1, C1), F32)
    square = jnp.zeros((1, C1), F32)
    for i in range(1, rows - 1):
        kept = jnp.where(own, z_one[i], 0.0)
        total = total + row_total(kept)
        square = square + row_total(kept * kept)
    send(sums, jnp.concatenate([total, square, sums_four[...]], axis=1))


def window_halves(
    coarse_pixels, windows, grad_one, z_one, total_one, grads_one, gain_one, halves
):
    args = (windows, grad_one, z_one, total_one, grads_one, gain_one)
    made = multiply_windows(coarse_pixels, *args)
    halves[0] = made[:, : C1 // 2]
    halves[1] = made[:, C1 // 2 :]


def window_product(
    coarse_pixels, flags, slots, windows, grad_one, z_one, total_one, grads_one, gain_one, mine, other
):
    args = (windows, grad_one, z_one, total_one, grads_one, gain_one)
    made = multiply_windows(coarse_pixels, *args)
    shards = mine.shape[0] * mine.shape[1]
    by_slot(made, mine, other, slots, flags[30] == 0.0, shards, 0)


def multiply_windows(coarse_pixels, windows, grad_one, z_one, total_one, grads_one, gain_one):
    rows, width, depth = windows.shape
    centre, spread = spread_of(channel_sums(total_one)[:, : 2 * C1], coarse_pixels)
    gained = channel_sums(grads_one)
    scale = gain_one[...] * spread
    mean_gain = gained[:, :C1] * (1.0 / coarse_pixels)
    mean_shift = gained[:, C1:] * (1.0 / coarse_pixels)
    own = cols_between(width, C1, 1, width - 2)
    parts = []
    for i in range(1, rows - 1):
        normed = (z_one[i] - centre) * spread
        value = scale * (grad_one[i] - mean_shift - normed * mean_gain)
        parts.append(jnp.where(own, value, 0.0))
    inside = windows[1 : rows - 1].reshape((rows - 2) * width, depth)
    return product(inside, jnp.concatenate(parts, axis=0), 0, 0)


def upsample(pixels, z_one, total_one, gain, shift, weight, z_three, act_one, slope_one, sums):
    rows, width = z_one.shape[0], z_one.shape[1]
    half_breadth = width - 3
    centre, spread = spread_of(channel_sums(total_one)[:, : 2 * C1], pixels)
    for i in range(rows):
        hidden = (z_one[i] - centre) * spread * gain[...] + shift[...]
        sigmoid = lax.logistic(hidden)
        act_one[i] = hidden * sigmoid
        slope_one[i] = sigmoid * (1.0 + hidden * (1.0 - sigmoid))
    active = act_one[...].reshape(rows * width, C1)
    own = cols_between(width, C1, 1, 1 + half_breadth)
    total = jnp.zeros((1, C1), F32)
    square = jnp.zeros((1, C1), F32)
    half = C1 // 2
    for a in range(2):
        for b in range(2):
            tap = 2 * a + b
            made = product(active, weight[tap * C1 : (tap + 1) * C1], 1, 0)
            for i in range(rows):
                part = made[i * width : (i + 1) * width]
                place = 2 * i + a - 1
                if 0 <= place < 2 * rows - 2:
                    for k in range(2):
                        z_three[k, place, pl.ds(b, width, 2), :] = part[:, k * half : (k + 1) * half]
                if 1 <= i < rows - 1:
                    kept = jnp.where(own, part, 0.0)
                    total = total + row_total(kept)
                    square = square + row_total(kept * kept)
    send(sums, jnp.concatenate([total, square], axis=1))


def pack_merging(weight, packed):
    for a in range(3):
        pieces = [
            weight[(3 * a + b) * 2 * C1 : (3 * a + b + 1) * 2 * C1] for b in range(3)
        ]
        pieces.append(jnp.zeros((2 * C1, C2), F32))
        packed[:, a * 4 * C2 : (a + 1) * 4 * C2] = jnp.concatenate(pieces, axis=1)


def arrange(first, rows, place, pieces, swapped, out):
    near, far, _, lanes = pieces.shape
    front = place[near * far] == 0
    for low in range(near):
        for high in range(far):
            at = pl.ds(pl.multiple_of(place[low * far + high] * rows, 8), rows)
            mine = pieces[low, high, first : first + rows]
            other = swapped[low, high, first : first + rows]
            out[at, 0:lanes] = jnp.where(front, mine, other)
            out[at, lanes:] = jnp.where(front, other, mine)


def arrange_merging(first, place, pieces, swapped, packed, weight):
    near, far, last, _ = pieces.shape
    rows = last - first
    front = place[near * far] == 0
    for low in range(near):
        for high in range(far):
            mine, other = pieces[low, high, first:], swapped[low, high, first:]
            values = (jnp.where(front, mine, other), jnp.where(front, other, mine))
            for core in range(2):
                for side in range(2):
                    start = (place[low * far + high] * 4 + 2 * core + side) * rows
                    at = pl.ds(pl.multiple_of(start, 8), rows)
                    weight[at, :] = values[core][:, side * C2 : (side + 1) * C2]
    pack_merging(weight, packed)


def start_copy(source, target, semaphore):
    copy = pltpu.make_async_copy(source, target, semaphore)
    copy.start()
    return copy


def merge(
    pixels,
    flags,
    z_three_far,
    z_four_far,
    total_three,
    total_one,
    norms,
    packed_far,
    merged,
    joined_far,
    slopes_far,
    sums,
    taps,
    z_three,
    z_four,
    packed,
    joined,
    slopes,
    arrived,
    left,
):
    rows, width = z_four.shape[0], z_four.shape[1]
    height = rows - 2
    breadth = width - 6
    tile = 6
    firsts = list(range(0, rows, tile))
    coming = []
    for t, r in enumerate(firsts):
        part = pl.ds(r, tile)
        coming.append(
            [
                start_copy(z_three_far.at[:, part], z_three.at[:, part], arrived.at[2 * t]),
                start_copy(z_four_far.at[part], z_four.at[part], arrived.at[2 * t + 1]),
            ]
        )
    weight_copy = start_copy(packed_far, packed, arrived.at[2 * len(firsts)])
    sum_three = channel_sums(total_three)
    sum_four = channel_sums(total_one)[:, 2 * C1 :]
    centre_three, spread_three = spread_of(sum_three, pixels)
    centre_four, spread_four = spread_of(sum_four, pixels)
    centre = jnp.concatenate([centre_three, centre_four], axis=1)
    spread = jnp.concatenate([spread_three, spread_four], axis=1)
    scale = spread * norms[0:1]
    offset = norms[1:2] - centre * scale
    col = lax.broadcasted_iota(jnp.int32, (width, 2 * C1), 0)
    dead = ((col == 1) & (flags[30] == 0.0)) | ((col == 2 + breadth) & (flags[31] == 0.0))

    def activate(r, carry):
        raw = jnp.concatenate([z_three[0, r], z_three[1, r], z_four[r]], axis=1)
        hidden = raw * scale + offset
        sigmoid = lax.logistic(hidden)
        joined[r] = jnp.where(dead, 0.0, hidden * sigmoid)
        slopes[r] = sigmoid * (1.0 + hidden * (1.0 - sigmoid))
        return carry

    going = []
    for t, r in enumerate(firsts):
        for copy in coming[t]:
            copy.wait()
        lax.fori_loop(r, r + tile, activate, 0)
        part = pl.ds(r, tile)
        going.append(start_copy(joined.at[part], joined_far.at[part], left.at[2 * t]))
        going.append(start_copy(slopes.at[part], slopes_far.at[part], left.at[2 * t + 1]))
    weight_copy.wait()

    long = rows // 2
    for r in range(0, rows, long):
        block = joined[r : r + long].reshape(long * width, 2 * C1)
        taps[r : r + long] = product(block, packed[...], 1, 0).reshape(long, width, 12 * C2)
    own = cols_between(width, 2 * C2, 2, 2 + breadth)
    lane = lax.broadcasted_iota(jnp.int32, (width, 2 * C2), 1)
    total = jnp.zeros((1, 2 * C2), F32)
    square = jnp.zeros((1, 2 * C2), F32)
    for row in range(height):
        r = row + 1
        both = (
            taps[r - 1, :, 0 : 4 * C2] * flags[10 + r]
            + taps[r, :, 4 * C2 : 8 * C2]
            + taps[r + 1, :, 8 * C2 : 12 * C2] * flags[11 + r]
        )
        first, second = both[:, : 2 * C2], both[:, 2 * C2 :]
        out = (
            pltpu.roll(first, 1, 0)
            + pltpu.roll(first, C2, 1)
            + pltpu.roll(second, width - 1, 0)
        )
        out = jnp.where(own & (lane < C2), out, 0.0)
        merged[row] = out
        total = total + row_total(out)
        square = square + row_total(out * out)
    send(sums, jnp.concatenate([total, square], axis=1))
    for copy in going:
        copy.wait()


def heads(
    pixels,
    flags,
    merged,
    total_five,
    norms,
    weight,
    bias,
    cotangent,
    maps,
    pairs,
    last_row,
    first_row,
    edge,
    weight_grad,
    sums,
    active,
    upstream,
):
    height, width, _ = merged.shape
    breadth = width - 6
    centre, spread = spread_of(channel_sums(total_five)[:, : 4 * C2], pixels)
    own = cols_between(width, 2 * C2, 2, 2 + breadth)
    upstream[...] = jnp.zeros(upstream.shape, F32)
    for r in range(height):
        upstream[r, 2 : 2 + breadth, 0:CH] = cotangent[r]
    flat = upstream[...].reshape(height * width, 2 * C2)
    grad = product(flat, weight[...], 1, 1).reshape(height, width, 2 * C2)
    grad_gain = jnp.zeros((1, 2 * C2), F32)
    grad_shift = jnp.zeros((1, 2 * C2), F32)
    for r in range(height):
        normed = jnp.where(own, (merged[r] - centre) * spread, 0.0)
        hidden = norms[0:1] * normed + norms[1:2]
        sigmoid = lax.logistic(hidden)
        active[r] = hidden * sigmoid
        grad_hidden = grad[r] * sigmoid * (1.0 + hidden * (1.0 - sigmoid))
        pair = grad_hidden + pltpu.roll(normed, C2, 1)
        pairs[r] = pair
        edge[r] = jnp.where(flags[30] == 0.0, pair[1 + breadth : 2 + breadth], pair[2:3])
        if r == 0:
            first_row[0] = pair
        if r == height - 1:
            last_row[0] = pair
        grad_gain = grad_gain + row_total(grad_hidden * normed)
        grad_shift = grad_shift + row_total(grad_hidden)
    send(sums, jnp.concatenate([grad_gain, grad_shift, row_total(flat)], axis=1))
    act = active[...].reshape(height * width, 2 * C2)
    made = product(act, weight[...], 1, 0).reshape(height, width, 2 * C2) + bias[...]
    for r in range(height):
        maps[r] = pltpu.roll(made[r], width - 2, 0).T[0:CH, 0:breadth]
    weight_grad[...] = product(act, flat, 0, 0)


def merged_gradient(
    pixels,
    flags,
    pairs,
    above,
    below,
    side,
    total_five,
    grads_five,
    norm_five,
    packed_far,
    z_three_far,
    z_four_far,
    slopes_far,
    total_three,
    total_one,
    grad_far,
    columns_far,
    sums,
    packed,
    z_three,
    z_four,
    slopes,
    grad_joined,
    columns,
    arrived,
    left_sems,
):
    height, width, _ = pairs.shape
    breadth = width - 6
    lanes = 2 * C2
    tile = 4
    weight_copy = start_copy(packed_far, packed, arrived.at[0])
    coming = []
    for t in range(height // tile):
        part = pl.ds(t * tile + 1, tile)
        coming.append(
            [
                start_copy(slopes_far.at[part], slopes.at[part], arrived.at[3 * t + 1]),
                start_copy(z_three_far.at[:, part], z_three.at[:, part], arrived.at[3 * t + 2]),
                start_copy(z_four_far.at[part], z_four.at[part], arrived.at[3 * t + 3]),
            ]
        )
    _, spread = spread_of(channel_sums(total_five)[:, : 4 * C2], pixels)
    gained = channel_sums(grads_five)
    scale = norm_five[0:1] * spread
    mean_gain = gained[:, :lanes] * (1.0 / pixels)
    mean_shift = gained[:, lanes : 2 * lanes] * (1.0 / pixels)
    col = lax.broadcasted_iota(jnp.int32, (width, lanes), 0)
    lane = lax.broadcasted_iota(jnp.int32, (width, lanes), 1)
    live = (
        ((col >= 2) & (col < 2 + breadth))
        | ((col == 1) & (flags[30] != 0.0))
        | ((col == 2 + breadth) & (flags[31] != 0.0))
    ) & (lane < C2)
    target = jnp.where(flags[30] == 0.0, 2 + breadth, 1)
    for r in range(height + 2):
        if r == 0:
            raw = above[0]
        elif r == height + 1:
            raw = below[0]
        else:
            raw = pairs[r - 1]
        raw = jnp.where(col == target, side[r], raw)
        normed = pltpu.roll(raw, C2, 1)
        value = jnp.where(live, scale * (raw - mean_shift - normed * mean_gain), 0.0)
        columns[r, :, 0:lanes] = pltpu.roll(value, width - 1, 0) + pltpu.roll(value, C2, 1)
        columns[r, :, lanes:] = pltpu.roll(value, 1, 0)
    going = [start_copy(columns, columns_far, left_sems.at[0])]
    centre_three, spread_three = spread_of(channel_sums(total_three), pixels)
    centre_four, spread_four = spread_of(channel_sums(total_one)[:, 2 * C1 :], pixels)
    centre = jnp.concatenate([centre_three, centre_four], axis=1)
    spread = jnp.concatenate([spread_three, spread_four], axis=1)
    own = cols_between(width, 2 * C1, 2, 2 + breadth)

    def gradient(t, carry):
        r = t * tile
        block = jnp.zeros((tile * width, 2 * C1), F32)
        for a in range(3):
            rows = []
            for k in range(tile):
                source = r + k + 2 - a
                row = columns[source]
                if a == 0:
                    row = row * flags[10 + source]
                if a == 2:
                    row = row * flags[11 + source]
                rows.append(row)
            block = block + product(
                jnp.concatenate(rows, axis=0), packed[:, a * 4 * C2 : (a + 1) * 4 * C2], 1, 1
            )
        gain_sum, shift_sum = carry
        for k in range(tile):
            grad = jnp.where(own, block[k * width : (k + 1) * width] * slopes[r + k + 1], 0.0)
            grad_joined[r + k] = grad
            raw = jnp.concatenate(
                [z_three[0, r + k + 1], z_three[1, r + k + 1], z_four[r + k + 1]], axis=1
            )
            normed = (raw - centre) * spread
            gain_sum = gain_sum + row_total(grad * normed)
            shift_sum = shift_sum + row_total(grad)
        return gain_sum, shift_sum

    empty = jnp.zeros((1, 2 * C1), F32)
    carry = (empty, empty)
    weight_copy.wait()
    for t in range(height // tile):
        for copy in coming[t]:
            copy.wait()
        carry = gradient(t, carry)
        part = pl.ds(t * tile, tile)
        going.append(start_copy(grad_joined.at[part], grad_far.at[part], left_sems.at[t + 1]))
    send(sums, jnp.concatenate(carry, axis=1))
    for copy in going:
        copy.wait()


def by_slot(value, mine, other, slots, front, shards, first):
    rows = value.shape[0] // shards
    half = value.shape[1] // 2
    for shard in range(shards):
        piece = value[shard * rows : (shard + 1) * rows]
        low, high = piece[:, :half], piece[:, half:]
        place = slots[shard % NEAR], shard // NEAR, slice(first, first + rows)
        mine[place] = jnp.where(front, low, high)
        other[place] = jnp.where(front, high, low)


def merging_product(flags, slots, joined, columns, mine, other, grads, shifted_rows):
    multiply_merging(flags, joined, columns, grads, shifted_rows)
    front = flags[30] == 0.0
    near, far, rows, _ = mine.shape
    for shard in range(near * far):
        start = 4 * rows * shard
        runs = [grads[start + i * rows : start + (i + 1) * rows] for i in range(4)]
        first = jnp.concatenate(runs[:2], axis=1)
        second = jnp.concatenate(runs[2:], axis=1)
        place = slots[shard % near], shard // near
        mine[place] = jnp.where(front, first, second)
        other[place] = jnp.where(front, second, first)


def multiply_merging(flags, joined, columns, grads, shifted_rows):
    rows, width, _ = joined.shape
    height = rows - 2
    inside = joined[1 : rows - 1].reshape(height * width, 2 * C1)
    own = cols_between(width, 4 * C2, 2, width - 4)
    for a in range(3):
        for r in range(height):
            source = r + 2 - a
            row = columns[source]
            if a == 0:
                row = row * flags[10 + source]
            if a == 2:
                row = row * flags[11 + source]
            shifted_rows[r] = jnp.where(own, row, 0.0)
        made = product(inside, shifted_rows[...].reshape(height * width, 4 * C2), 0, 0)
        for b in range(3):
            grads[(3 * a + b) * 2 * C1 : (3 * a + b + 1) * 2 * C1] = made[:, b * C2 : (b + 1) * C2]


def coarse_gradient(
    pixels,
    coarse_pixels,
    grad_joined,
    z_three,
    total_three,
    grads_joined,
    gain_three,
    weight,
    z_one,
    total_one,
    slope_one,
    quads,
    grad_one,
    top,
    side,
    sums,
    fine,
):
    height, width = grad_joined.shape[0], grad_joined.shape[1]
    rows, half_width = z_one.shape[0], z_one.shape[1]
    half = C1 // 2
    centre, spread = spread_of(channel_sums(total_three), pixels)
    gained = channel_sums(grads_joined)
    scale = gain_three[...] * spread
    mean_gain = gained[:, :C1] * (1.0 / pixels)
    mean_shift = gained[:, 2 * C1 : 3 * C1] * (1.0 / pixels)
    own = cols_between(width, C1, 2, width - 4)

    def fill(r, carry):
        raw = jnp.concatenate([z_three[0, r + 1], z_three[1, r + 1]], axis=1)
        normed = (raw - centre) * spread
        value = scale * (grad_joined[r, :, 0:C1] - mean_shift - normed * mean_gain)
        value = jnp.where(own, value, 0.0)
        fine[0, r] = value[:, :half]
        fine[1, r] = value[:, half:]
        return carry

    lax.fori_loop(0, height, fill, 0)
    grad = jnp.zeros(((rows - 2) * half_width, C1), F32)
    for a in range(2):
        for b in range(2):
            tap = 2 * a + b
            for i in range(rows - 2):
                for k in range(2):
                    quads[tap, i, :, k * half : (k + 1) * half] = fine[
                        k, 2 * i + a, pl.ds(b, half_width, 2), :
                    ]
            flat = quads[tap].reshape((rows - 2) * half_width, C1)
            grad = grad + product(flat, weight[tap * C1 : (tap + 1) * C1], 1, 1)
    centre, spread = spread_of(channel_sums(total_one)[:, : 2 * C1], coarse_pixels)
    own = cols_between(half_width, C1, 1, half_width - 2)
    gain_sum = jnp.zeros((1, C1), F32)
    shift_sum = jnp.zeros((1, C1), F32)
    grad_one[0] = jnp.zeros((half_width, C1), F32)
    grad_one[rows - 1] = jnp.zeros((half_width, C1), F32)
    for i in range(1, rows - 1):
        value = grad[(i - 1) * half_width : i * half_width] * slope_one[i]
        value = jnp.where(own, value, 0.0)
        grad_one[i] = value
        side[i - 1] = value[1:2]
        if i == 1:
            top[0] = value
        gain_sum = gain_sum + row_total(value * ((z_one[i] - centre) * spread))
        shift_sum = shift_sum + row_total(value)
    send(sums, jnp.concatenate([gain_sum, shift_sum], axis=1))


def lateral_gradient(pixels, grad_joined, z_four, total_one, grads_joined, gain_four, fine):
    height, width = grad_joined.shape[0], grad_joined.shape[1]
    centre, spread = spread_of(channel_sums(total_one)[:, 2 * C1 :], pixels)
    gained = channel_sums(grads_joined)
    scale = gain_four[...] * spread
    mean_gain = gained[:, C1 : 2 * C1] * (1.0 / pixels)
    mean_shift = gained[:, 3 * C1 :] * (1.0 / pixels)
    own = cols_between(width, C1, 2, width - 4)

    def fill(r, carry):
        normed = (z_four[r + 1] - centre) * spread
        value = scale * (grad_joined[r, :, C1:] - mean_shift - normed * mean_gain)
        fine[r] = jnp.where(own, value, 0.0)
        return carry

    lax.fori_loop(0, height, fill, 0)


def fine_halves(
    pixels,
    grad_joined,
    z_four,
    total_one,
    grads_joined,
    gain_four,
    grid,
    act_one,
    quads,
    upward_halves,
    lateral_halves,
    fine,
):
    height, width = grad_joined.shape[0], grad_joined.shape[1]
    rows, half_width = act_one.shape[0], act_one.shape[1]
    half = C1 // 2
    lateral_gradient(pixels, grad_joined, z_four, total_one, grads_joined, gain_four, fine)
    flat = fine[...].reshape(height * width, C1)
    source = grid[RIM_UP : RIM_UP + height, LEAD - 2 : LEAD - 2 + width]
    made = product(source.reshape(height * width, C0), flat, 0, 0)
    lateral_halves[0] = made[:, :half]
    lateral_halves[1] = made[:, half:]
    inside = act_one[1 : rows - 1].reshape((rows - 2) * half_width, C1)
    for tap in range(4):
        made = product(inside, quads[tap].reshape((rows - 2) * half_width, C1), 0, 0)
        for side in range(2):
            upward_halves[side, tap * C1 : (tap + 1) * C1] = made[
                :, side * half : (side + 1) * half
            ]


def fine_products(
    pixels,
    flags,
    slots,
    grad_joined,
    z_four,
    total_one,
    grads_joined,
    gain_four,
    grid,
    act_one,
    quads,
    heads_grad,
    merging_mine,
    merging_other,
    mine,
    other,
    fine,
):
    height, width = grad_joined.shape[0], grad_joined.shape[1]
    rows, half_width = act_one.shape[0], act_one.shape[1]
    shards = mine.shape[0] * mine.shape[1]
    front = flags[30] == 0.0
    lateral_gradient(pixels, grad_joined, z_four, total_one, grads_joined, gain_four, fine)
    inside = act_one[1 : rows - 1].reshape((rows - 2) * half_width, C1)
    parts = [
        product(inside, quads[tap].reshape((rows - 2) * half_width, C1), 0, 0)
        for tap in range(4)
    ]
    first = merging_mine.shape[2]
    mine[:, :, :first] = merging_mine[...]
    other[:, :, :first] = merging_other[...]
    by_slot(jnp.concatenate(parts, axis=0), mine, other, slots, front, shards, first)
    flat = fine[...].reshape(height * width, C1)
    source = grid[RIM_UP : RIM_UP + height, LEAD - 2 : LEAD - 2 + width]
    made = product(source.reshape(height * width, C0), flat, 0, 0)
    first += 4 * C1 // shards
    by_slot(made, mine, other, slots, front, shards, first)
    first += C0 // shards
    both = jnp.concatenate([heads_grad[0 : C2 // 2], heads_grad[C2 // 2 : C2]], axis=1)
    by_slot(both, mine, other, slots, front, shards, first)


def input_gradient(
    pixels,
    coarse_pixels,
    flags,
    grad_one,
    below,
    right,
    z_one,
    total_one,
    grads_one,
    gain_one,
    weight,
    grad_joined,
    z_four,
    grads_joined,
    gain_four,
    lateral,
    occupancy,
    out,
    taps,
    fine,
    wide_fine,
):
    lateral_gradient(
        pixels, grad_joined, z_four, total_one, grads_joined, gain_four, wide_fine
    )
    flat = wide_fine[...].reshape(-1, C1)
    grad_masked = product(flat, lateral[...], 1, 1).reshape(fine.shape)
    rows, half_width = z_one.shape[0], z_one.shape[1]
    height, breadth, _ = occupancy.shape
    centre, spread = spread_of(channel_sums(total_one)[:, : 2 * C1], coarse_pixels)
    gained = channel_sums(grads_one)
    scale = gain_one[...] * spread
    mean_gain = gained[:, :C1] * (1.0 / coarse_pixels)
    mean_shift = gained[:, C1:] * (1.0 / coarse_pixels)
    col = lax.broadcasted_iota(jnp.int32, (half_width, C1), 0)
    edge = half_width - 2
    live = ((col >= 1) & (col < edge)) | ((col == edge) & (flags[31] != 0.0))
    parts = []
    for i in range(1, rows):
        raw = grad_one[i] if i < rows - 1 else below[0]
        raw = jnp.where(col == edge, right[i - 1], raw)
        normed = (z_one[i] - centre) * spread
        value = scale * (raw - mean_shift - normed * mean_gain)
        parts.append(jnp.where(live, value, 0.0))
    made = product(jnp.concatenate(parts, axis=0), weight[...], 1, 1)
    taps[...] = made.reshape(rows - 1, half_width, 9 * C0)

    def tap(a, b, i):
        value = taps[i, :, (3 * a + b) * C0 : (3 * a + b + 1) * C0]
        if b == 0:
            value = pltpu.roll(value, half_width - 1, 0)
        if a == 0:
            value = value * flags[i + 1]
        return value

    for i in range(rows - 2):
        fine[2 * i, pl.ds(0, half_width, 2), :] = tap(1, 1, i)
        fine[2 * i, pl.ds(1, half_width, 2), :] = tap(1, 2, i) + tap(1, 0, i)
        fine[2 * i + 1, pl.ds(0, half_width, 2), :] = tap(2, 1, i) + tap(0, 1, i + 1)
        fine[2 * i + 1, pl.ds(1, half_width, 2), :] = (
            tap(2, 2, i) + tap(2, 0, i) + tap(0, 2, i + 1) + tap(0, 0, i + 1)
        )
    for r in range(height):
        total = fine[r] + grad_masked[r]
        out[pl.ds(r, breadth, height), :] = total[2 : 2 + breadth] * occupancy[r]


def dot(a,b,ca,cb):
    return lax.dot_general(a,b,(((ca,),(cb,)),((),())),precision=HIGHEST,preferred_element_type=F32)
NB=64
W=8
def base_inverse(blocks):
    lane=lax.broadcasted_iota(jnp.int32,(8,128),1); row=lax.broadcasted_iota(jnp.int32,(8,128),0)
    T=NB//8
    xs=[]
    for b in blocks:
        tiles=[]
        for t in range(T):
            pad=jnp.zeros((8,128-NB),F32)
            tiles.append(jnp.concatenate([b[8*t:8*t+8],pad],axis=1)+(lane==row+(NB+8*t)).astype(F32))
        xs.append(tiles)
    for g in range(0,NB,W):
        own=g//8
        cols=[[{t:jnp.broadcast_to(x[t][:,g+j:g+j+1],(8,128)) for t in range(own,T)} for j in range(W)] for x in xs]
        for j in range(W):
            k=(g+j)%8
            for m in range(len(xs)):
                c=cols[m][j]
                inv=1.0/c[own][k:k+1,:]
                rest=[(xs[m],xs[m][own][k:k+1,:])]+[(cols[m][u],cols[m][u][own][k:k+1,:]) for u in range(j+1,W)]
                for t in range(own,T):
                    f=(jnp.where(row>k,c[t],0.0) if t==own else c[t])*inv
                    for target,pivot_row in rest:
                        target[t]=target[t]-f*pivot_row
    outs=[]
    for x in xs:
        done=[]
        for t in range(T):
            d=jnp.sum(jnp.where(lane==row+8*t,x[t],0.0),axis=1,keepdims=True)
            done.append((x[t]*lax.rsqrt(d))[:,NB:2*NB])
        outs.append(jnp.concatenate(done,axis=0))
    return outs
def kern(ns,*refs):
    m=len(ns)
    gram=refs[0:m]; add=refs[m:2*m]; basis=refs[2*m:3*m]
    out_gram=refs[3*m:4*m]; out_rot=refs[4*m:5*m]
    both=refs[5*m:6*m]
    for i,n in enumerate(ns):
        g=0.95*gram[i][...]+0.05*add[i][...]
        out_gram[i][...]=g
        turned=dot(basis[i][...],g,0,0)
        a=dot(turned,turned,1,1)
        npad=both[i].shape[0]
        if npad!=n:
            r=lax.broadcasted_iota(jnp.int32,(npad,2*npad),0); c=lax.broadcasted_iota(jnp.int32,(npad,2*npad),1)
            both[i][...]=((r==c)&(r>=n)).astype(F32)
        both[i][0:n,0:n]=a
        both[i][0:n,npad:npad+n]=turned
    for b in range(max(a.shape[0] for a in both)//NB):
        s=b*NB
        live=[i for i in range(m) if s<both[i].shape[0]]
        inv=base_inverse([both[i][s:s+NB,s:s+NB] for i in live])
        for i,li in zip(live,inv):
            npad=both[i].shape[0]
            e=s+NB
            left=min(e//128*128,npad)
            panel=dot(li,both[i][s:e,left:],1,0)
            both[i][s:e,left:]=panel
            if e<npad:
                both[i][e:,left:]=both[i][e:,left:]-dot(panel[:,e-left:npad-left],panel,0,0)
    for i,n in enumerate(ns):
        npad=both[i].shape[0]
        out_rot[i][...]=both[i][:,npad:].T[0:n,0:n]


def keep_rows(global_rows, total_rows):
    wrapped = jnp.remainder(global_rows, total_rows)
    return ((wrapped + SCENE_ROWS // 2) % SCENE_ROWS != 0).astype(jnp.float32)


def from_behind(block, axis, distance):
    devices = range(lax.axis_size(axis))
    route = [(i - distance, i) for i in devices if i - distance in devices]
    return lax.ppermute(block, axis, route)


def shifted(value, axis, steps):
    count = lax.axis_size(axis)
    pairs = [(source, (source + steps) % count) for source in range(count)]
    return lax.ppermute(value, axis, pairs)


def after(value, *others):
    return lax.optimization_barrier((value,) + others)[0]


def exchange(value):
    return lax.ppermute(value, "stream", [(0, 1), (1, 0)])


def to_all(rows):
    return lax.all_to_all(rows, ("dp", "stream"), 0, 0, tiled=True)


def everyone(value):
    count = lax.axis_size("dp")
    copies = jnp.broadcast_to(value[None], (count,) + value.shape)
    return lax.all_to_all(copies, "dp", 0, 0, tiled=True)


def far_groups():
    far = lax.axis_size("dp") // NEAR
    return [[low + NEAR * high for high in range(far)] for low in range(NEAR)]


def across(value, low):
    count = lax.axis_size("dp")
    return lax.ppermute(value, "dp", [(i, i ^ low) for i in range(count)])


def gather_pieces(value, *first):
    count = lax.axis_size("dp")
    far = count // NEAR
    if far <= NEAR:
        held = [value] + [shifted(value, "dp", NEAR * step) for step in range(1, far)]
        column = jnp.stack(held)
    else:
        copies = jnp.broadcast_to(value[None], (far,) + value.shape)
        column = lax.all_to_all(
            copies, "dp", 0, 0, axis_index_groups=far_groups(), tiled=True
        )
    column = after(column, *first)
    return jnp.stack([column] + [across(column, low) for low in range(1, NEAR)])


def by_low(value):
    low = lax.axis_index("dp") % NEAR
    pairs = value.reshape((2, 2) + value.shape[1:])
    pairs = jnp.where(low % 2 == 1, lax.rev(pairs, (1,)), pairs)
    pairs = jnp.where(low // 2 == 1, lax.rev(pairs, (0,)), pairs)
    return pairs.reshape(value.shape)


def by_index(pieces):
    far = pieces.shape[1]
    pieces = by_low(pieces)
    if far <= NEAR:
        back = lax.rev(pieces, (1,))
        start = (-1 - lax.axis_index("dp") // NEAR) % far
        pieces = lax.dynamic_slice_in_dim(jnp.concatenate([back, back], axis=1), start, far, 1)
    return jnp.swapaxes(pieces, 0, 1).reshape((NEAR * far,) + pieces.shape[2:])


def gather_order():
    count = lax.axis_size("dp")
    far = count // NEAR
    index = lax.axis_index("dp")
    low = (index % NEAR) ^ jnp.arange(NEAR)
    high = (index // NEAR - jnp.arange(far)) % far if far <= NEAR else jnp.arange(far)
    return (high[None, :] * NEAR + low[:, None]).reshape(-1).astype(jnp.int32)


def chip_sums(mine, other):
    return [mine[step] + other[step] for step in range(NEAR)]


def near_sum(sums, *first):
    total = after(sums[0], *first)
    for step in range(1, NEAR):
        total = total + across(sums[step], step)
    return total


def slotted(pair):
    core = lax.axis_index("stream")
    shape = (lax.axis_size("dp") // NEAR, NEAR) + pair.shape[2:]
    parts = (pick(pair, 0, which).reshape(shape) for which in (core, 1 - core))
    return [by_low(jnp.swapaxes(part, 0, 1)) for part in parts]


def far_sum(column):
    moved = lax.all_to_all(column, "dp", 0, 0, axis_index_groups=far_groups(), tiled=True)
    return moved


def in_order(mine, other):
    first = lax.axis_index("stream") == 0
    return jnp.where(first, mine, other), jnp.where(first, other, mine)


def pick(pair, axis, which):
    return lax.dynamic_index_in_dim(pair, which, axis, keepdims=False)


def by_shard(halves):
    count = lax.axis_size("dp")
    short = -halves.shape[1] % count
    if short:
        halves = jnp.pad(halves, ((0, 0), (0, short), (0, 0)))
    return halves.reshape(2, count, halves.shape[1] // count, halves.shape[2])


def fold_rows(rows, count):
    parts = rows.reshape(count, 2, 2, rows.shape[0] // (4 * count), C2)
    return jnp.swapaxes(jnp.concatenate([parts[:, :, 0], parts[:, :, 1]], axis=-1), 0, 1)


def unfold_rows(first, second):
    both = jnp.stack([first, second], axis=1)
    parts = jnp.stack([both[..., :C2], both[..., C2:]], axis=2)
    return parts.reshape(-1, C2)


def arranged(place, pieces, swapped, first=0, past=None):
    past = pieces.shape[2] if past is None else past
    count, rows = pieces.shape[0] * pieces.shape[1], past - first
    if rows % 8 == 0:
        body = functools.partial(arrange, first, rows)
        outs = [(count * rows, 2 * pieces.shape[3])]
        return stage(body, outs, [pieces, swapped], scalars=[place], name="arrange")[0]
    both = in_order(pieces[:, :, first:past], swapped[:, :, first:past])
    both = [by_index(part) for part in both]
    return jnp.concatenate([part.reshape(count * rows, -1) for part in both], axis=1)


def packed_merging(place, pieces, swapped, first, moment):
    count, rows = pieces.shape[0] * pieces.shape[1], pieces.shape[2] - first
    if rows % 8 == 0:
        return stage(
            functools.partial(arrange_merging, first),
            [(2 * C1, 12 * C2)],
            [after(pieces, moment), swapped],
            scalars=[place],
            scratch=[pltpu.VMEM((18 * C1, C2), F32)],
            name="pack",
        )[0]
    both = in_order(pieces[:, :, first:], swapped[:, :, first:])
    both = [by_index(part) for part in both]
    return stage(pack_merging, [(2 * C1, 12 * C2)], [unfold_rows(*both)], name="pack")[0]


def lanes_of(row, width):
    return jnp.pad(row, (0, width - row.shape[0]))[None]


def adam_vector(params, moment, square, gradient):
    momentum = BETA_ONE * moment + (1.0 - BETA_ONE) * gradient
    variance = BETA_TWO * square + (1.0 - BETA_TWO) * gradient * gradient
    direction = (
        momentum / (1.0 - BETA_ONE**STEP) / (jnp.sqrt(variance / (1.0 - BETA_TWO**STEP)) + EPS_ADAM)
    )
    return (params - VECTOR_RATE * (direction + DECAY * params), momentum, variance)


def soap_one(rate, flipped, weight, moment, square, basis, gradient, outs):
    if flipped:
        rotated = product(basis, gradient, 0, 1, HIGHEST)
    else:
        rotated = product(gradient, basis, 1, 0, HIGHEST)
    momentum = BETA_ONE * moment[...] + (1.0 - BETA_ONE) * rotated
    variance = BETA_TWO * square[...] + (1.0 - BETA_TWO) * rotated * rotated
    direction = momentum * (1.0 / (1.0 - BETA_ONE**STEP)) / (
        jnp.sqrt(variance * (1.0 / (1.0 - BETA_TWO**STEP))) + EPS_ADAM
    )
    if flipped:
        turned = product(basis, direction, 1, 0, HIGHEST)
    else:
        turned = product(direction, basis, 1, 1, HIGHEST)
    old = weight[...]
    outs[0][...] = old - rate * (turned + DECAY * old)
    outs[1][...] = momentum
    outs[2][...] = variance


def soap_shards(rates, *refs):
    count = len(rates)
    for i, (rate, flipped) in enumerate(rates):
        group = refs[5 * i : 5 * i + 3]
        outs = refs[5 * count + 3 * i : 5 * count + 3 * i + 3]
        basis, gradient = refs[5 * i + 3][...], refs[5 * i + 4][...]
        soap_one(rate, flipped, *group, basis, gradient, outs)


def close(rates, *refs):
    grams, bases, adds = refs[0:5], refs[5:10], refs[10:15]
    lateral, head = refs[15:18], refs[18:21]
    outs, lateral_outs, head_outs = refs[21:31], refs[31:34], refs[34:37]
    lateral_gram, head_gram = refs[37:39]
    total_lateral, total_heads = adds[2][...], adds[4][...]
    lateral_gram[...] = product(total_lateral, total_lateral, 0, 0, HIGHEST)
    head_gram[...] = product(total_heads, total_heads, 0, 0, HIGHEST)
    sums = (adds[0], adds[1], lateral_gram, adds[3], head_gram)
    kern([C1, C1, C1, C2, CH], *grams, *sums, *bases, *outs, *refs[39:])
    soap_one(rates[0], False, *lateral, bases[2][...], total_lateral, lateral_outs)
    soap_one(rates[1], False, *head, bases[4][...], total_heads, head_outs)


def close_parts(rates, cuts, flags, mine, other, *refs):
    shards = mine.shape[0]
    front = flags[30] == 0.0
    down, upward, lateral, merging, head = adds = refs[-5:]
    half = C1 // 2
    count = C1 // shards
    small = cuts[0] - 2 * count
    for d in range(shards):
        first = jnp.where(front, mine[d], other[d])
        second = jnp.where(front, other[d], mine[d])
        for side in range(2):
            rows, lanes = slice(side * count, (side + 1) * count), slice(side * half, (side + 1) * half)
            down[d * count : (d + 1) * count, lanes] = first[rows]
            upward[d * count : (d + 1) * count, lanes] = second[rows]
        merging[d * small : (d + 1) * small] = second[2 * count : cuts[0], 0:C2]
        rows = cuts[1] - cuts[0]
        lateral[d * rows : (d + 1) * rows, 0:half] = first[cuts[0] : cuts[1]]
        lateral[d * rows : (d + 1) * rows, half:] = second[cuts[0] : cuts[1]]
        rows = cuts[2] - cuts[1]
        head[d * rows : (d + 1) * rows] = first[cuts[1] : cuts[2], 0:CH]
        start = C2 // 2 + d * rows
        head[start : start + rows] = second[cuts[1] : cuts[2], 0:CH]
    close(rates, *refs[:10], *adds, *refs[10:-5])


def partial_gram(shard):
    return jnp.tensordot(shard, shard, axes=((0,), (0,)), precision=HIGHEST)


def assembled(final, other, gram_rows, small):
    final_first, final_second = in_order(final, other)
    shards, half, wide = final.shape[0], C1 // 2, 2 * C2

    def square_of(value):
        count = C1 // shards
        return jnp.concatenate(
            [value[:, k * count : (k + 1) * count].reshape(C1, half) for k in range(2)], axis=1
        )

    gram_down = square_of(final_first)
    gram_upward = square_of(final_second)
    gram_merging = final_second[:, 2 * (C1 // shards) : gram_rows].reshape(-1, wide)[:C2, :C2]
    total_lateral = jnp.concatenate(
        [v[:, gram_rows : gram_rows + small].reshape(C0, half) for v in (final_first, final_second)],
        axis=1,
    )
    total_heads = jnp.concatenate(
        [
            v[:, gram_rows + small :].reshape(-1, wide)[: C2 // 2]
            for v in (final_first, final_second)
        ],
        axis=0,
    )[:, :CH]
    return gram_down, gram_upward, total_lateral, gram_merging, total_heads


def local(
    feats,
    occupied,
    cotangent,
    vector_params,
    vector_moment,
    vector_square,
    down_weight,
    down_moment,
    down_square,
    down_gram,
    down_basis,
    upward_weight,
    upward_moment,
    upward_square,
    upward_gram,
    upward_basis,
    lateral_weight,
    lateral_moment,
    lateral_square,
    lateral_gram,
    lateral_basis,
    merging_weight,
    merging_moment,
    merging_square,
    merging_gram,
    merging_basis,
    heads_weight,
    heads_moment,
    heads_square,
    heads_gram,
    heads_basis,
):
    height, breadth, _ = feats.shape
    half_height, half_breadth = height // 2, breadth // 2
    shards = lax.axis_size("dp")
    cores = lax.axis_size("stream")
    everybody = shards * cores
    total_rows = height * shards
    fine_count = float(height * breadth * everybody)
    coarse_count = fine_count / 4.0
    shard_index, core = lax.axis_index("dp"), lax.axis_index("stream")
    first_row = shard_index * height
    width, half_width = breadth + 6, half_breadth + 3
    rows, half_rows = height + 2, half_height + 2
    flags = jnp.concatenate(
        [
            keep_rows(first_row + 2 * jnp.arange(-1, half_height + 1), total_rows),
            keep_rows(first_row + jnp.arange(-1, height + 3), total_rows),
            (core != 0).astype(F32)[None],
            (core != cores - 1).astype(F32)[None],
        ]
    )
    gains = [vector_params[i * C1 : (i + 1) * C1] for i in range(6)]
    late = 6 * C1
    gain_five, shift_five = vector_params[late : late + C2], vector_params[late + C2 : late + 2 * C2]
    head_bias = vector_params[late + 2 * C2 :]
    wide = 2 * C2
    norm_fine = jnp.stack(
        [jnp.concatenate([gains[2], gains[4]]), jnp.concatenate([gains[3], gains[5]])]
    )
    norm_five = jnp.concatenate([lanes_of(gain_five, wide), lanes_of(shift_five, wide)])

    half = C1 // 2
    weight_halves = [
        lax.dynamic_slice_in_dim(w, core * half, half, 1) for w in (down_weight, upward_weight)
    ]
    quarter = merging_weight.shape[0] // 4
    runs = [
        lax.dynamic_slice_in_dim(merging_weight, (2 * core + i) * quarter, quarter, 0)
        for i in range(2)
    ]
    weight_halves.append(jnp.concatenate(runs, axis=1))
    place = jnp.concatenate([gather_order(), core[None].astype(jnp.int32)])
    occupancy = occupied.astype(F32)[..., None]
    masked = feats * occupancy
    shown = jnp.broadcast_to(occupancy, feats.shape)
    up = shifted(masked[height - RIM_UP :], "dp", 1)
    down = shifted(masked[:RIM_DOWN], "dp", -1)
    edges = jnp.concatenate([up, masked, down], axis=0)
    gathered = gather_pieces(jnp.concatenate(weight_halves, axis=0), up, down)
    left = from_behind(edges[:, breadth - RIM_LEFT :], "stream", 1)
    right = from_behind(edges[:, :RIM_RIGHT], "stream", -1)
    grid, z_four, sums_four = stage(
        pad_lateral,
        [
            (height + RIM_UP + RIM_DOWN, width + LEAD - 2, C0),
            (rows, width, C1),
            (1, 2 * C1),
        ],
        [masked, up, down, left, right, lateral_weight],
        name="pad_lateral",
    )

    swapped = exchange(after(gathered, grid))
    bounds = [0]
    for part in weight_halves:
        bounds.append(bounds[-1] + part.shape[0])
    map_outs = [
        (half_rows, half_width, C1),
        (half_rows, half_width, 9 * C0),
        (everybody, 1, 4 * C1),
    ]
    if bounds[1] % 8 == 0:
        part_shape = (NEAR, shards // NEAR, bounds[1], half)
        z_one, windows, sums_one, down_full = stage(
            coarse_arranged,
            [*map_outs, (9 * C0, C1)],
            [grid, gathered, swapped, sums_four],
            scalars=[flags, place],
            scratch=[pltpu.VMEM(part_shape, F32)] * 2 + [pltpu.SemaphoreType.DMA((2,))],
            name="coarse",
            far_args=(1, 2),
        )
    else:
        down_full = arranged(place, gathered, swapped, 0, bounds[1])
        z_one, windows, sums_one = stage(
            coarse_map, map_outs, [grid, down_full, sums_four], scalars=[flags], name="coarse"
        )
    upward_full = arranged(place, after(gathered, z_one), swapped, bounds[1], bounds[2])
    total_one = after(to_all(sums_one), upward_full)

    z_three, act_one, slope_one, sums_three = stage(
        functools.partial(upsample, coarse_count),
        [
            (2, rows, width, C1 // 2),
            (half_rows, half_width, C1),
            (half_rows, half_width, C1),
            (everybody, 1, 2 * C1),
        ],
        [z_one, total_one, gains[0][None], gains[1][None], upward_full],
        name="upsample",
    )
    packed = packed_merging(place, gathered, swapped, bounds[2], sums_three)
    total_three = after(to_all(sums_three), packed)

    merged, joined, slopes, sums_five = stage(
        functools.partial(merge, fine_count),
        [
            (height, width, wide),
            (rows, width, 2 * C1),
            (rows, width, 2 * C1),
            (everybody, 1, 2 * wide),
        ],
        [z_three, z_four, total_three, total_one, norm_fine, packed],
        scalars=[flags],
        scratch=[
            pltpu.VMEM((rows, width, 12 * C2), F32),
            pltpu.VMEM((2, rows, width, half), F32),
            pltpu.VMEM((rows, width, C1), F32),
            pltpu.VMEM((2 * C1, 12 * C2), F32),
            pltpu.VMEM((rows, width, 2 * C1), F32),
            pltpu.VMEM((rows, width, 2 * C1), F32),
            pltpu.SemaphoreType.DMA((rows // 3 + 1,)),
            pltpu.SemaphoreType.DMA((rows // 3,)),
        ],
        name="merge",
        far_args=(0, 1, 5),
        far_outs=(1, 2),
    )
    total_five = to_all(sums_five)

    heads_padded = jnp.pad(heads_weight, ((0, wide - C2), (0, wide - CH)))
    head_maps, pairs, last_row, first_row_pair, edge, heads_grad, grad_sums_five = stage(
        functools.partial(heads, fine_count),
        [
            (height, CH, breadth),
            (height, width, wide),
            (1, width, wide),
            (1, width, wide),
            (height, 1, wide),
            (wide, wide),
            (everybody, 1, 3 * wide),
        ],
        [merged, total_five, norm_five, heads_padded, lanes_of(head_bias, wide), cotangent],
        scalars=[flags],
        scratch=[pltpu.VMEM((height, width, wide), F32)] * 2,
        name="heads",
    )
    head_maps = jnp.swapaxes(head_maps, 1, 2)
    grads_five = to_all(grad_sums_five)
    above = shifted(last_row, "dp", 1)
    below = shifted(first_row_pair, "dp", -1)
    ends = [jnp.where(core == 0, v[:, 1 + breadth : 2 + breadth], v[:, 2:3]) for v in (above, below)]
    side = exchange(jnp.concatenate([ends[0], edge, ends[1]], axis=0))

    grad_joined, columns, grad_sums = stage(
        functools.partial(merged_gradient, fine_count),
        [
            (height, width, 2 * C1),
            (rows, width, 4 * C2),
            (everybody, 1, 4 * C1),
        ],
        [
            pairs,
            above,
            below,
            side,
            total_five,
            grads_five,
            norm_five,
            packed,
            z_three,
            z_four,
            slopes,
            total_three,
            total_one,
        ],
        scalars=[flags],
        scratch=[
            pltpu.VMEM((2 * C1, 12 * C2), F32),
            pltpu.VMEM((2, rows, width, half), F32),
            pltpu.VMEM((rows, width, C1), F32),
            pltpu.VMEM((rows, width, 2 * C1), F32),
            pltpu.VMEM((height, width, 2 * C1), F32),
            pltpu.VMEM((rows, width, 4 * C2), F32),
            pltpu.SemaphoreType.DMA((3 * height // 4 + 1,)),
            pltpu.SemaphoreType.DMA((height // 4 + 1,)),
        ],
        name="merged_gradient",
        far_args=(7, 8, 9, 10),
        far_outs=(0, 1),
    )
    far = shards // NEAR
    slots = jnp.arange(NEAR, dtype=jnp.int32) ^ (shard_index % NEAR).astype(jnp.int32)
    shifted_rows = pltpu.VMEM((height, width, 4 * C2), F32)
    aligned = quarter % 8 == 0
    if aligned:
        merging_grads = stage(
            merging_product,
            [(NEAR, far, quarter, wide)] * 2,
            [joined, columns],
            scalars=[flags, slots],
            scratch=[pltpu.VMEM((18 * C1, C2), F32), shifted_rows],
            name="merging_product",
        )
    else:
        (merging_grad,) = stage(
            multiply_merging,
            [(18 * C1, C2)],
            [joined, columns],
            scalars=[flags],
            scratch=[shifted_rows],
            name="merging_product",
        )
        merging_grads = slotted(fold_rows(merging_grad, shards))
    merging_grad = merging_grads[0]
    grads_joined = after(to_all(grad_sums), merging_grad)

    quads, grad_one, top_one, side_one, grad_sums_one = stage(
        functools.partial(coarse_gradient, fine_count, coarse_count),
        [
            (4, half_height, half_width, C1),
            (half_rows, half_width, C1),
            (1, half_width, C1),
            (half_height, 1, C1),
            (everybody, 1, 2 * C1),
        ],
        [
            grad_joined,
            z_three,
            total_three,
            grads_joined,
            gains[2][None],
            upward_full,
            z_one,
            total_one,
            slope_one,
        ],
        scratch=[pltpu.VMEM((2, height, width, C1 // 2), F32)],
        name="coarse_gradient",
    )
    late_rows = [4 * C1 // shards, C0 // shards, -(-C2 // (2 * shards))]
    late_args = [
        grad_joined,
        z_four,
        total_one,
        grads_joined,
        gains[4][None],
        grid,
        act_one,
        quads,
        heads_grad,
    ]
    fine_scratch = pltpu.VMEM((height, width, C1), F32)
    if aligned:
        late_grads = stage(
            functools.partial(fine_products, fine_count),
            [(NEAR, far, quarter + sum(late_rows), half)] * 2,
            [*late_args, *merging_grads],
            scalars=[flags, slots],
            scratch=[fine_scratch],
            name="fine_products",
        )
    else:
        late_halves = stage(
            functools.partial(fine_halves, fine_count),
            [(2, 4 * C1, half), (2, C0, half)],
            late_args[:-1],
            scratch=[fine_scratch],
            name="fine_products",
        )
        heads_halves = heads_grad[:C2].reshape(2, C2 // 2, wide)
        blocks = [by_shard(value) for value in (*late_halves, heads_halves)]
        pairs_of = zip(merging_grads, slotted(jnp.concatenate(blocks, axis=2)))
        late_grads = [jnp.concatenate(pair, axis=2) for pair in pairs_of]
    grads_one = after(to_all(grad_sums_one), late_grads[0])
    down_args = [windows, grad_one, z_one, total_one, grads_one, gains[0][None]]
    if aligned:
        down_grads = stage(
            functools.partial(window_product, coarse_count),
            [(NEAR, far, 9 * C0 // shards, half)] * 2,
            down_args,
            scalars=[flags, slots],
            name="window_product",
        )
    else:
        (halves,) = stage(
            functools.partial(window_halves, coarse_count),
            [(2, 9 * C0, half)],
            down_args,
            name="window_product",
        )
        down_grads = slotted(by_shard(halves))
    down_sums = chip_sums(down_grads[0], exchange(down_grads[1]))
    rest_other = exchange(after(late_grads[1], down_grads[0]))
    rest_sums = chip_sums(after(late_grads[0], *down_sums), rest_other)
    down_mine = near_sum(down_sums)
    below = shifted(after(top_one, *rest_sums), "dp", -1)
    first_col = jnp.concatenate([side_one, below[:, 1:2]], axis=0)
    right = from_behind(first_col, "stream", -1)
    received = far_sum(after(down_mine, *rest_sums))
    rest = near_sum(rest_sums, received, below)
    rest_received = far_sum(rest)
    cuts = [0]
    for count in (quarter, *late_rows):
        cuts.append(cuts[-1] + count)

    sums_back = jnp.sum(grads_one[:, 0], axis=0)
    down_part = jnp.sum(received, axis=0)
    down_shard = jnp.concatenate(in_order(down_part, exchange(down_part)), axis=1)
    gram_one = partial_gram(down_shard)
    part = jnp.sum(after(rest_received, gram_one, right), axis=0)
    swapped = exchange(part[: cuts[2]])
    first_part, second_part = in_order(part[: cuts[2]], swapped)
    merging_shard = unfold_rows(first_part[None, : cuts[1]], second_part[None, : cuts[1]])
    upward_shard = jnp.concatenate([first_part[cuts[1] :], second_part[cuts[1] :]], axis=1)

    def lane_rows(gram):
        count = gram.shape[0] // shards
        return jnp.concatenate(
            [
                gram[:, k * half : (k + 1) * half].reshape(shards, count, half)
                for k in range(C1 // half)
            ],
            axis=1,
        )

    shard_groups = [
        (down_weight, down_moment, down_square, down_basis, down_shard),
        (upward_weight, upward_moment, upward_square, upward_basis, upward_shard),
        (merging_weight.T, merging_moment.T, merging_square.T, merging_basis, merging_shard),
    ]
    stepped = stage(
        functools.partial(
            soap_shards,
            (
                (1.0 / math.sqrt(9 * C0), False),
                (1.0 / math.sqrt(C1), False),
                (1.0 / math.sqrt(18 * C1), True),
            ),
        ),
        [group[0].shape for group in shard_groups for _ in range(3)],
        [array for group in shard_groups for array in group],
        name="soap",
    )
    down_renewed, down_momentum, down_variance = stepped[:3]
    upward_renewed, upward_momentum, upward_variance = stepped[3:6]
    merging_renewed, merging_momentum, merging_variance = (value.T for value in stepped[6:])
    gram_two = jnp.pad(partial_gram(merging_shard), ((0, -C2 % shards), (0, wide - C2)))
    gram_two = gram_two.reshape(shards, -1, wide)
    firsts = jnp.pad(lane_rows(gram_one), ((0, 0), (0, gram_two.shape[1]), (0, 0)))
    seconds = jnp.concatenate([lane_rows(partial_gram(upward_shard)), gram_two], axis=1)
    parts = jnp.where(core == 0, firsts, seconds)
    gram_parts = after(lax.all_to_all(parts, "dp", 0, 0, tiled=True), *stepped)
    gram_sum = jnp.sum(gram_parts, axis=0)
    (feats_grad,) = stage(
        functools.partial(input_gradient, fine_count, coarse_count),
        [(breadth * height, C0)],
        [
            grad_one,
            below,
            right,
            z_one,
            total_one,
            after(grads_one, gram_sum),
            gains[0][None],
            down_full,
            grad_joined,
            z_four,
            grads_joined,
            gains[4][None],
            lateral_weight,
            shown,
        ],
        scalars=[flags],
        scratch=[
            pltpu.VMEM((half_rows - 1, half_width, 9 * C0), F32),
            pltpu.VMEM((height, width, C0), F32),
            fine_scratch,
        ],
        name="input_gradient",
    )
    feats_grad = jnp.swapaxes(feats_grad.reshape(breadth, height, C0), 0, 1)
    gram_rows = gram_sum.shape[0]
    final = everyone(jnp.concatenate([gram_sum, part[cuts[2] :]], axis=0))
    final = after(final, feats_grad)
    final_other = exchange(final)
    grams = (down_gram, upward_gram, lateral_gram, merging_gram, heads_gram)
    bases = (down_basis, upward_basis, lateral_basis, merging_basis, heads_basis)
    orders = [C1, C1, C1, C2, CH]
    padded = [-(-n // NB) * NB for n in orders]
    close_args = [
        *grams,
        *bases,
        lateral_weight,
        lateral_moment,
        lateral_square,
        heads_weight,
        heads_moment,
        heads_square,
    ]
    close_outs = [(n, n) for n in orders] * 2 + [(C0, C1)] * 3 + [(C2, CH)] * 3
    close_scratch = [pltpu.VMEM((n, n), F32) for n in (C1, CH)]
    close_scratch += [pltpu.VMEM((n, 2 * n), F32) for n in padded]
    rates = (1.0 / math.sqrt(C0), 1.0 / math.sqrt(C2))
    add_shapes = [(C1, C1), (C1, C1), (C0, C1), (C2, C2), (C2, CH)]
    if aligned:
        ends = (gram_rows, gram_rows + late_rows[1], gram_rows + sum(late_rows[1:]))
        closed = stage(
            functools.partial(close_parts, rates, ends),
            close_outs,
            [final, final_other, *close_args],
            scalars=[flags],
            scratch=close_scratch + [pltpu.VMEM(shape, F32) for shape in add_shapes],
            name="close",
        )
    else:
        adds = assembled(final, final_other, gram_rows, late_rows[1])
        closed = stage(
            functools.partial(close, rates),
            close_outs,
            [*close_args[:10], *adds, *close_args[10:]],
            scratch=close_scratch,
            name="close",
        )
    down_gramian, upward_gramian, lateral_gramian, merging_gramian, heads_gramian = closed[:5]
    down_rotation, upward_rotation, lateral_rotation, merging_rotation, heads_rotation = closed[5:10]
    lateral_renewed, lateral_momentum, lateral_variance = closed[10:13]
    heads_renewed, heads_momentum, heads_variance = closed[13:]

    sums_fine = jnp.sum(grads_joined[:, 0], axis=0)
    sums_late = jnp.sum(grads_five[:, 0], axis=0)
    grad_vector = jnp.concatenate(
        [
            sums_back,
            sums_fine[:C1],
            sums_fine[2 * C1 : 3 * C1],
            sums_fine[C1 : 2 * C1],
            sums_fine[3 * C1 :],
            sums_late[:C2],
            sums_late[wide : wide + C2],
            sums_late[2 * wide : 2 * wide + CH],
        ]
    )
    vector_renewed, vector_momentum, vector_variance = adam_vector(
        vector_params, vector_moment, vector_square, grad_vector
    )
    return (
        head_maps,
        feats_grad,
        vector_renewed,
        vector_momentum,
        vector_variance,
        down_renewed,
        down_momentum,
        down_variance,
        down_gramian,
        down_rotation,
        upward_renewed,
        upward_momentum,
        upward_variance,
        upward_gramian,
        upward_rotation,
        lateral_renewed,
        lateral_momentum,
        lateral_variance,
        lateral_gramian,
        lateral_rotation,
        merging_renewed,
        merging_momentum,
        merging_variance,
        merging_gramian,
        merging_rotation,
        heads_renewed,
        heads_momentum,
        heads_variance,
        heads_gramian,
        heads_rotation,
    )


def solution(mesh):
    in_specs = (
        P("dp", "stream", None),
        P("dp", "stream"),
        P("dp", "stream", None),
        P(),
        P(),
        P(),
        P("dp", None),
        P("dp", None),
        P("dp", None),
        P(),
        P(),
        P("dp", None),
        P("dp", None),
        P("dp", None),
        P(),
        P(),
        P(),
        P(),
        P(),
        P(),
        P(),
        P("dp", None),
        P("dp", None),
        P("dp", None),
        P(),
        P(),
        P(),
        P(),
        P(),
        P(),
        P(),
    )
    out_specs = (
        P("dp", "stream", None),
        P("dp", "stream", None),
        P(),
        P(),
        P(),
        P("dp", None),
        P("dp", None),
        P("dp", None),
        P(),
        P(),
        P("dp", None),
        P("dp", None),
        P("dp", None),
        P(),
        P(),
        P(),
        P(),
        P(),
        P(),
        P(),
        P("dp", None),
        P("dp", None),
        P("dp", None),
        P(),
        P(),
        P(),
        P(),
        P(),
        P(),
        P(),
    )
    return jax.shard_map(local, mesh=mesh, in_specs=in_specs, out_specs=out_specs, check_vma=False)
```

```python
import functools
import math

import jax
import jax.numpy as jnp
from jax import lax
from jax.experimental import pallas as pl
from jax.experimental.pallas import tpu as pltpu
from jax.sharding import PartitionSpec as P

C0 = 128
C1 = 256
C2 = 64
CH = 70
SCENE_ROWS = 180
STEP = 10


EPS_NORM = 1e-05
BETA_ONE = 0.9
BETA_TWO = 0.95
BETA_GRAM = 0.95
EPS_ADAM = 1e-08
DECAY = 0.01
VECTOR_RATE = 0.1
HIGHEST = lax.Precision.HIGHEST


F32 = jnp.float32
HIGH = lax.Precision.HIGH
RIM_UP, RIM_DOWN, RIM_LEFT, RIM_RIGHT = 3, 2, 3, 2
LEAD = 10
NEAR = 4


def product(left, right, over_left, over_right, precision=HIGH):
    dims = (((over_left,), (over_right,)), ((), ()))
    return lax.dot_general(
        left, right, dims, precision=precision, preferred_element_type=F32
    )


def stage(body, outs, args, scalars=(), scratch=(), name=None, far_args=(), far_outs=()):
    vmem = pl.BlockSpec(memory_space=pltpu.VMEM)
    smem = pl.BlockSpec(memory_space=pltpu.SMEM)
    away = pl.BlockSpec(memory_space=pl.ANY)
    shapes = [jax.ShapeDtypeStruct(shape, F32) for shape in outs]
    return pl.pallas_call(
        body,
        out_shape=shapes,
        in_specs=[smem] * len(scalars)
        + [away if i in far_args else vmem for i in range(len(args))],
        out_specs=[away if i in far_outs else vmem for i in range(len(shapes))],
        scratch_shapes=list(scratch),
        compiler_params=pltpu.CompilerParams(vmem_limit_bytes=56 << 20),
        name=name,
    )(*scalars, *args)


def channel_sums(ref):
    return jnp.sum(ref[...], axis=0)


def spread_of(total, pixels):
    half = total.shape[1] // 2
    centre = total[:, :half] * (1.0 / pixels)
    second = total[:, half:] * (1.0 / pixels)
    return centre, lax.rsqrt(second - centre * centre + EPS_NORM)


def cols_between(count, lanes, first, past):
    col = lax.broadcasted_iota(jnp.int32, (count, lanes), 0)
    return (col >= first) & (col < past)


def row_total(value):
    return jnp.sum(value, axis=0, keepdims=True)


def send(ref, row):
    ref[...] = jnp.broadcast_to(row[None], ref.shape)


def pad_lateral(masked, up, down, left, right, lateral, grid, z_four, sums):
    height, breadth, channels = masked.shape
    grid[...] = jnp.zeros(grid.shape, F32)
    inner = slice(LEAD, LEAD + breadth)
    grid[0:RIM_UP, inner] = up[...]
    grid[RIM_UP : RIM_UP + height, inner] = masked[...]
    grid[RIM_UP + height :, inner] = down[...]
    grid[:, LEAD - RIM_LEFT : LEAD] = left[...]
    grid[:, LEAD + breadth : LEAD + breadth + RIM_RIGHT] = right[...]
    width = z_four.shape[1]
    own = cols_between(width, C1, 2, 2 + breadth)
    total = jnp.zeros((1, C1), F32)
    square = jnp.zeros((1, C1), F32)
    tile = 6
    for first in range(0, height + 2, tile):
        block = grid[2 + first : 2 + first + tile, LEAD - 2 : LEAD - 2 + width]
        made = product(block.reshape(tile * width, channels), lateral[...], 1, 0)
        made = made.reshape(tile, width, C1)
        z_four[first : first + tile] = made
        for row in range(tile):
            if 1 <= first + row <= height:
                kept = jnp.where(own, made[row], 0.0)
                total = total + row_total(kept)
                square = square + row_total(kept * kept)
    sums[...] = jnp.concatenate([total, square], axis=1)


def coarse_arranged(
    flags, place, grid, pieces_far, swapped_far, sums_four, z_one, windows, sums, weight, *scratch
):
    pieces, swapped, arrived = scratch
    rows = pieces.shape[2]
    copies = [
        start_copy(pieces_far.at[:, :, pl.ds(0, rows)], pieces, arrived.at[0]),
        start_copy(swapped_far.at[:, :, pl.ds(0, rows)], swapped, arrived.at[1]),
    ]
    build_windows(flags, grid, windows, z_one.shape[1])
    for copy in copies:
        copy.wait()
    arrange(0, rows, place, pieces, swapped, weight)
    multiply_map(weight, sums_four, z_one, windows, sums)


def coarse_map(flags, grid, weight, sums_four, z_one, windows, sums):
    build_windows(flags, grid, windows, z_one.shape[1])
    multiply_map(weight, sums_four, z_one, windows, sums)


def build_windows(flags, grid, windows, width):
    for i in range(windows.shape[0]):
        for a in range(3):
            for b in range(3):
                piece = grid[2 * i + a, pl.ds(LEAD - 3 + b, width, 2), :]
                if a == 0:
                    piece = piece * flags[i]
                tap = 3 * a + b
                windows[i, :, tap * C0 : (tap + 1) * C0] = piece


def multiply_map(weight, sums_four, z_one, windows, sums):
    rows, width = z_one.shape[0], z_one.shape[1]
    half_breadth = width - 3
    made = product(windows[...].reshape(rows * width, 9 * C0), weight[...], 1, 0)
    z_one[...] = made.reshape(rows, width, C1)
    own = cols_between(width, C1, 1, 1 + half_breadth)
    total = jnp.zeros((1, C1), F32)
    square = jnp.zeros((1, C1), F32)
    for i in range(1, rows - 1):
        kept = jnp.where(own, z_one[i], 0.0)
        total = total + row_total(kept)
        square = square + row_total(kept * kept)
    send(sums, jnp.concatenate([total, square, sums_four[...]], axis=1))


def window_halves(
    coarse_pixels, windows, grad_one, z_one, total_one, grads_one, gain_one, halves
):
    args = (windows, grad_one, z_one, total_one, grads_one, gain_one)
    made = multiply_windows(coarse_pixels, *args)
    halves[0] = made[:, : C1 // 2]
    halves[1] = made[:, C1 // 2 :]


def window_product(
    coarse_pixels, flags, slots, windows, grad_one, z_one, total_one, grads_one, gain_one, mine, other
):
    args = (windows, grad_one, z_one, total_one, grads_one, gain_one)
    made = multiply_windows(coarse_pixels, *args)
    shards = mine.shape[0] * mine.shape[1]
    by_slot(made, mine, other, slots, flags[30] == 0.0, shards, 0)


def multiply_windows(coarse_pixels, windows, grad_one, z_one, total_one, grads_one, gain_one):
    rows, width, depth = windows.shape
    centre, spread = spread_of(channel_sums(total_one)[:, : 2 * C1], coarse_pixels)
    gained = channel_sums(grads_one)
    scale = gain_one[...] * spread
    mean_gain = gained[:, :C1] * (1.0 / coarse_pixels)
    mean_shift = gained[:, C1:] * (1.0 / coarse_pixels)
    own = cols_between(width, C1, 1, width - 2)
    parts = []
    for i in range(1, rows - 1):
        normed = (z_one[i] - centre) * spread
        value = scale * (grad_one[i] - mean_shift - normed * mean_gain)
        parts.append(jnp.where(own, value, 0.0))
    inside = windows[1 : rows - 1].reshape((rows - 2) * width, depth)
    return product(inside, jnp.concatenate(parts, axis=0), 0, 0)


def upsample(pixels, z_one, total_one, gain, shift, weight, z_three, act_one, slope_one, sums):
    rows, width = z_one.shape[0], z_one.shape[1]
    half_breadth = width - 3
    centre, spread = spread_of(channel_sums(total_one)[:, : 2 * C1], pixels)
    for i in range(rows):
        hidden = (z_one[i] - centre) * spread * gain[...] + shift[...]
        sigmoid = lax.logistic(hidden)
        act_one[i] = hidden * sigmoid
        slope_one[i] = sigmoid * (1.0 + hidden * (1.0 - sigmoid))
    active = act_one[...].reshape(rows * width, C1)
    own = cols_between(width, C1, 1, 1 + half_breadth)
    total = jnp.zeros((1, C1), F32)
    square = jnp.zeros((1, C1), F32)
    half = C1 // 2
    for a in range(2):
        for b in range(2):
            tap = 2 * a + b
            made = product(active, weight[tap * C1 : (tap + 1) * C1], 1, 0)
            for i in range(rows):
                part = made[i * width : (i + 1) * width]
                place = 2 * i + a - 1
                if 0 <= place < 2 * rows - 2:
                    for k in range(2):
                        z_three[k, place, pl.ds(b, width, 2), :] = part[:, k * half : (k + 1) * half]
                if 1 <= i < rows - 1:
                    kept = jnp.where(own, part, 0.0)
                    total = total + row_total(kept)
                    square = square + row_total(kept * kept)
    send(sums, jnp.concatenate([total, square], axis=1))


def pack_merging(weight, packed):
    for a in range(3):
        pieces = [
            weight[(3 * a + b) * 2 * C1 : (3 * a + b + 1) * 2 * C1] for b in range(3)
        ]
        pieces.append(jnp.zeros((2 * C1, C2), F32))
        packed[:, a * 4 * C2 : (a + 1) * 4 * C2] = jnp.concatenate(pieces, axis=1)


def arrange(first, rows, place, pieces, swapped, out):
    near, far, _, lanes = pieces.shape
    front = place[near * far] == 0
    for low in range(near):
        for high in range(far):
            at = pl.ds(pl.multiple_of(place[low * far + high] * rows, 8), rows)
            mine = pieces[low, high, first : first + rows]
            other = swapped[low, high, first : first + rows]
            out[at, 0:lanes] = jnp.where(front, mine, other)
            out[at, lanes:] = jnp.where(front, other, mine)


def arrange_merging(first, place, pieces, swapped, packed, weight):
    near, far, last, _ = pieces.shape
    rows = last - first
    front = place[near * far] == 0
    for low in range(near):
        for high in range(far):
            mine, other = pieces[low, high, first:], swapped[low, high, first:]
            values = (jnp.where(front, mine, other), jnp.where(front, other, mine))
            for core in range(2):
                for side in range(2):
                    start = (place[low * far + high] * 4 + 2 * core + side) * rows
                    at = pl.ds(pl.multiple_of(start, 8), rows)
                    weight[at, :] = values[core][:, side * C2 : (side + 1) * C2]
    pack_merging(weight, packed)


def start_copy(source, target, semaphore):
    copy = pltpu.make_async_copy(source, target, semaphore)
    copy.start()
    return copy


def merge(
    pixels,
    flags,
    z_three_far,
    z_four_far,
    total_three,
    total_one,
    norms,
    packed_far,
    merged,
    joined_far,
    slopes_far,
    sums,
    taps,
    z_three,
    z_four,
    packed,
    joined,
    slopes,
    arrived,
    left,
):
    rows, width = z_four.shape[0], z_four.shape[1]
    height = rows - 2
    breadth = width - 6
    tile = 6
    firsts = list(range(0, rows, tile))
    coming = []
    for t, r in enumerate(firsts):
        part = pl.ds(r, tile)
        coming.append(
            [
                start_copy(z_three_far.at[:, part], z_three.at[:, part], arrived.at[2 * t]),
                start_copy(z_four_far.at[part], z_four.at[part], arrived.at[2 * t + 1]),
            ]
        )
    weight_copy = start_copy(packed_far, packed, arrived.at[2 * len(firsts)])
    sum_three = channel_sums(total_three)
    sum_four = channel_sums(total_one)[:, 2 * C1 :]
    centre_three, spread_three = spread_of(sum_three, pixels)
    centre_four, spread_four = spread_of(sum_four, pixels)
    centre = jnp.concatenate([centre_three, centre_four], axis=1)
    spread = jnp.concatenate([spread_three, spread_four], axis=1)
    scale = spread * norms[0:1]
    offset = norms[1:2] - centre * scale
    col = lax.broadcasted_iota(jnp.int32, (width, 2 * C1), 0)
    dead = ((col == 1) & (flags[30] == 0.0)) | ((col == 2 + breadth) & (flags[31] == 0.0))

    def activate(r, carry):
        raw = jnp.concatenate([z_three[0, r], z_three[1, r], z_four[r]], axis=1)
        hidden = raw * scale + offset
        sigmoid = lax.logistic(hidden)
        joined[r] = jnp.where(dead, 0.0, hidden * sigmoid)
        slopes[r] = sigmoid * (1.0 + hidden * (1.0 - sigmoid))
        return carry

    going = []
    for t, r in enumerate(firsts):
        for copy in coming[t]:
            copy.wait()
        lax.fori_loop(r, r + tile, activate, 0)
        part = pl.ds(r, tile)
        going.append(start_copy(joined.at[part], joined_far.at[part], left.at[2 * t]))
        going.append(start_copy(slopes.at[part], slopes_far.at[part], left.at[2 * t + 1]))
    weight_copy.wait()

    long = rows // 2
    for r in range(0, rows, long):
        block = joined[r : r + long].reshape(long * width, 2 * C1)
        taps[r : r + long] = product(block, packed[...], 1, 0).reshape(long, width, 12 * C2)
    own = cols_between(width, 2 * C2, 2, 2 + breadth)
    lane = lax.broadcasted_iota(jnp.int32, (width, 2 * C2), 1)
    total = jnp.zeros((1, 2 * C2), F32)
    square = jnp.zeros((1, 2 * C2), F32)
    for row in range(height):
        r = row + 1
        both = (
            taps[r - 1, :, 0 : 4 * C2] * flags[10 + r]
            + taps[r, :, 4 * C2 : 8 * C2]
            + taps[r + 1, :, 8 * C2 : 12 * C2] * flags[11 + r]
        )
        first, second = both[:, : 2 * C2], both[:, 2 * C2 :]
        out = (
            pltpu.roll(first, 1, 0)
            + pltpu.roll(first, C2, 1)
            + pltpu.roll(second, width - 1, 0)
        )
        out = jnp.where(own & (lane < C2), out, 0.0)
        merged[row] = out
        total = total + row_total(out)
        square = square + row_total(out * out)
    send(sums, jnp.concatenate([total, square], axis=1))
    for copy in going:
        copy.wait()


def heads(
    pixels,
    flags,
    merged,
    total_five,
    norms,
    weight,
    bias,
    cotangent,
    maps,
    pairs,
    last_row,
    first_row,
    edge,
    weight_grad,
    sums,
    active,
    upstream,
):
    height, width, _ = merged.shape
    breadth = width - 6
    centre, spread = spread_of(channel_sums(total_five)[:, : 4 * C2], pixels)
    own = cols_between(width, 2 * C2, 2, 2 + breadth)
    upstream[...] = jnp.zeros(upstream.shape, F32)
    for r in range(height):
        upstream[r, 2 : 2 + breadth, 0:CH] = cotangent[r]
    flat = upstream[...].reshape(height * width, 2 * C2)
    grad = product(flat, weight[...], 1, 1).reshape(height, width, 2 * C2)
    grad_gain = jnp.zeros((1, 2 * C2), F32)
    grad_shift = jnp.zeros((1, 2 * C2), F32)
    for r in range(height):
        normed = jnp.where(own, (merged[r] - centre) * spread, 0.0)
        hidden = norms[0:1] * normed + norms[1:2]
        sigmoid = lax.logistic(hidden)
        active[r] = hidden * sigmoid
        grad_hidden = grad[r] * sigmoid * (1.0 + hidden * (1.0 - sigmoid))
        pair = grad_hidden + pltpu.roll(normed, C2, 1)
        pairs[r] = pair
        edge[r] = jnp.where(flags[30] == 0.0, pair[1 + breadth : 2 + breadth], pair[2:3])
        if r == 0:
            first_row[0] = pair
        if r == height - 1:
            last_row[0] = pair
        grad_gain = grad_gain + row_total(grad_hidden * normed)
        grad_shift = grad_shift + row_total(grad_hidden)
    send(sums, jnp.concatenate([grad_gain, grad_shift, row_total(flat)], axis=1))
    act = active[...].reshape(height * width, 2 * C2)
    made = product(act, weight[...], 1, 0).reshape(height, width, 2 * C2) + bias[...]
    for r in range(height):
        maps[r] = pltpu.roll(made[r], width - 2, 0).T[0:CH, 0:breadth]
    weight_grad[...] = product(act, flat, 0, 0)


def merged_gradient(
    pixels,
    flags,
    pairs,
    above,
    below,
    side,
    total_five,
    grads_five,
    norm_five,
    packed_far,
    z_three_far,
    z_four_far,
    slopes_far,
    total_three,
    total_one,
    grad_far,
    columns_far,
    sums,
    packed,
    z_three,
    z_four,
    slopes,
    grad_joined,
    columns,
    arrived,
    left_sems,
):
    height, width, _ = pairs.shape
    breadth = width - 6
    lanes = 2 * C2
    tile = 4
    weight_copy = start_copy(packed_far, packed, arrived.at[0])
    coming = []
    for t in range(height // tile):
        part = pl.ds(t * tile + 1, tile)
        coming.append(
            [
                start_copy(slopes_far.at[part], slopes.at[part], arrived.at[3 * t + 1]),
                start_copy(z_three_far.at[:, part], z_three.at[:, part], arrived.at[3 * t + 2]),
                start_copy(z_four_far.at[part], z_four.at[part], arrived.at[3 * t + 3]),
            ]
        )
    _, spread = spread_of(channel_sums(total_five)[:, : 4 * C2], pixels)
    gained = channel_sums(grads_five)
    scale = norm_five[0:1] * spread
    mean_gain = gained[:, :lanes] * (1.0 / pixels)
    mean_shift = gained[:, lanes : 2 * lanes] * (1.0 / pixels)
    col = lax.broadcasted_iota(jnp.int32, (width, lanes), 0)
    lane = lax.broadcasted_iota(jnp.int32, (width, lanes), 1)
    live = (
        ((col >= 2) & (col < 2 + breadth))
        | ((col == 1) & (flags[30] != 0.0))
        | ((col == 2 + breadth) & (flags[31] != 0.0))
    ) & (lane < C2)
    target = jnp.where(flags[30] == 0.0, 2 + breadth, 1)
    for r in range(height + 2):
        if r == 0:
            raw = above[0]
        elif r == height + 1:
            raw = below[0]
        else:
            raw = pairs[r - 1]
        raw = jnp.where(col == target, side[r], raw)
        normed = pltpu.roll(raw, C2, 1)
        value = jnp.where(live, scale * (raw - mean_shift - normed * mean_gain), 0.0)
        columns[r, :, 0:lanes] = pltpu.roll(value, width - 1, 0) + pltpu.roll(value, C2, 1)
        columns[r, :, lanes:] = pltpu.roll(value, 1, 0)
    going = [start_copy(columns, columns_far, left_sems.at[0])]
    centre_three, spread_three = spread_of(channel_sums(total_three), pixels)
    centre_four, spread_four = spread_of(channel_sums(total_one)[:, 2 * C1 :], pixels)
    centre = jnp.concatenate([centre_three, centre_four], axis=1)
    spread = jnp.concatenate([spread_three, spread_four], axis=1)
    own = cols_between(width, 2 * C1, 2, 2 + breadth)

    def gradient(t, carry):
        r = t * tile
        block = jnp.zeros((tile * width, 2 * C1), F32)
        for a in range(3):
            rows = []
            for k in range(tile):
                source = r + k + 2 - a
                row = columns[source]
                if a == 0:
                    row = row * flags[10 + source]
                if a == 2:
                    row = row * flags[11 + source]
                rows.append(row)
            block = block + product(
                jnp.concatenate(rows, axis=0), packed[:, a * 4 * C2 : (a + 1) * 4 * C2], 1, 1
            )
        gain_sum, shift_sum = carry
        for k in range(tile):
            grad = jnp.where(own, block[k * width : (k + 1) * width] * slopes[r + k + 1], 0.0)
            grad_joined[r + k] = grad
            raw = jnp.concatenate(
                [z_three[0, r + k + 1], z_three[1, r + k + 1], z_four[r + k + 1]], axis=1
            )
            normed = (raw - centre) * spread
            gain_sum = gain_sum + row_total(grad * normed)
            shift_sum = shift_sum + row_total(grad)
        return gain_sum, shift_sum

    empty = jnp.zeros((1, 2 * C1), F32)
    carry = (empty, empty)
    weight_copy.wait()
    for t in range(height // tile):
        for copy in coming[t]:
            copy.wait()
        carry = gradient(t, carry)
        part = pl.ds(t * tile, tile)
        going.append(start_copy(grad_joined.at[part], grad_far.at[part], left_sems.at[t + 1]))
    send(sums, jnp.concatenate(carry, axis=1))
    for copy in going:
        copy.wait()


def by_slot(value, mine, other, slots, front, shards, first):
    rows = value.shape[0] // shards
    half = value.shape[1] // 2
    for shard in range(shards):
        piece = value[shard * rows : (shard + 1) * rows]
        low, high = piece[:, :half], piece[:, half:]
        place = slots[shard % NEAR], shard // NEAR, slice(first, first + rows)
        mine[place] = jnp.where(front, low, high)
        other[place] = jnp.where(front, high, low)


def merging_product(flags, slots, joined, columns, mine, other, grads, shifted_rows):
    multiply_merging(flags, joined, columns, grads, shifted_rows)
    front = flags[30] == 0.0
    near, far, rows, _ = mine.shape
    for shard in range(near * far):
        start = 4 * rows * shard
        runs = [grads[start + i * rows : start + (i + 1) * rows] for i in range(4)]
        first = jnp.concatenate(runs[:2], axis=1)
        second = jnp.concatenate(runs[2:], axis=1)
        place = slots[shard % near], shard // near
        mine[place] = jnp.where(front, first, second)
        other[place] = jnp.where(front, second, first)


def multiply_merging(flags, joined, columns, grads, shifted_rows):
    rows, width, _ = joined.shape
    height = rows - 2
    inside = joined[1 : rows - 1].reshape(height * width, 2 * C1)
    own = cols_between(width, 4 * C2, 2, width - 4)
    for a in range(3):
        for r in range(height):
            source = r + 2 - a
            row = columns[source]
            if a == 0:
                row = row * flags[10 + source]
            if a == 2:
                row = row * flags[11 + source]
            shifted_rows[r] = jnp.where(own, row, 0.0)
        made = product(inside, shifted_rows[...].reshape(height * width, 4 * C2), 0, 0)
        for b in range(3):
            grads[(3 * a + b) * 2 * C1 : (3 * a + b + 1) * 2 * C1] = made[:, b * C2 : (b + 1) * C2]


def coarse_gradient(
    pixels,
    coarse_pixels,
    grad_joined,
    z_three,
    total_three,
    grads_joined,
    gain_three,
    weight,
    z_one,
    total_one,
    slope_one,
    quads,
    grad_one,
    top,
    side,
    sums,
    fine,
):
    height, width = grad_joined.shape[0], grad_joined.shape[1]
    rows, half_width = z_one.shape[0], z_one.shape[1]
    half = C1 // 2
    centre, spread = spread_of(channel_sums(total_three), pixels)
    gained = channel_sums(grads_joined)
    scale = gain_three[...] * spread
    mean_gain = gained[:, :C1] * (1.0 / pixels)
    mean_shift = gained[:, 2 * C1 : 3 * C1] * (1.0 / pixels)
    own = cols_between(width, C1, 2, width - 4)

    def fill(r, carry):
        raw = jnp.concatenate([z_three[0, r + 1], z_three[1, r + 1]], axis=1)
        normed = (raw - centre) * spread
        value = scale * (grad_joined[r, :, 0:C1] - mean_shift - normed * mean_gain)
        value = jnp.where(own, value, 0.0)
        fine[0, r] = value[:, :half]
        fine[1, r] = value[:, half:]
        return carry

    lax.fori_loop(0, height, fill, 0)
    grad = jnp.zeros(((rows - 2) * half_width, C1), F32)
    for a in range(2):
        for b in range(2):
            tap = 2 * a + b
            for i in range(rows - 2):
                for k in range(2):
                    quads[tap, i, :, k * half : (k + 1) * half] = fine[
                        k, 2 * i + a, pl.ds(b, half_width, 2), :
                    ]
            flat = quads[tap].reshape((rows - 2) * half_width, C1)
            grad = grad + product(flat, weight[tap * C1 : (tap + 1) * C1], 1, 1)
    centre, spread = spread_of(channel_sums(total_one)[:, : 2 * C1], coarse_pixels)
    own = cols_between(half_width, C1, 1, half_width - 2)
    gain_sum = jnp.zeros((1, C1), F32)
    shift_sum = jnp.zeros((1, C1), F32)
    grad_one[0] = jnp.zeros((half_width, C1), F32)
    grad_one[rows - 1] = jnp.zeros((half_width, C1), F32)
    for i in range(1, rows - 1):
        value = grad[(i - 1) * half_width : i * half_width] * slope_one[i]
        value = jnp.where(own, value, 0.0)
        grad_one[i] = value
        side[i - 1] = value[1:2]
        if i == 1:
            top[0] = value
        gain_sum = gain_sum + row_total(value * ((z_one[i] - centre) * spread))
        shift_sum = shift_sum + row_total(value)
    send(sums, jnp.concatenate([gain_sum, shift_sum], axis=1))


def lateral_gradient(pixels, grad_joined, z_four, total_one, grads_joined, gain_four, fine):
    height, width = grad_joined.shape[0], grad_joined.shape[1]
    centre, spread = spread_of(channel_sums(total_one)[:, 2 * C1 :], pixels)
    gained = channel_sums(grads_joined)
    scale = gain_four[...] * spread
    mean_gain = gained[:, C1 : 2 * C1] * (1.0 / pixels)
    mean_shift = gained[:, 3 * C1 :] * (1.0 / pixels)
    own = cols_between(width, C1, 2, width - 4)

    def fill(r, carry):
        normed = (z_four[r + 1] - centre) * spread
        value = scale * (grad_joined[r, :, C1:] - mean_shift - normed * mean_gain)
        fine[r] = jnp.where(own, value, 0.0)
        return carry

    lax.fori_loop(0, height, fill, 0)


def fine_halves(
    pixels,
    grad_joined,
    z_four,
    total_one,
    grads_joined,
    gain_four,
    grid,
    act_one,
    quads,
    upward_halves,
    lateral_halves,
    fine,
):
    height, width = grad_joined.shape[0], grad_joined.shape[1]
    rows, half_width = act_one.shape[0], act_one.shape[1]
    half = C1 // 2
    lateral_gradient(pixels, grad_joined, z_four, total_one, grads_joined, gain_four, fine)
    flat = fine[...].reshape(height * width, C1)
    source = grid[RIM_UP : RIM_UP + height, LEAD - 2 : LEAD - 2 + width]
    made = product(source.reshape(height * width, C0), flat, 0, 0)
    lateral_halves[0] = made[:, :half]
    lateral_halves[1] = made[:, half:]
    inside = act_one[1 : rows - 1].reshape((rows - 2) * half_width, C1)
    for tap in range(4):
        made = product(inside, quads[tap].reshape((rows - 2) * half_width, C1), 0, 0)
        for side in range(2):
            upward_halves[side, tap * C1 : (tap + 1) * C1] = made[
                :, side * half : (side + 1) * half
            ]


def fine_products(
    pixels,
    flags,
    slots,
    grad_joined,
    z_four,
    total_one,
    grads_joined,
    gain_four,
    grid,
    act_one,
    quads,
    heads_grad,
    merging_mine,
    merging_other,
    mine,
    other,
    fine,
):
    height, width = grad_joined.shape[0], grad_joined.shape[1]
    rows, half_width = act_one.shape[0], act_one.shape[1]
    shards = mine.shape[0] * mine.shape[1]
    front = flags[30] == 0.0
    lateral_gradient(pixels, grad_joined, z_four, total_one, grads_joined, gain_four, fine)
    inside = act_one[1 : rows - 1].reshape((rows - 2) * half_width, C1)
    parts = [
        product(inside, quads[tap].reshape((rows - 2) * half_width, C1), 0, 0)
        for tap in range(4)
    ]
    first = merging_mine.shape[2]
    mine[:, :, :first] = merging_mine[...]
    other[:, :, :first] = merging_other[...]
    by_slot(jnp.concatenate(parts, axis=0), mine, other, slots, front, shards, first)
    flat = fine[...].reshape(height * width, C1)
    source = grid[RIM_UP : RIM_UP + height, LEAD - 2 : LEAD - 2 + width]
    made = product(source.reshape(height * width, C0), flat, 0, 0)
    first += 4 * C1 // shards
    by_slot(made, mine, other, slots, front, shards, first)
    first += C0 // shards
    both = jnp.concatenate([heads_grad[0 : C2 // 2], heads_grad[C2 // 2 : C2]], axis=1)
    by_slot(both, mine, other, slots, front, shards, first)


def input_gradient(
    pixels,
    coarse_pixels,
    flags,
    grad_one,
    below,
    right,
    z_one,
    total_one,
    grads_one,
    gain_one,
    weight,
    grad_joined,
    z_four,
    grads_joined,
    gain_four,
    lateral,
    occupancy,
    out,
    taps,
    fine,
    wide_fine,
):
    lateral_gradient(
        pixels, grad_joined, z_four, total_one, grads_joined, gain_four, wide_fine
    )
    flat = wide_fine[...].reshape(-1, C1)
    grad_masked = product(flat, lateral[...], 1, 1).reshape(fine.shape)
    rows, half_width = z_one.shape[0], z_one.shape[1]
    height, breadth, _ = occupancy.shape
    centre, spread = spread_of(channel_sums(total_one)[:, : 2 * C1], coarse_pixels)
    gained = channel_sums(grads_one)
    scale = gain_one[...] * spread
    mean_gain = gained[:, :C1] * (1.0 / coarse_pixels)
    mean_shift = gained[:, C1:] * (1.0 / coarse_pixels)
    col = lax.broadcasted_iota(jnp.int32, (half_width, C1), 0)
    edge = half_width - 2
    live = ((col >= 1) & (col < edge)) | ((col == edge) & (flags[31] != 0.0))
    parts = []
    for i in range(1, rows):
        raw = grad_one[i] if i < rows - 1 else below[0]
        raw = jnp.where(col == edge, right[i - 1], raw)
        normed = (z_one[i] - centre) * spread
        value = scale * (raw - mean_shift - normed * mean_gain)
        parts.append(jnp.where(live, value, 0.0))
    made = product(jnp.concatenate(parts, axis=0), weight[...], 1, 1)
    taps[...] = made.reshape(rows - 1, half_width, 9 * C0)

    def tap(a, b, i):
        value = taps[i, :, (3 * a + b) * C0 : (3 * a + b + 1) * C0]
        if b == 0:
            value = pltpu.roll(value, half_width - 1, 0)
        if a == 0:
            value = value * flags[i + 1]
        return value

    for i in range(rows - 2):
        fine[2 * i, pl.ds(0, half_width, 2), :] = tap(1, 1, i)
        fine[2 * i, pl.ds(1, half_width, 2), :] = tap(1, 2, i) + tap(1, 0, i)
        fine[2 * i + 1, pl.ds(0, half_width, 2), :] = tap(2, 1, i) + tap(0, 1, i + 1)
        fine[2 * i + 1, pl.ds(1, half_width, 2), :] = (
            tap(2, 2, i) + tap(2, 0, i) + tap(0, 2, i + 1) + tap(0, 0, i + 1)
        )
    for r in range(height):
        total = fine[r] + grad_masked[r]
        out[pl.ds(r, breadth, height), :] = total[2 : 2 + breadth] * occupancy[r]


def dot(a,b,ca,cb):
    return lax.dot_general(a,b,(((ca,),(cb,)),((),())),precision=HIGHEST,preferred_element_type=F32)
NB=64
W=8
def base_inverse(blocks):
    lane=lax.broadcasted_iota(jnp.int32,(8,128),1); row=lax.broadcasted_iota(jnp.int32,(8,128),0)
    T=NB//8
    xs=[]
    for b in blocks:
        tiles=[]
        for t in range(T):
            pad=jnp.zeros((8,128-NB),F32)
            tiles.append(jnp.concatenate([b[8*t:8*t+8],pad],axis=1)+(lane==row+(NB+8*t)).astype(F32))
        xs.append(tiles)
    for g in range(0,NB,W):
        own=g//8
        cols=[[{t:jnp.broadcast_to(x[t][:,g+j:g+j+1],(8,128)) for t in range(own,T)} for j in range(W)] for x in xs]
        for j in range(W):
            k=(g+j)%8
            for m in range(len(xs)):
                c=cols[m][j]
                inv=1.0/c[own][k:k+1,:]
                rest=[(xs[m],xs[m][own][k:k+1,:])]+[(cols[m][u],cols[m][u][own][k:k+1,:]) for u in range(j+1,W)]
                for t in range(own,T):
                    f=(jnp.where(row>k,c[t],0.0) if t==own else c[t])*inv
                    for target,pivot_row in rest:
                        target[t]=target[t]-f*pivot_row
    outs=[]
    for x in xs:
        done=[]
        for t in range(T):
            d=jnp.sum(jnp.where(lane==row+8*t,x[t],0.0),axis=1,keepdims=True)
            done.append((x[t]*lax.rsqrt(d))[:,NB:2*NB])
        outs.append(jnp.concatenate(done,axis=0))
    return outs
def kern(ns,*refs):
    m=len(ns)
    gram=refs[0:m]; add=refs[m:2*m]; basis=refs[2*m:3*m]
    out_gram=refs[3*m:4*m]; out_rot=refs[4*m:5*m]
    both=refs[5*m:6*m]
    for i,n in enumerate(ns):
        g=0.95*gram[i][...]+0.05*add[i][...]
        out_gram[i][...]=g
        turned=dot(basis[i][...],g,0,0)
        a=dot(turned,turned,1,1)
        npad=both[i].shape[0]
        if npad!=n:
            r=lax.broadcasted_iota(jnp.int32,(npad,2*npad),0); c=lax.broadcasted_iota(jnp.int32,(npad,2*npad),1)
            both[i][...]=((r==c)&(r>=n)).astype(F32)
        both[i][0:n,0:n]=a
        both[i][0:n,npad:npad+n]=turned
    for b in range(max(a.shape[0] for a in both)//NB):
        s=b*NB
        live=[i for i in range(m) if s<both[i].shape[0]]
        inv=base_inverse([both[i][s:s+NB,s:s+NB] for i in live])
        for i,li in zip(live,inv):
            npad=both[i].shape[0]
            e=s+NB
            left=min(e//128*128,npad)
            panel=dot(li,both[i][s:e,left:],1,0)
            both[i][s:e,left:]=panel
            if e<npad:
                both[i][e:,left:]=both[i][e:,left:]-dot(panel[:,e-left:npad-left],panel,0,0)
    for i,n in enumerate(ns):
        npad=both[i].shape[0]
        out_rot[i][...]=both[i][:,npad:].T[0:n,0:n]


def keep_rows(global_rows, total_rows):
    wrapped = jnp.remainder(global_rows, total_rows)
    return ((wrapped + SCENE_ROWS // 2) % SCENE_ROWS != 0).astype(jnp.float32)


def from_behind(block, axis, distance):
    devices = range(lax.axis_size(axis))
    route = [(i - distance, i) for i in devices if i - distance in devices]
    return lax.ppermute(block, axis, route)


def shifted(value, axis, steps):
    count = lax.axis_size(axis)
    pairs = [(source, (source + steps) % count) for source in range(count)]
    return lax.ppermute(value, axis, pairs)


def after(value, *others):
    return lax.optimization_barrier((value,) + others)[0]


def exchange(value):
    return lax.ppermute(value, "stream", [(0, 1), (1, 0)])


def to_all(rows):
    return lax.all_to_all(rows, ("dp", "stream"), 0, 0, tiled=True)


def everyone(value):
    count = lax.axis_size("dp")
    copies = jnp.broadcast_to(value[None], (count,) + value.shape)
    return lax.all_to_all(copies, "dp", 0, 0, tiled=True)


def far_groups():
    far = lax.axis_size("dp") // NEAR
    return [[low + NEAR * high for high in range(far)] for low in range(NEAR)]


def across(value, low):
    count = lax.axis_size("dp")
    return lax.ppermute(value, "dp", [(i, i ^ low) for i in range(count)])


def gather_pieces(value, *first):
    count = lax.axis_size("dp")
    far = count // NEAR
    if far <= NEAR:
        held = [value] + [shifted(value, "dp", NEAR * step) for step in range(1, far)]
        column = jnp.stack(held)
    else:
        copies = jnp.broadcast_to(value[None], (far,) + value.shape)
        column = lax.all_to_all(
            copies, "dp", 0, 0, axis_index_groups=far_groups(), tiled=True
        )
    column = after(column, *first)
    return jnp.stack([column] + [across(column, low) for low in range(1, NEAR)])


def by_low(value):
    low = lax.axis_index("dp") % NEAR
    pairs = value.reshape((2, 2) + value.shape[1:])
    pairs = jnp.where(low % 2 == 1, lax.rev(pairs, (1,)), pairs)
    pairs = jnp.where(low // 2 == 1, lax.rev(pairs, (0,)), pairs)
    return pairs.reshape(value.shape)


def by_index(pieces):
    far = pieces.shape[1]
    pieces = by_low(pieces)
    if far <= NEAR:
        back = lax.rev(pieces, (1,))
        start = (-1 - lax.axis_index("dp") // NEAR) % far
        pieces = lax.dynamic_slice_in_dim(jnp.concatenate([back, back], axis=1), start, far, 1)
    return jnp.swapaxes(pieces, 0, 1).reshape((NEAR * far,) + pieces.shape[2:])


def gather_order():
    count = lax.axis_size("dp")
    far = count // NEAR
    index = lax.axis_index("dp")
    low = (index % NEAR) ^ jnp.arange(NEAR)
    high = (index // NEAR - jnp.arange(far)) % far if far <= NEAR else jnp.arange(far)
    return (high[None, :] * NEAR + low[:, None]).reshape(-1).astype(jnp.int32)


def chip_sums(mine, other):
    return [mine[step] + other[step] for step in range(NEAR)]


def near_sum(sums, *first):
    total = after(sums[0], *first)
    for step in range(1, NEAR):
        total = total + across(sums[step], step)
    return total


def slotted(pair):
    core = lax.axis_index("stream")
    shape = (lax.axis_size("dp") // NEAR, NEAR) + pair.shape[2:]
    parts = (pick(pair, 0, which).reshape(shape) for which in (core, 1 - core))
    return [by_low(jnp.swapaxes(part, 0, 1)) for part in parts]


def far_sum(column):
    moved = lax.all_to_all(column, "dp", 0, 0, axis_index_groups=far_groups(), tiled=True)
    return moved


def in_order(mine, other):
    first = lax.axis_index("stream") == 0
    return jnp.where(first, mine, other), jnp.where(first, other, mine)


def pick(pair, axis, which):
    return lax.dynamic_index_in_dim(pair, which, axis, keepdims=False)


def by_shard(halves):
    count = lax.axis_size("dp")
    short = -halves.shape[1] % count
    if short:
        halves = jnp.pad(halves, ((0, 0), (0, short), (0, 0)))
    return halves.reshape(2, count, halves.shape[1] // count, halves.shape[2])


def fold_rows(rows, count):
    parts = rows.reshape(count, 2, 2, rows.shape[0] // (4 * count), C2)
    return jnp.swapaxes(jnp.concatenate([parts[:, :, 0], parts[:, :, 1]], axis=-1), 0, 1)


def unfold_rows(first, second):
    both = jnp.stack([first, second], axis=1)
    parts = jnp.stack([both[..., :C2], both[..., C2:]], axis=2)
    return parts.reshape(-1, C2)


def arranged(place, pieces, swapped, first=0, past=None):
    past = pieces.shape[2] if past is None else past
    count, rows = pieces.shape[0] * pieces.shape[1], past - first
    if rows % 8 == 0:
        body = functools.partial(arrange, first, rows)
        outs = [(count * rows, 2 * pieces.shape[3])]
        return stage(body, outs, [pieces, swapped], scalars=[place], name="arrange")[0]
    both = in_order(pieces[:, :, first:past], swapped[:, :, first:past])
    both = [by_index(part) for part in both]
    return jnp.concatenate([part.reshape(count * rows, -1) for part in both], axis=1)


def packed_merging(place, pieces, swapped, first, moment):
    count, rows = pieces.shape[0] * pieces.shape[1], pieces.shape[2] - first
    if rows % 8 == 0:
        return stage(
            functools.partial(arrange_merging, first),
            [(2 * C1, 12 * C2)],
            [after(pieces, moment), swapped],
            scalars=[place],
            scratch=[pltpu.VMEM((18 * C1, C2), F32)],
            name="pack",
        )[0]
    both = in_order(pieces[:, :, first:], swapped[:, :, first:])
    both = [by_index(part) for part in both]
    return stage(pack_merging, [(2 * C1, 12 * C2)], [unfold_rows(*both)], name="pack")[0]


def lanes_of(row, width):
    return jnp.pad(row, (0, width - row.shape[0]))[None]


def adam_vector(params, moment, square, gradient):
    momentum = BETA_ONE * moment + (1.0 - BETA_ONE) * gradient
    variance = BETA_TWO * square + (1.0 - BETA_TWO) * gradient * gradient
    direction = (
        momentum / (1.0 - BETA_ONE**STEP) / (jnp.sqrt(variance / (1.0 - BETA_TWO**STEP)) + EPS_ADAM)
    )
    return (params - VECTOR_RATE * (direction + DECAY * params), momentum, variance)


def soap_one(rate, flipped, weight, moment, square, basis, gradient, outs):
    if flipped:
        rotated = product(basis, gradient, 0, 1, HIGHEST)
    else:
        rotated = product(gradient, basis, 1, 0, HIGHEST)
    momentum = BETA_ONE * moment[...] + (1.0 - BETA_ONE) * rotated
    variance = BETA_TWO * square[...] + (1.0 - BETA_TWO) * rotated * rotated
    direction = momentum * (1.0 / (1.0 - BETA_ONE**STEP)) / (
        jnp.sqrt(variance * (1.0 / (1.0 - BETA_TWO**STEP))) + EPS_ADAM
    )
    if flipped:
        turned = product(basis, direction, 1, 0, HIGHEST)
    else:
        turned = product(direction, basis, 1, 1, HIGHEST)
    old = weight[...]
    outs[0][...] = old - rate * (turned + DECAY * old)
    outs[1][...] = momentum
    outs[2][...] = variance


def soap_shards(rates, *refs):
    count = len(rates)
    for i, (rate, flipped) in enumerate(rates):
        group = refs[5 * i : 5 * i + 3]
        outs = refs[5 * count + 3 * i : 5 * count + 3 * i + 3]
        basis, gradient = refs[5 * i + 3][...], refs[5 * i + 4][...]
        soap_one(rate, flipped, *group, basis, gradient, outs)


def close(rates, *refs):
    grams, bases, adds = refs[0:5], refs[5:10], refs[10:15]
    lateral, head = refs[15:18], refs[18:21]
    outs, lateral_outs, head_outs = refs[21:31], refs[31:34], refs[34:37]
    lateral_gram, head_gram = refs[37:39]
    total_lateral, total_heads = adds[2][...], adds[4][...]
    lateral_gram[...] = product(total_lateral, total_lateral, 0, 0, HIGHEST)
    head_gram[...] = product(total_heads, total_heads, 0, 0, HIGHEST)
    sums = (adds[0], adds[1], lateral_gram, adds[3], head_gram)
    kern([C1, C1, C1, C2, CH], *grams, *sums, *bases, *outs, *refs[39:])
    soap_one(rates[0], False, *lateral, bases[2][...], total_lateral, lateral_outs)
    soap_one(rates[1], False, *head, bases[4][...], total_heads, head_outs)


def close_parts(rates, cuts, flags, mine, other, *refs):
    shards = mine.shape[0]
    front = flags[30] == 0.0
    down, upward, lateral, merging, head = adds = refs[-5:]
    half = C1 // 2
    count = C1 // shards
    small = cuts[0] - 2 * count
    for d in range(shards):
        first = jnp.where(front, mine[d], other[d])
        second = jnp.where(front, other[d], mine[d])
        for side in range(2):
            rows, lanes = slice(side * count, (side + 1) * count), slice(side * half, (side + 1) * half)
            down[d * count : (d + 1) * count, lanes] = first[rows]
            upward[d * count : (d + 1) * count, lanes] = second[rows]
        merging[d * small : (d + 1) * small] = second[2 * count : cuts[0], 0:C2]
        rows = cuts[1] - cuts[0]
        lateral[d * rows : (d + 1) * rows, 0:half] = first[cuts[0] : cuts[1]]
        lateral[d * rows : (d + 1) * rows, half:] = second[cuts[0] : cuts[1]]
        rows = cuts[2] - cuts[1]
        head[d * rows : (d + 1) * rows] = first[cuts[1] : cuts[2], 0:CH]
        start = C2 // 2 + d * rows
        head[start : start + rows] = second[cuts[1] : cuts[2], 0:CH]
    close(rates, *refs[:10], *adds, *refs[10:-5])


def partial_gram(shard):
    return jnp.tensordot(shard, shard, axes=((0,), (0,)), precision=HIGHEST)


def assembled(final, other, gram_rows, small):
    final_first, final_second = in_order(final, other)
    shards, half, wide = final.shape[0], C1 // 2, 2 * C2

    def square_of(value):
        count = C1 // shards
        return jnp.concatenate(
            [value[:, k * count : (k + 1) * count].reshape(C1, half) for k in range(2)], axis=1
        )

    gram_down = square_of(final_first)
    gram_upward = square_of(final_second)
    gram_merging = final_second[:, 2 * (C1 // shards) : gram_rows].reshape(-1, wide)[:C2, :C2]
    total_lateral = jnp.concatenate(
        [v[:, gram_rows : gram_rows + small].reshape(C0, half) for v in (final_first, final_second)],
        axis=1,
    )
    total_heads = jnp.concatenate(
        [
            v[:, gram_rows + small :].reshape(-1, wide)[: C2 // 2]
            for v in (final_first, final_second)
        ],
        axis=0,
    )[:, :CH]
    return gram_down, gram_upward, total_lateral, gram_merging, total_heads


def local(
    feats,
    occupied,
    cotangent,
    vector_params,
    vector_moment,
    vector_square,
    down_weight,
    down_moment,
    down_square,
    down_gram,
    down_basis,
    upward_weight,
    upward_moment,
    upward_square,
    upward_gram,
    upward_basis,
    lateral_weight,
    lateral_moment,
    lateral_square,
    lateral_gram,
    lateral_basis,
    merging_weight,
    merging_moment,
    merging_square,
    merging_gram,
    merging_basis,
    heads_weight,
    heads_moment,
    heads_square,
    heads_gram,
    heads_basis,
):
    height, breadth, _ = feats.shape
    half_height, half_breadth = height // 2, breadth // 2
    shards = lax.axis_size("dp")
    cores = lax.axis_size("stream")
    everybody = shards * cores
    total_rows = height * shards
    fine_count = float(height * breadth * everybody)
    coarse_count = fine_count / 4.0
    shard_index, core = lax.axis_index("dp"), lax.axis_index("stream")
    first_row = shard_index * height
    width, half_width = breadth + 6, half_breadth + 3
    rows, half_rows = height + 2, half_height + 2
    flags = jnp.concatenate(
        [
            keep_rows(first_row + 2 * jnp.arange(-1, half_height + 1), total_rows),
            keep_rows(first_row + jnp.arange(-1, height + 3), total_rows),
            (core != 0).astype(F32)[None],
            (core != cores - 1).astype(F32)[None],
        ]
    )
    gains = [vector_params[i * C1 : (i + 1) * C1] for i in range(6)]
    late = 6 * C1
    gain_five, shift_five = vector_params[late : late + C2], vector_params[late + C2 : late + 2 * C2]
    head_bias = vector_params[late + 2 * C2 :]
    wide = 2 * C2
    norm_fine = jnp.stack(
        [jnp.concatenate([gains[2], gains[4]]), jnp.concatenate([gains[3], gains[5]])]
    )
    norm_five = jnp.concatenate([lanes_of(gain_five, wide), lanes_of(shift_five, wide)])

    half = C1 // 2
    weight_halves = [
        lax.dynamic_slice_in_dim(w, core * half, half, 1) for w in (down_weight, upward_weight)
    ]
    quarter = merging_weight.shape[0] // 4
    runs = [
        lax.dynamic_slice_in_dim(merging_weight, (2 * core + i) * quarter, quarter, 0)
        for i in range(2)
    ]
    weight_halves.append(jnp.concatenate(runs, axis=1))
    place = jnp.concatenate([gather_order(), core[None].astype(jnp.int32)])
    occupancy = occupied.astype(F32)[..., None]
    masked = feats * occupancy
    shown = jnp.broadcast_to(occupancy, feats.shape)
    up = shifted(masked[height - RIM_UP :], "dp", 1)
    down = shifted(masked[:RIM_DOWN], "dp", -1)
    edges = jnp.concatenate([up, masked, down], axis=0)
    gathered = gather_pieces(jnp.concatenate(weight_halves, axis=0), up, down)
    left = from_behind(edges[:, breadth - RIM_LEFT :], "stream", 1)
    right = from_behind(edges[:, :RIM_RIGHT], "stream", -1)
    grid, z_four, sums_four = stage(
        pad_lateral,
        [
            (height + RIM_UP + RIM_DOWN, width + LEAD - 2, C0),
            (rows, width, C1),
            (1, 2 * C1),
        ],
        [masked, up, down, left, right, lateral_weight],
        name="pad_lateral",
    )

    swapped = exchange(after(gathered, grid))
    bounds = [0]
    for part in weight_halves:
        bounds.append(bounds[-1] + part.shape[0])
    map_outs = [
        (half_rows, half_width, C1),
        (half_rows, half_width, 9 * C0),
        (everybody, 1, 4 * C1),
    ]
    if bounds[1] % 8 == 0:
        part_shape = (NEAR, shards // NEAR, bounds[1], half)
        z_one, windows, sums_one, down_full = stage(
            coarse_arranged,
            [*map_outs, (9 * C0, C1)],
            [grid, gathered, swapped, sums_four],
            scalars=[flags, place],
            scratch=[pltpu.VMEM(part_shape, F32)] * 2 + [pltpu.SemaphoreType.DMA((2,))],
            name="coarse",
            far_args=(1, 2),
        )
    else:
        down_full = arranged(place, gathered, swapped, 0, bounds[1])
        z_one, windows, sums_one = stage(
            coarse_map, map_outs, [grid, down_full, sums_four], scalars=[flags], name="coarse"
        )
    upward_full = arranged(place, after(gathered, z_one), swapped, bounds[1], bounds[2])
    total_one = after(to_all(sums_one), upward_full)

    z_three, act_one, slope_one, sums_three = stage(
        functools.partial(upsample, coarse_count),
        [
            (2, rows, width, C1 // 2),
            (half_rows, half_width, C1),
            (half_rows, half_width, C1),
            (everybody, 1, 2 * C1),
        ],
        [z_one, total_one, gains[0][None], gains[1][None], upward_full],
        name="upsample",
    )
    packed = packed_merging(place, gathered, swapped, bounds[2], sums_three)
    total_three = after(to_all(sums_three), packed)

    merged, joined, slopes, sums_five = stage(
        functools.partial(merge, fine_count),
        [
            (height, width, wide),
            (rows, width, 2 * C1),
            (rows, width, 2 * C1),
            (everybody, 1, 2 * wide),
        ],
        [z_three, z_four, total_three, total_one, norm_fine, packed],
        scalars=[flags],
        scratch=[
            pltpu.VMEM((rows, width, 12 * C2), F32),
            pltpu.VMEM((2, rows, width, half), F32),
            pltpu.VMEM((rows, width, C1), F32),
            pltpu.VMEM((2 * C1, 12 * C2), F32),
            pltpu.VMEM((rows, width, 2 * C1), F32),
            pltpu.VMEM((rows, width, 2 * C1), F32),
            pltpu.SemaphoreType.DMA((rows // 3 + 1,)),
            pltpu.SemaphoreType.DMA((rows // 3,)),
        ],
        name="merge",
        far_args=(0, 1, 5),
        far_outs=(1, 2),
    )
    total_five = to_all(sums_five)

    heads_padded = jnp.pad(heads_weight, ((0, wide - C2), (0, wide - CH)))
    head_maps, pairs, last_row, first_row_pair, edge, heads_grad, grad_sums_five = stage(
        functools.partial(heads, fine_count),
        [
            (height, CH, breadth),
            (height, width, wide),
            (1, width, wide),
            (1, width, wide),
            (height, 1, wide),
            (wide, wide),
            (everybody, 1, 3 * wide),
        ],
        [merged, total_five, norm_five, heads_padded, lanes_of(head_bias, wide), cotangent],
        scalars=[flags],
        scratch=[pltpu.VMEM((height, width, wide), F32)] * 2,
        name="heads",
    )
    head_maps = jnp.swapaxes(head_maps, 1, 2)
    grads_five = to_all(grad_sums_five)
    above = shifted(last_row, "dp", 1)
    below = shifted(first_row_pair, "dp", -1)
    ends = [jnp.where(core == 0, v[:, 1 + breadth : 2 + breadth], v[:, 2:3]) for v in (above, below)]
    side = exchange(jnp.concatenate([ends[0], edge, ends[1]], axis=0))

    grad_joined, columns, grad_sums = stage(
        functools.partial(merged_gradient, fine_count),
        [
            (height, width, 2 * C1),
            (rows, width, 4 * C2),
            (everybody, 1, 4 * C1),
        ],
        [
            pairs,
            above,
            below,
            side,
            total_five,
            grads_five,
            norm_five,
            packed,
            z_three,
            z_four,
            slopes,
            total_three,
            total_one,
        ],
        scalars=[flags],
        scratch=[
            pltpu.VMEM((2 * C1, 12 * C2), F32),
            pltpu.VMEM((2, rows, width, half), F32),
            pltpu.VMEM((rows, width, C1), F32),
            pltpu.VMEM((rows, width, 2 * C1), F32),
            pltpu.VMEM((height, width, 2 * C1), F32),
            pltpu.VMEM((rows, width, 4 * C2), F32),
            pltpu.SemaphoreType.DMA((3 * height // 4 + 1,)),
            pltpu.SemaphoreType.DMA((height // 4 + 1,)),
        ],
        name="merged_gradient",
        far_args=(7, 8, 9, 10),
        far_outs=(0, 1),
    )
    far = shards // NEAR
    slots = jnp.arange(NEAR, dtype=jnp.int32) ^ (shard_index % NEAR).astype(jnp.int32)
    shifted_rows = pltpu.VMEM((height, width, 4 * C2), F32)
    aligned = quarter % 8 == 0
    if aligned:
        merging_grads = stage(
            merging_product,
            [(NEAR, far, quarter, wide)] * 2,
            [joined, columns],
            scalars=[flags, slots],
            scratch=[pltpu.VMEM((18 * C1, C2), F32), shifted_rows],
            name="merging_product",
        )
    else:
        (merging_grad,) = stage(
            multiply_merging,
            [(18 * C1, C2)],
            [joined, columns],
            scalars=[flags],
            scratch=[shifted_rows],
            name="merging_product",
        )
        merging_grads = slotted(fold_rows(merging_grad, shards))
    merging_grad = merging_grads[0]
    grads_joined = after(to_all(grad_sums), merging_grad)

    quads, grad_one, top_one, side_one, grad_sums_one = stage(
        functools.partial(coarse_gradient, fine_count, coarse_count),
        [
            (4, half_height, half_width, C1),
            (half_rows, half_width, C1),
            (1, half_width, C1),
            (half_height, 1, C1),
            (everybody, 1, 2 * C1),
        ],
        [
            grad_joined,
            z_three,
            total_three,
            grads_joined,
            gains[2][None],
            upward_full,
            z_one,
            total_one,
            slope_one,
        ],
        scratch=[pltpu.VMEM((2, height, width, C1 // 2), F32)],
        name="coarse_gradient",
    )
    late_rows = [4 * C1 // shards, C0 // shards, -(-C2 // (2 * shards))]
    late_args = [
        grad_joined,
        z_four,
        total_one,
        grads_joined,
        gains[4][None],
        grid,
        act_one,
        quads,
        heads_grad,
    ]
    fine_scratch = pltpu.VMEM((height, width, C1), F32)
    if aligned:
        late_grads = stage(
            functools.partial(fine_products, fine_count),
            [(NEAR, far, quarter + sum(late_rows), half)] * 2,
            [*late_args, *merging_grads],
            scalars=[flags, slots],
            scratch=[fine_scratch],
            name="fine_products",
        )
    else:
        late_halves = stage(
            functools.partial(fine_halves, fine_count),
            [(2, 4 * C1, half), (2, C0, half)],
            late_args[:-1],
            scratch=[fine_scratch],
            name="fine_products",
        )
        heads_halves = heads_grad[:C2].reshape(2, C2 // 2, wide)
        blocks = [by_shard(value) for value in (*late_halves, heads_halves)]
        pairs_of = zip(merging_grads, slotted(jnp.concatenate(blocks, axis=2)))
        late_grads = [jnp.concatenate(pair, axis=2) for pair in pairs_of]
    grads_one = after(to_all(grad_sums_one), late_grads[0])
    down_args = [windows, grad_one, z_one, total_one, grads_one, gains[0][None]]
    if aligned:
        down_grads = stage(
            functools.partial(window_product, coarse_count),
            [(NEAR, far, 9 * C0 // shards, half)] * 2,
            down_args,
            scalars=[flags, slots],
            name="window_product",
        )
    else:
        (halves,) = stage(
            functools.partial(window_halves, coarse_count),
            [(2, 9 * C0, half)],
            down_args,
            name="window_product",
        )
        down_grads = slotted(by_shard(halves))
    down_sums = chip_sums(down_grads[0], exchange(down_grads[1]))
    rest_other = exchange(after(late_grads[1], down_grads[0]))
    rest_sums = chip_sums(after(late_grads[0], *down_sums), rest_other)
    down_mine = near_sum(down_sums)
    received = far_sum(after(down_mine, *rest_sums))
    rest = near_sum(rest_sums, received)
    rest_received = far_sum(rest)
    below = shifted(after(top_one, received), "dp", -1)
    first_col = jnp.concatenate([side_one, below[:, 1:2]], axis=0)
    right = from_behind(first_col, "stream", -1)
    cuts = [0]
    for count in (quarter, *late_rows):
        cuts.append(cuts[-1] + count)

    sums_back = jnp.sum(grads_one[:, 0], axis=0)
    down_part = jnp.sum(received, axis=0)
    down_shard = jnp.concatenate(in_order(down_part, exchange(down_part)), axis=1)
    gram_one = partial_gram(down_shard)
    part = jnp.sum(after(rest_received, gram_one, right), axis=0)
    swapped = exchange(part[: cuts[2]])
    first_part, second_part = in_order(part[: cuts[2]], swapped)
    merging_shard = unfold_rows(first_part[None, : cuts[1]], second_part[None, : cuts[1]])
    upward_shard = jnp.concatenate([first_part[cuts[1] :], second_part[cuts[1] :]], axis=1)

    def lane_rows(gram):
        count = gram.shape[0] // shards
        return jnp.concatenate(
            [
                gram[:, k * half : (k + 1) * half].reshape(shards, count, half)
                for k in range(C1 // half)
            ],
            axis=1,
        )

    shard_groups = [
        (down_weight, down_moment, down_square, down_basis, down_shard),
        (upward_weight, upward_moment, upward_square, upward_basis, upward_shard),
        (merging_weight.T, merging_moment.T, merging_square.T, merging_basis, merging_shard),
    ]
    stepped = stage(
        functools.partial(
            soap_shards,
            (
                (1.0 / math.sqrt(9 * C0), False),
                (1.0 / math.sqrt(C1), False),
                (1.0 / math.sqrt(18 * C1), True),
            ),
        ),
        [group[0].shape for group in shard_groups for _ in range(3)],
        [array for group in shard_groups for array in group],
        name="soap",
    )
    down_renewed, down_momentum, down_variance = stepped[:3]
    upward_renewed, upward_momentum, upward_variance = stepped[3:6]
    merging_renewed, merging_momentum, merging_variance = (value.T for value in stepped[6:])
    gram_two = jnp.pad(partial_gram(merging_shard), ((0, -C2 % shards), (0, wide - C2)))
    gram_two = gram_two.reshape(shards, -1, wide)
    firsts = jnp.pad(lane_rows(gram_one), ((0, 0), (0, gram_two.shape[1]), (0, 0)))
    seconds = jnp.concatenate([lane_rows(partial_gram(upward_shard)), gram_two], axis=1)
    parts = jnp.where(core == 0, firsts, seconds)
    gram_parts = after(lax.all_to_all(parts, "dp", 0, 0, tiled=True), *stepped)
    gram_sum = jnp.sum(gram_parts, axis=0)
    (feats_grad,) = stage(
        functools.partial(input_gradient, fine_count, coarse_count),
        [(breadth * height, C0)],
        [
            grad_one,
            below,
            right,
            z_one,
            total_one,
            after(grads_one, gram_sum),
            gains[0][None],
            down_full,
            grad_joined,
            z_four,
            grads_joined,
            gains[4][None],
            lateral_weight,
            shown,
        ],
        scalars=[flags],
        scratch=[
            pltpu.VMEM((half_rows - 1, half_width, 9 * C0), F32),
            pltpu.VMEM((height, width, C0), F32),
            fine_scratch,
        ],
        name="input_gradient",
    )
    feats_grad = jnp.swapaxes(feats_grad.reshape(breadth, height, C0), 0, 1)
    gram_rows = gram_sum.shape[0]
    final = everyone(jnp.concatenate([gram_sum, part[cuts[2] :]], axis=0))
    final = after(final, feats_grad)
    final_other = exchange(final)
    grams = (down_gram, upward_gram, lateral_gram, merging_gram, heads_gram)
    bases = (down_basis, upward_basis, lateral_basis, merging_basis, heads_basis)
    orders = [C1, C1, C1, C2, CH]
    padded = [-(-n // NB) * NB for n in orders]
    close_args = [
        *grams,
        *bases,
        lateral_weight,
        lateral_moment,
        lateral_square,
        heads_weight,
        heads_moment,
        heads_square,
    ]
    close_outs = [(n, n) for n in orders] * 2 + [(C0, C1)] * 3 + [(C2, CH)] * 3
    close_scratch = [pltpu.VMEM((n, n), F32) for n in (C1, CH)]
    close_scratch += [pltpu.VMEM((n, 2 * n), F32) for n in padded]
    rates = (1.0 / math.sqrt(C0), 1.0 / math.sqrt(C2))
    add_shapes = [(C1, C1), (C1, C1), (C0, C1), (C2, C2), (C2, CH)]
    if aligned:
        ends = (gram_rows, gram_rows + late_rows[1], gram_rows + sum(late_rows[1:]))
        closed = stage(
            functools.partial(close_parts, rates, ends),
            close_outs,
            [final, final_other, *close_args],
            scalars=[flags],
            scratch=close_scratch + [pltpu.VMEM(shape, F32) for shape in add_shapes],
            name="close",
        )
    else:
        adds = assembled(final, final_other, gram_rows, late_rows[1])
        closed = stage(
            functools.partial(close, rates),
            close_outs,
            [*close_args[:10], *adds, *close_args[10:]],
            scratch=close_scratch,
            name="close",
        )
    down_gramian, upward_gramian, lateral_gramian, merging_gramian, heads_gramian = closed[:5]
    down_rotation, upward_rotation, lateral_rotation, merging_rotation, heads_rotation = closed[5:10]
    lateral_renewed, lateral_momentum, lateral_variance = closed[10:13]
    heads_renewed, heads_momentum, heads_variance = closed[13:]

    sums_fine = jnp.sum(grads_joined[:, 0], axis=0)
    sums_late = jnp.sum(grads_five[:, 0], axis=0)
    grad_vector = jnp.concatenate(
        [
            sums_back,
            sums_fine[:C1],
            sums_fine[2 * C1 : 3 * C1],
            sums_fine[C1 : 2 * C1],
            sums_fine[3 * C1 :],
            sums_late[:C2],
            sums_late[wide : wide + C2],
            sums_late[2 * wide : 2 * wide + CH],
        ]
    )
    vector_renewed, vector_momentum, vector_variance = adam_vector(
        vector_params, vector_moment, vector_square, grad_vector
    )
    return (
        head_maps,
        feats_grad,
        vector_renewed,
        vector_momentum,
        vector_variance,
        down_renewed,
        down_momentum,
        down_variance,
        down_gramian,
        down_rotation,
        upward_renewed,
        upward_momentum,
        upward_variance,
        upward_gramian,
        upward_rotation,
        lateral_renewed,
        lateral_momentum,
        lateral_variance,
        lateral_gramian,
        lateral_rotation,
        merging_renewed,
        merging_momentum,
        merging_variance,
        merging_gramian,
        merging_rotation,
        heads_renewed,
        heads_momentum,
        heads_variance,
        heads_gramian,
        heads_rotation,
    )


def solution(mesh):
    in_specs = (
        P("dp", "stream", None),
        P("dp", "stream"),
        P("dp", "stream", None),
        P(),
        P(),
        P(),
        P("dp", None),
        P("dp", None),
        P("dp", None),
        P(),
        P(),
        P("dp", None),
        P("dp", None),
        P("dp", None),
        P(),
        P(),
        P(),
        P(),
        P(),
        P(),
        P(),
        P("dp", None),
        P("dp", None),
        P("dp", None),
        P(),
        P(),
        P(),
        P(),
        P(),
        P(),
        P(),
    )
    out_specs = (
        P("dp", "stream", None),
        P("dp", "stream", None),
        P(),
        P(),
        P(),
        P("dp", None),
        P("dp", None),
        P("dp", None),
        P(),
        P(),
        P("dp", None),
        P("dp", None),
        P("dp", None),
        P(),
        P(),
        P(),
        P(),
        P(),
        P(),
        P(),
        P("dp", None),
        P("dp", None),
        P("dp", None),
        P(),
        P(),
        P(),
        P(),
        P(),
        P(),
        P(),
    )
    return jax.shard_map(local, mesh=mesh, in_specs=in_specs, out_specs=out_specs, check_vma=False)
```
